32 devices in a mesh: seq: 2 (over core), fsdp: 16 (over z, y, x).
Axes of the slice: x: 2, y: 2, z: 4, core: 2. Of those that a mesh axis runs over, the one named last changes fastest.
Arguments:
- inputs: bfloat16 [2, 16, 512, 768], P(None, 'fsdp', 'seq'), may hold values from -6 to 6
- order: int32 [2, 16, 512], P(None, 'fsdp'), may hold values from 0 to 511, each once within a row
- lengths: int32 [2, 16, 2], P(None, 'fsdp'), may hold values from 128 to 384, as said below
- cotangent: bfloat16 [2, 16, 512, 768], P(None, 'fsdp', 'seq'), may hold values from -6 to 6
- weight_qkv: bfloat16 [768, 2304], P(('seq', 'fsdp')), may hold values from -0.21875 to 0.21875
- bias_qv: bfloat16 [1536], P(('seq', 'fsdp')), may hold values from -3 to 3
- weight_out: bfloat16 [768, 768], P(('seq', 'fsdp')), may hold values from -0.625 to 0.625
- bias_out: bfloat16 [768], P(('seq', 'fsdp')), may hold values from -3 to 3
- weight_in: bfloat16 [768, 3072], P(('seq', 'fsdp')), may hold values from -0.21875 to 0.21875
- bias_in: bfloat16 [3072], P(('seq', 'fsdp')), may hold values from -3 to 3
- weight_back: bfloat16 [3072, 768], P(('seq', 'fsdp')), may hold values from -0.21875 to 0.21875
- bias_back: bfloat16 [768], P(('seq', 'fsdp')), may hold values from -3 to 3
- gain_first: bfloat16 [768], P(('seq', 'fsdp')), may hold values from 0.25 to 1.75
- shift_first: bfloat16 [768], P(('seq', 'fsdp')), may hold values from -2 to 2
- gain_second: bfloat16 [768], P(('seq', 'fsdp')), may hold values from 0.25 to 1.75
- shift_second: bfloat16 [768], P(('seq', 'fsdp')), may hold values from -2 to 2
Outputs:
- block_out: bfloat16 [2, 16, 512, 768], P(None, 'fsdp', 'seq')
- input_grad: bfloat16 [2, 16, 512, 768], P(None, 'fsdp', 'seq')
- grad_weight_qkv: float32 [768, 2304], P(('seq', 'fsdp'))
- grad_bias_qv: float32 [1536], P(('seq', 'fsdp'))
- grad_weight_out: float32 [768, 768], P(('seq', 'fsdp'))
- grad_bias_out: float32 [768], P(('seq', 'fsdp'))
- grad_weight_in: float32 [768, 3072], P(('seq', 'fsdp'))
- grad_bias_in: float32 [3072], P(('seq', 'fsdp'))
- grad_weight_back: float32 [3072, 768], P(('seq', 'fsdp'))
- grad_bias_back: float32 [768], P(('seq', 'fsdp'))
- grad_gain_first: float32 [768], P(('seq', 'fsdp'))
- grad_shift_first: float32 [768], P(('seq', 'fsdp'))
- grad_gain_second: float32 [768], P(('seq', 'fsdp'))
- grad_shift_second: float32 [768], P(('seq', 'fsdp'))
The draws below stay inside these ranges and needn't reach their ends.
Inputs may be any that keep to these rules, and one draw needn't show every extreme that they name: Each row order[m, g, :] holds every packed position 0 to 511 once. Each row lengths[m, g, :] holds the lengths 512 * 3 // 4 and 128 of two sequences packed one after another, in either order.
All inputs are finite; a program needn't handle non-finite values.
Results may differ from the reference program's by a relative error of at most 0.014.
Values may be sent and summed in bfloat16 or wider, within the bound.
No kernel may reach another device: no remote copies, remote signals or barrier semaphores. Data moves between devices by JAX's collectives and lax.ppermute only.
A program may use at most 192 MiB of HBM per device.

```python
import jax
import jax.numpy as jnp
from jax import lax

D = 768
HEADS = 12
HD = 64
FF = 3072
MB = 2
NSEQ = 2
GROUP_TOK = 512
GROUPS = 16


def draw_lengths(key, part):
    flips = jax.random.randint(jax.random.fold_in(key, 7), (MB, GROUPS, 1), 0, 2).astype(jnp.int32)
    longer = GROUP_TOK * 3 // 4
    shorter = GROUP_TOK - longer
    first = jnp.where(flips == 1, longer, shorter).astype(jnp.int32)
    second = (GROUP_TOK - first).astype(jnp.int32)
    return jnp.concatenate([first, second], axis=2).astype(jnp.int32)


def spiked(array, rng, source, target, shards_of, factor):
    def block_of(dim):
        return (jnp.arange(array.shape[dim]) // (array.shape[dim] // shards_of)).reshape((-1,) + (1,) * (array.ndim - 1 - dim))

    one_side = jax.random.permutation(rng, shards_of)[block_of(target)]
    second = (block_of(target) + shards_of // 2) % shards_of
    return jnp.where((block_of(source) == one_side) | (block_of(source) == second), factor * array, array)


def block_scale(key, extent, pieces, least, largest):
    factor_of = 1.0
    for position, shards_of in pieces:
        steps = jax.random.uniform(jax.random.fold_in(jax.random.fold_in(key, 6), position), (shards_of,), jnp.float32, least / len(pieces), largest / len(pieces))
        factor_of = factor_of * jnp.repeat(jnp.exp(steps), extent[position] // shards_of).reshape((-1,) + (1,) * (len(extent) - 1 - position))
    return factor_of


def noise(key, dims, spread, limit, split=(), kind=jnp.bfloat16):
    array = jax.random.normal(key, dims, jnp.float32) * spread
    if len(split) > 0:
        array = block_scale(key, dims, split, -0.22, 0.18) * array
    return jnp.clip(array, min=-limit, max=limit).astype(kind)


def noise_with(own_key, dims, width, reach, pieces, heavy, held_as=jnp.bfloat16):
    drawn = width * jax.random.normal(own_key, dims, jnp.float32)
    if pieces:
        drawn = drawn * block_scale(own_key, dims, pieces, -0.22, 0.18)
    return jnp.clip(spiked(drawn, jax.random.fold_in(own_key, 3), *heavy), -reach, reach).astype(held_as)


def setup_inputs(seed: int = 0) -> dict:
    keys = jax.random.split(jax.random.key(seed), 17)
    inputs = noise(keys[0], (MB, GROUPS, GROUP_TOK, D), 1.0, 6.0, ((1, 16), (2, 2)))
    order = jax.vmap(lambda own: jax.random.permutation(own, GROUP_TOK))(jax.random.split(keys[1], MB * GROUPS)).reshape((MB, GROUPS, GROUP_TOK)).astype(jnp.int32)
    lengths = draw_lengths(jax.random.fold_in(keys[16], 71), 0)
    cotangent = noise_with(keys[3], (MB, GROUPS, GROUP_TOK, D), 1.0, 6.0, ((1, 16), (2, 2)), (1, 3, 16, 2.0))
    weight_qkv = noise(keys[4], (D, 3 * D), D ** -0.5, 0.21875, ((0, 32),))
    bias_qv = noise(keys[5], (2 * D,), 0.5, 3.0, ((0, 32),))
    weight_out = noise(keys[6], (D, D), (D // 8) ** -0.5, 0.625, ((0, 32),))
    bias_out = noise(keys[7], (D,), 0.5, 3.0, ((0, 32),))
    weight_in = noise(keys[8], (D, FF), D ** -0.5, 0.21875, ((0, 32),))
    bias_in = noise(keys[9], (FF,), 0.5, 3.0, ((0, 32),))
    weight_back = noise(keys[10], (FF, D), (FF // 4) ** -0.5, 0.21875, ((0, 32),))
    bias_back = noise(keys[11], (D,), 0.5, 3.0, ((0, 32),))
    gain_first = jnp.clip(1.0 + 0.15 * jax.random.normal(keys[12], (D,), jnp.float32), 0.25, 1.75).astype(jnp.bfloat16)
    shift_first = noise(keys[13], (D,), 0.3, 2.0, ((0, 32),))
    gain_second = jnp.clip(1.0 + 0.15 * jax.random.normal(keys[14], (D,), jnp.float32), 0.25, 1.75).astype(jnp.bfloat16)
    shift_second = noise(keys[15], (D,), 0.3, 2.0, ((0, 32),))
    return {"inputs": inputs, "order": order, "lengths": lengths, "cotangent": cotangent, "weight_qkv": weight_qkv, "bias_qv": bias_qv, "weight_out": weight_out, "bias_out": bias_out, "weight_in": weight_in, "bias_in": bias_in, "weight_back": weight_back, "bias_back": bias_back, "gain_first": gain_first, "shift_first": shift_first, "gain_second": gain_second, "shift_second": shift_second}


@jax.custom_vjp
def low(v):
    return lax.optimization_barrier(v.astype(jnp.bfloat16)).astype(jnp.float32)

@jax.custom_vjp
def low_back(v):
    return v

def low_keep(v):
    return (low(v), None)

def low_pass(kept, grad):
    return (grad,)

def back_keep(v):
    return (v, None)

def back_low(kept, grad):
    return (low(grad),)
low.defvjp(low_keep, low_pass)
low_back.defvjp(back_keep, back_low)
eps = 1e-05
score_scale = 0.125

def matmul_high(left, right):
    return jnp.dot(left, right, precision=lax.Precision.HIGHEST)

def layer_norm(values, gain, shift):
    row_mean = lax.optimization_barrier(jnp.mean(values, axis=-1, keepdims=True))
    centred = values - row_mean
    variance = lax.optimization_barrier(jnp.mean(centred * centred, axis=-1, keepdims=True))
    return centred * lax.rsqrt(variance + eps) * gain + shift

def gelu_tanh(values):
    return 0.5 * values * (1.0 + jnp.tanh(0.7978845608028654 * (values + 0.044715 * values * values * values)))

def attention(queries, key_rows, value_rows, slot_ids, seq_starts):
    block_rows = min(512, GROUP_TOK)
    block_count = GROUP_TOK // block_rows
    key_heads = key_rows.reshape(GROUP_TOK, HEADS, HD)
    value_heads = value_rows.reshape(GROUP_TOK, HEADS, HD)

    def one_block(block_id):
        first = (block_id * block_rows).astype(jnp.int32)
        q_blk = lax.dynamic_slice_in_dim(queries, first, block_rows, 0).reshape(block_rows, HEADS, HD)
        q_pos = lax.dynamic_slice_in_dim(slot_ids, first, block_rows, 0)
        q_start = lax.dynamic_slice_in_dim(seq_starts, first, block_rows, 0)
        raw_scores = jnp.einsum('qhd,khd->hqk', q_blk, key_heads, precision=lax.Precision.HIGHEST) * score_scale
        allowed = (slot_ids[None, :] <= q_pos[:, None]) & (slot_ids[None, :] >= q_start[:, None])
        scores = low_back(jnp.where(allowed[None], raw_scores, -1e+30))
        row_max = lax.optimization_barrier(jnp.max(scores, axis=-1, keepdims=True))
        expo = jnp.exp(scores - row_max)
        prob_rows = expo / lax.optimization_barrier(jnp.sum(expo, axis=-1, keepdims=True))
        head_out = jnp.einsum('hqk,khd->qhd', low(prob_rows), value_heads, precision=lax.Precision.HIGHEST)
        return head_out.reshape(block_rows, D)
    blocks = lax.map(jax.checkpoint(one_block), jnp.arange(block_count, dtype=jnp.int32))
    return blocks.reshape(GROUP_TOK, D)

def block_forward(params, inputs, slot_ids, seq_starts):
    weight_qkv, bias_qv, weight_out, bias_out, weight_in, bias_in, weight_back, bias_back, gain_first, shift_first, gain_second, shift_second = params
    normed = low(layer_norm(inputs, gain_first, shift_first))
    projected = matmul_high(normed, weight_qkv)
    queries = low_back(low(projected[:, :D] + bias_qv[:D]))
    key_rows = low_back(low(projected[:, D:2 * D]))
    value_rows = low_back(low(projected[:, 2 * D:] + bias_qv[D:]))
    attn_heads = attention(queries, key_rows, value_rows, slot_ids, seq_starts)
    attn_heads = low_back(low(attn_heads))
    mid_stream = inputs + low_back(matmul_high(attn_heads, weight_out)) + bias_out
    normed_two = low(layer_norm(mid_stream, gain_second, shift_second))
    pre_act = low_back(matmul_high(normed_two, weight_in) + bias_in)
    hidden = low(gelu_tanh(pre_act))
    return mid_stream + matmul_high(hidden, weight_back) + bias_back

def reference(inputs, order, lengths, cotangent, weight_qkv, bias_qv, weight_out, bias_out, weight_in, bias_in, weight_back, bias_back, gain_first, shift_first, gain_second, shift_second):
    params = tuple((p.astype(jnp.float32) for p in (weight_qkv, bias_qv, weight_out, bias_out, weight_in, bias_in, weight_back, bias_back, gain_first, shift_first, gain_second, shift_second)))
    streams = MB * GROUPS
    flat_inputs = inputs.reshape(streams, GROUP_TOK, D)
    flat_order = order.reshape(streams, GROUP_TOK).astype(jnp.int32)
    flat_lengths = lengths.reshape(streams, NSEQ).astype(jnp.int32)
    flat_cot = cotangent.reshape(streams, GROUP_TOK, D)

    def group_step(totals, group_item):
        x_grp, slot_ids, seq_lens, grad_rows = group_item
        seq_ends = jnp.cumsum(seq_lens).astype(jnp.int32)
        seq_starts = lax.optimization_barrier(jnp.max(jnp.where(seq_ends[None, :] <= slot_ids[:, None], seq_ends[None, :], 0), axis=1)).astype(jnp.int32)

        def forward(weights, block_in):
            return block_forward(weights, block_in, slot_ids, seq_starts)
        outputs, pull = jax.vjp(forward, params, x_grp.astype(jnp.float32))
        gradients, grad_in = pull(grad_rows.astype(jnp.float32))
        totals = jax.tree.map(lambda a, b: a + b, totals, gradients)
        return (totals, (outputs.astype(jnp.bfloat16), grad_in.astype(jnp.bfloat16)))
    start_totals = jax.tree.map(jnp.zeros_like, params)
    totals, (outputs, grad_ins) = lax.scan(group_step, start_totals, (flat_inputs, flat_order, flat_lengths, flat_cot))
    block_out = outputs.reshape(MB, GROUPS, GROUP_TOK, D)
    input_grad = grad_ins.reshape(MB, GROUPS, GROUP_TOK, D)
    return (block_out, input_grad, totals[0], totals[1], totals[2], totals[3], totals[4], totals[5], totals[6], totals[7], totals[8], totals[9], totals[10], totals[11])
```

```python
import jax
import jax.numpy as jnp
from jax import lax
from jax.experimental import pallas as pl
from jax.experimental.pallas import tpu as pltpu
from jax.sharding import PartitionSpec as P

D = 768
HEADS = 12
HD = 64
FF = 3072
MB = 2
PAIR = 2 * HD

eps = 1e-05
score_scale = 0.125
BF = jnp.bfloat16
F32 = jnp.float32


def norm_parts(values):
    row_mean = jnp.mean(values, axis=-1, keepdims=True)
    centred = values - row_mean
    inv_std = lax.rsqrt(jnp.mean(centred * centred, axis=-1, keepdims=True) + eps)
    return (centred * inv_std, inv_std)


def norm_back(grad_norm, x_hat, inv_std, gain):
    scaled = grad_norm * gain
    return inv_std * (
        scaled
        - jnp.mean(scaled, axis=-1, keepdims=True)
        - x_hat * jnp.mean(scaled * x_hat, axis=-1, keepdims=True)
    )


def gelu_tanh(values):
    return (
        0.5
        * values
        * (1.0 + jnp.tanh(0.7978845608028654 * (values + 0.044715 * values * values * values)))
    )


def dot_first(left, right):
    return lax.dot_general(left, right, (((0,), (0,)), ((), ())), preferred_element_type=F32)


def dot_last(left, right):
    return lax.dot_general(left, right, (((1,), (1,)), ((), ())), preferred_element_type=F32)


def dot_plain(left, right):
    return jnp.dot(left, right, preferred_element_type=F32)


def attend_kernel(q_ref, k_ref, v_ref, qpos_ref, qstart_ref, kpos_ref, out_ref, prob_ref, bias_ref):
    @pl.when(pl.program_id(1) == 0)
    def _():
        kpos = kpos_ref[0]
        seen = (kpos <= qpos_ref[0]) & (kpos >= qstart_ref[0])
        bias_ref[...] = jnp.where(seen, 0.0, -1e30)

    q, k, v = q_ref[0], k_ref[0], v_ref[0]
    lane = lax.broadcasted_iota(jnp.int32, q.shape, 1)
    scaled = q * jnp.asarray(score_scale, BF)
    halves = []
    for j in range(2):
        q_head = jnp.where((lane // HD) == j, scaled, jnp.zeros_like(scaled))
        scores = dot_last(k, q_head) + bias_ref[...]
        col_max = jnp.max(scores, axis=0, keepdims=True)
        expo = jnp.exp(scores - col_max)
        probs = (expo * (1.0 / jnp.sum(expo, axis=0, keepdims=True))).astype(BF)
        prob_ref[0, j] = probs
        halves.append(dot_first(v, probs))
    row = lax.broadcasted_iota(jnp.int32, halves[0].shape, 0)
    out_ref[0] = jnp.where(row < HD, halves[0], halves[1]).T.astype(BF)


def attend_back_kernel(q_ref, k_ref, v_ref, dh_ref, prob_ref, dq_ref, dk_ref, dv_ref):
    q, k, v, dh = q_ref[0], k_ref[0], v_ref[0], dh_ref[0]
    lane = lax.broadcasted_iota(jnp.int32, dh.shape, 1)
    dq, dk, dv = [], [], []
    for j in range(2):
        probs = prob_ref[0, j]
        dh_head = jnp.where((lane // HD) == j, dh, jnp.zeros_like(dh))
        d_prob = dot_last(v, dh_head)
        wide = probs.astype(F32)
        moved = wide * d_prob
        centre = jnp.sum(moved, axis=0, keepdims=True)
        d_scores = (moved - wide * centre).astype(BF)
        dq.append(dot_first(k, d_scores))
        dk.append(dot_plain(d_scores, q))
        dv.append(dot_plain(probs, dh))
    row = lax.broadcasted_iota(jnp.int32, dq[0].shape, 0)
    col = lax.broadcasted_iota(jnp.int32, dk[0].shape, 1)
    dq_ref[0] = (score_scale * jnp.where(row < HD, dq[0], dq[1])).T.astype(BF)
    dk_ref[0] = (score_scale * jnp.where(col < HD, dk[0], dk[1])).astype(BF)
    dv_ref[0] = jnp.where(col < HD, dv[0], dv[1]).astype(BF)


def cols(rows, offset):
    return pl.BlockSpec((1, rows, PAIR), lambda s, h: (s, 0, h + offset))


def attend(q, k, v, qpos, qstart, kpos):
    (q_arr, q_off), (k_arr, k_off), (v_arr, v_off) = q, k, v
    streams, rows = q_arr.shape[:2]
    keys = k_arr.shape[1]
    pairs = HEADS // 2
    return pl.pallas_call(
        attend_kernel,
        grid=(streams, pairs),
        in_specs=[
            cols(rows, q_off),
            cols(keys, k_off),
            cols(keys, v_off),
            pl.BlockSpec((1, 1, rows), lambda s, h: (s, 0, 0)),
            pl.BlockSpec((1, 1, rows), lambda s, h: (s, 0, 0)),
            pl.BlockSpec((1, keys, 1), lambda s, h: (s, 0, 0)),
        ],
        out_specs=[
            cols(rows, 0),
            pl.BlockSpec((1, 2, keys, rows), lambda s, h: (s, h, 0, 0)),
        ],
        out_shape=[
            jax.ShapeDtypeStruct((streams, rows, D), BF),
            jax.ShapeDtypeStruct((streams, HEADS, keys, rows), BF),
        ],
        scratch_shapes=[pltpu.VMEM((keys, rows), F32)],
        cost_estimate=pl.CostEstimate(
            flops=4 * streams * HEADS * rows * keys * PAIR,
            transcendentals=streams * HEADS * rows * keys,
            bytes_accessed=2 * streams * (HEADS * rows * keys + 4 * rows * D),
        ),
        name="attend",
    )(q_arr, k_arr, v_arr, qpos[:, None, :], qstart[:, None, :], kpos[:, :, None])


def attend_back(q, k, v, d_heads, probs):
    (q_arr, q_off), (k_arr, k_off), (v_arr, v_off) = q, k, v
    streams, rows = q_arr.shape[:2]
    keys = k_arr.shape[1]
    pairs = HEADS // 2
    return pl.pallas_call(
        attend_back_kernel,
        grid=(streams, pairs),
        in_specs=[
            cols(rows, q_off),
            cols(keys, k_off),
            cols(keys, v_off),
            cols(rows, 0),
            pl.BlockSpec((1, 2, keys, rows), lambda s, h: (s, h, 0, 0)),
        ],
        out_specs=[cols(rows, 0), cols(keys, 0), cols(keys, 0)],
        out_shape=[
            jax.ShapeDtypeStruct((streams, rows, D), BF),
            jax.ShapeDtypeStruct((streams, keys, D), BF),
            jax.ShapeDtypeStruct((streams, keys, D), BF),
        ],
        cost_estimate=pl.CostEstimate(
            flops=8 * streams * HEADS * rows * keys * PAIR,
            transcendentals=0,
            bytes_accessed=2 * streams * (HEADS * rows * keys + 7 * rows * D),
        ),
        name="attend_back",
    )(q_arr, k_arr, v_arr, d_heads, probs)


def bits_of(count):
    return [1 << b for b in range(count.bit_length() - 1)]


def swap(value, axis, count, bit):
    return lax.ppermute(value, axis, [(i, i ^ bit) for i in range(count)])


def chip_order(count, first):
    bits = bits_of(count)
    near = [b for b in bits[:2] if b != first]
    return bits[2:] + near + [first]


def gather_blocks(shard, order, n_seq, n_chip):
    parts, rel = [shard[None]], [0]
    for bit in order:
        whole = parts[0] if len(parts) == 1 else jnp.concatenate(parts, axis=0)
        parts = [whole, swap(whole, "fsdp", n_chip, bit)]
        rel = rel + [r ^ bit for r in rel]
    for bit in bits_of(n_seq):
        parts = parts + [swap(part, "seq", n_seq, bit) for part in parts]
        rel = rel + [r ^ (bit * n_chip) for r in rel]
    return parts, rel


def reorder_kernel(counts, widths, table_ref, *refs):
    ins, outs = refs[: len(counts)], refs[len(counts) :]
    place = 0
    for part_ref, count in zip(ins, counts):
        for i in range(count):
            target = table_ref[place]
            for out_ref in outs:
                out_ref[target] = part_ref[i]
            place += 1


def reorder(parts, rel, me, chunks):
    rows, width = parts[0].shape[1:]
    counts = [part.shape[0] for part in parts]
    total = sum(counts)
    step = width // chunks
    table = jnp.bitwise_xor(me, jnp.asarray(rel, jnp.int32))
    out = pl.pallas_call(
        lambda *refs: reorder_kernel(counts, None, *refs),
        grid=(chunks,),
        in_specs=[pl.BlockSpec(memory_space=pltpu.SMEM)]
        + [pl.BlockSpec((count, rows, step), lambda c: (0, 0, c)) for count in counts],
        out_specs=pl.BlockSpec((total, rows, step), lambda c: (0, 0, c)),
        out_shape=jax.ShapeDtypeStruct((total, rows, width), parts[0].dtype),
        cost_estimate=pl.CostEstimate(
            flops=0, transcendentals=0, bytes_accessed=4 * total * rows * width
        ),
        name="reorder",
    )(table, *parts)
    return out.reshape(total * rows, width)


def split_bit(index, bit):
    return (index // bit) % 2


def scatter_steps(keep, recv, order, n_seq, n_chip, seq_pos, chip_pos, wire):
    seq_bits = bits_of(n_seq)[:-1][::-1]
    chip_bits = bits_of(n_chip)[::-1]
    rows, width = keep.shape[1:]
    total = keep.astype(F32) + recv.astype(F32)
    left = [("seq", b) for b in seq_bits] + [("fsdp", b) for b in chip_bits]
    total = total.astype(wire).reshape((2,) * len(left) + (rows, width))
    todo = [("seq", b) for b in seq_bits] + [("fsdp", b) for b in order[::-1]]
    for item in todo:
        axis, bit = item
        place = left.index(item)
        mine = split_bit(seq_pos if axis == "seq" else chip_pos, bit)
        give = lax.dynamic_index_in_dim(total, 1 - mine, place, keepdims=False)
        got = swap(give, axis, n_seq if axis == "seq" else n_chip, bit)
        kept = lax.dynamic_index_in_dim(total, mine, place, keepdims=False)
        total = kept.astype(F32) + got.astype(F32)
        left.remove(item)
        if left:
            total = total.astype(wire)
    return total


def solution(mesh):
    n_seq, n_chip = mesh.shape["seq"], mesh.shape["fsdp"]
    devices = n_seq * n_chip
    low_bits = bits_of(n_chip)
    order_a = chip_order(n_chip, low_bits[0])
    order_b = chip_order(n_chip, low_bits[1])
    top_seq = n_seq // 2
    swapped = n_seq == MB

    def local(
        inputs,
        order,
        lengths,
        cotangent,
        weight_qkv,
        bias_qv,
        weight_out,
        bias_out,
        weight_in,
        bias_in,
        weight_back,
        bias_back,
        gain_first,
        shift_first,
        gain_second,
        shift_second,
    ):
        seq_pos, chip_pos = lax.axis_index("seq"), lax.axis_index("fsdp")
        me = seq_pos * n_chip + chip_pos
        rows_here = inputs.shape[2]

        small = [
            bias_qv,
            bias_out,
            bias_in,
            bias_back,
            gain_first,
            shift_first,
            gain_second,
            shift_second,
        ]
        widths = [v.shape[0] for v in small]
        vec_parts, vec_rel = gather_blocks(
            jnp.concatenate(small)[None], order_a, n_seq, n_chip
        )
        a_parts, a_rel = gather_blocks(weight_qkv[:, : 2 * D], order_a, n_seq, n_chip)
        b_parts, b_rel = gather_blocks(
            jnp.concatenate([weight_qkv[:, 2 * D :], weight_out], axis=1), order_b, n_seq, n_chip
        )
        late_in, late_back, _ = lax.optimization_barrier(
            (weight_in, weight_back, a_parts[0][0, 0, 0])
        )
        in_parts, in_rel = gather_blocks(late_in, order_a, n_seq, n_chip)
        back_parts, back_rel = gather_blocks(late_back, order_b, n_seq, n_chip)

        qk_mat = reorder(a_parts, a_rel, me, 2)
        vo_mat = reorder(b_parts, b_rel, me, 2)
        v_mat, out_mat = vo_mat[:, :D], vo_mat[:, D:]
        in_mat = reorder(in_parts, in_rel, me, 4)
        back_mat = reorder(back_parts, back_rel, me, 3)

        wanted = jnp.bitwise_xor(me, jnp.arange(devices, dtype=jnp.int32))
        spots = jnp.asarray(vec_rel, jnp.int32)
        pick = (wanted[:, None] == spots[None, :]).astype(BF)
        vec_all = dot_plain(pick, jnp.concatenate(vec_parts, axis=0)[:, 0])
        vectors, at = [], 0
        for width in widths:
            vectors.append(vec_all[:, at : at + width].reshape(-1))
            at += width
        qv_vec, out_vec, in_vec, back_vec, gain_one, shift_one, gain_two, shift_two = vectors

        def bring(rows):
            if not swapped:
                return rows[:, 0].reshape(MB * rows_here, D)
            mine = lax.dynamic_index_in_dim(rows[:, 0], seq_pos, 0, keepdims=False)
            other = lax.dynamic_index_in_dim(rows[:, 0], 1 - seq_pos, 0, keepdims=False)
            return jnp.concatenate([mine, swap(other, "seq", n_seq, 1)], axis=0)

        def bring_back(rows):
            if not swapped:
                return rows.reshape(MB, 1, rows_here, D)
            mine, other = rows[:rows_here], swap(rows[rows_here:], "seq", n_seq, 1)
            first = seq_pos == 0
            return jnp.stack([jnp.where(first, mine, other), jnp.where(first, other, mine)])[
                :, None
            ]

        ends = jnp.cumsum(lengths[:, 0], axis=1)
        if swapped:
            ids = lax.dynamic_index_in_dim(order[:, 0], seq_pos, 0, keepdims=False)
            ids = jnp.concatenate(
                [
                    lax.dynamic_slice_in_dim(ids, seq_pos * rows_here, rows_here, 0),
                    lax.dynamic_slice_in_dim(ids, (1 - seq_pos) * rows_here, rows_here, 0),
                ]
            )
            qpos = kpos = ids[None]
            ends = lax.dynamic_index_in_dim(ends, seq_pos, 0, keepdims=True)
        else:
            kpos = order[:, 0]
            qpos = lax.dynamic_slice_in_dim(kpos, seq_pos * rows_here, rows_here, 1)
        qstart = jnp.max(
            jnp.where(ends[:, None, :] <= qpos[:, :, None], ends[:, None, :], 0), axis=2
        )
        streams = qpos.shape[0]

        def by_stream(rows):
            return rows.reshape(streams, -1, rows.shape[-1])

        x_float = bring(inputs).astype(F32)
        grad_rows = bring(cotangent)
        grad_float = grad_rows.astype(F32)
        x_hat_one, inv_one = norm_parts(x_float)
        normed = (x_hat_one * gain_one + shift_one).astype(BF)
        q_bias = jnp.concatenate([qv_vec[:D], jnp.zeros((D,), F32)])
        qk = by_stream((dot_plain(normed, qk_mat) + q_bias).astype(BF))
        value_rows = by_stream((dot_plain(normed, v_mat) + qv_vec[D:]).astype(BF))
        pairs = HEADS // 2
        if swapped:
            q, k, v = (qk, 0), (qk, pairs), (value_rows, 0)
        else:
            q = (qk, 0)
            k = (lax.all_gather(qk[:, :, D:], "seq", axis=1, tiled=True), 0)
            v = (lax.all_gather(value_rows, "seq", axis=1, tiled=True), 0)
        attn_heads, probs = attend(q, k, v, qpos, qstart, kpos)
        attn_heads = attn_heads.reshape(-1, D)
        mid_stream = x_float + dot_plain(attn_heads, out_mat) + out_vec
        x_hat_two, inv_two = norm_parts(mid_stream)
        normed_two = (x_hat_two * gain_two + shift_two).astype(BF)
        pre_act = dot_plain(normed_two, in_mat) + in_vec
        hidden_float, gelu_pull = jax.vjp(gelu_tanh, pre_act)
        hidden = hidden_float.astype(BF)
        result = mid_stream + dot_plain(hidden, back_mat) + back_vec
        block_out = bring_back(result.astype(BF))

        top_mine = split_bit(seq_pos, top_seq)

        def weight_grad(left, right, chip_bits):
            half = left.shape[1] // 2

            def part(which):
                return dot_first(
                    lax.dynamic_slice_in_dim(left, which * half, half, 1), right
                ).astype(BF)

            recv = swap(part(1 - top_mine), "seq", n_seq, top_seq)
            keep = part(top_mine)
            shape = (devices // 2, half // (devices // 2), right.shape[1])
            return scatter_steps(
                keep.reshape(shape),
                recv.reshape(shape),
                chip_bits,
                n_seq,
                n_chip,
                seq_pos,
                chip_pos,
                BF,
            )

        d_back_mat = weight_grad(hidden, grad_rows, order_b)
        d_back_vec = jnp.sum(grad_float, axis=0)
        d_hidden = dot_last(grad_rows, back_mat)
        d_pre = gelu_pull(d_hidden)[0].astype(BF)
        d_in_mat = weight_grad(normed_two, d_pre, order_a)
        d_in_vec = jnp.sum(d_pre.astype(F32), axis=0)
        d_norm_two = dot_last(d_pre, in_mat)
        d_gain_two = jnp.sum(d_norm_two * x_hat_two, axis=0)
        d_shift_two = jnp.sum(d_norm_two, axis=0)
        d_mid = grad_float + norm_back(d_norm_two, x_hat_two, inv_two, gain_two)
        d_out_vec = jnp.sum(d_mid, axis=0)
        d_mid_low = d_mid.astype(BF)
        d_heads = by_stream(dot_last(d_mid_low, out_mat).astype(BF))
        d_query, d_keys, d_values = attend_back(q, k, v, d_heads, probs)
        if not swapped:
            d_keys = lax.psum_scatter(d_keys, "seq", scatter_dimension=1, tiled=True)
            d_values = lax.psum_scatter(d_values, "seq", scatter_dimension=1, tiled=True)
        d_qk = jnp.concatenate([d_query, d_keys], axis=2).reshape(-1, 2 * D)
        d_values = d_values.reshape(-1, D)
        d_qk_mat = weight_grad(normed, d_qk, order_a)
        d_v_mat = weight_grad(normed, d_values, order_b)
        d_out_mat = weight_grad(attn_heads, d_mid_low, order_b)
        q_sums = jnp.sum(d_qk[:, :D].astype(F32), axis=0)
        v_sums = jnp.sum(d_values.astype(F32), axis=0)
        d_qv_vec = jnp.concatenate([q_sums, v_sums])
        d_norm_one = dot_last(d_qk, qk_mat) + dot_last(d_values, v_mat)
        d_gain_one = jnp.sum(d_norm_one * x_hat_one, axis=0)
        d_shift_one = jnp.sum(d_norm_one, axis=0)
        d_inputs = d_mid + norm_back(d_norm_one, x_hat_one, inv_one, gain_one)
        input_grad = bring_back(d_inputs.astype(BF))

        vec_grads = [
            d_qv_vec,
            d_out_vec,
            d_in_vec,
            d_back_vec,
            d_gain_one,
            d_shift_one,
            d_gain_two,
            d_shift_two,
        ]
        packed = jnp.concatenate([g.reshape(devices, -1) for g in vec_grads], axis=1)
        packed = packed.reshape(2, devices // 2, 1, -1)
        give = lax.dynamic_index_in_dim(packed, 1 - top_mine, 0, keepdims=False)
        keep = lax.dynamic_index_in_dim(packed, top_mine, 0, keepdims=False)
        vec_sum = scatter_steps(
            keep,
            swap(give, "seq", n_seq, top_seq),
            order_a,
            n_seq,
            n_chip,
            seq_pos,
            chip_pos,
            F32,
        )[0]
        g_out, at = [], 0
        for width in widths:
            g_out.append(vec_sum[at : at + width])
            at += width
        g_qv, g_out_vec, g_in, g_back, g_gain1, g_shift1, g_gain2, g_shift2 = g_out
        return (
            block_out,
            input_grad,
            jnp.concatenate([d_qk_mat, d_v_mat], axis=1),
            g_qv,
            d_out_mat,
            g_out_vec,
            d_in_mat,
            g_in,
            d_back_mat,
            g_back,
            g_gain1,
            g_shift1,
            g_gain2,
            g_shift2,
        )

    tokens, sharded, vector = P(None, "fsdp", "seq", None), P(("seq", "fsdp"), None), P(("seq", "fsdp"))
    streams_spec = P(None, "fsdp", None)
    return jax.shard_map(
        local,
        mesh=mesh,
        in_specs=(tokens, streams_spec, streams_spec, tokens) + (sharded, vector) * 4 + (vector,) * 4,
        out_specs=(tokens, tokens) + (sharded, vector) * 4 + (vector,) * 4,
        check_vma=False,
    )
```

```python
import jax
import jax.numpy as jnp
from jax import lax
from jax.experimental import pallas as pl
from jax.experimental.pallas import tpu as pltpu
from jax.sharding import PartitionSpec as P

D = 768
HEADS = 12
HD = 64
FF = 3072
MB = 2
PAIR = 2 * HD

eps = 1e-05
score_scale = 0.125
BF = jnp.bfloat16
F32 = jnp.float32


def norm_parts(values):
    row_mean = jnp.mean(values, axis=-1, keepdims=True)
    centred = values - row_mean
    inv_std = lax.rsqrt(jnp.mean(centred * centred, axis=-1, keepdims=True) + eps)
    return (centred * inv_std, inv_std)


def norm_back(grad_norm, x_hat, inv_std, gain):
    scaled = grad_norm * gain
    return inv_std * (
        scaled
        - jnp.mean(scaled, axis=-1, keepdims=True)
        - x_hat * jnp.mean(scaled * x_hat, axis=-1, keepdims=True)
    )


def gelu_tanh(values):
    return (
        0.5
        * values
        * (1.0 + jnp.tanh(0.7978845608028654 * (values + 0.044715 * values * values * values)))
    )


def dot_first(left, right):
    return lax.dot_general(left, right, (((0,), (0,)), ((), ())), preferred_element_type=F32)


def dot_last(left, right):
    return lax.dot_general(left, right, (((1,), (1,)), ((), ())), preferred_element_type=F32)


def dot_plain(left, right):
    return jnp.dot(left, right, preferred_element_type=F32)


def attend_kernel(q_ref, k_ref, v_ref, qpos_ref, qstart_ref, kpos_ref, out_ref, prob_ref, bias_ref):
    @pl.when(pl.program_id(1) == 0)
    def _():
        kpos = kpos_ref[0]
        seen = (kpos <= qpos_ref[0]) & (kpos >= qstart_ref[0])
        bias_ref[...] = jnp.where(seen, 0.0, -1e30)

    q, k, v = q_ref[0], k_ref[0], v_ref[0]
    lane = lax.broadcasted_iota(jnp.int32, q.shape, 1)
    scaled = q * jnp.asarray(score_scale, BF)
    halves = []
    for j in range(2):
        q_head = jnp.where((lane // HD) == j, scaled, jnp.zeros_like(scaled))
        scores = dot_last(k, q_head) + bias_ref[...]
        col_max = jnp.max(scores, axis=0, keepdims=True)
        expo = jnp.exp(scores - col_max)
        probs = (expo * (1.0 / jnp.sum(expo, axis=0, keepdims=True))).astype(BF)
        prob_ref[0, j] = probs
        halves.append(dot_first(v, probs))
    row = lax.broadcasted_iota(jnp.int32, halves[0].shape, 0)
    out_ref[0] = jnp.where(row < HD, halves[0], halves[1]).T.astype(BF)


def attend_back_kernel(q_ref, k_ref, v_ref, dh_ref, prob_ref, dq_ref, dk_ref, dv_ref):
    q, k, v, dh = q_ref[0], k_ref[0], v_ref[0], dh_ref[0]
    lane = lax.broadcasted_iota(jnp.int32, dh.shape, 1)
    dq, dk, dv = [], [], []
    for j in range(2):
        probs = prob_ref[0, j]
        dh_head = jnp.where((lane // HD) == j, dh, jnp.zeros_like(dh))
        d_prob = dot_last(v, dh_head)
        wide = probs.astype(F32)
        moved = wide * d_prob
        centre = jnp.sum(moved, axis=0, keepdims=True)
        d_scores = (moved - wide * centre).astype(BF)
        dq.append(dot_first(k, d_scores))
        dk.append(dot_plain(d_scores, q))
        dv.append(dot_plain(probs, dh))
    row = lax.broadcasted_iota(jnp.int32, dq[0].shape, 0)
    col = lax.broadcasted_iota(jnp.int32, dk[0].shape, 1)
    dq_ref[0] = (score_scale * jnp.where(row < HD, dq[0], dq[1])).T.astype(BF)
    dk_ref[0] = (score_scale * jnp.where(col < HD, dk[0], dk[1])).astype(BF)
    dv_ref[0] = jnp.where(col < HD, dv[0], dv[1]).astype(BF)


def cols(rows, offset):
    return pl.BlockSpec((1, rows, PAIR), lambda s, h: (s, 0, h + offset))


def attend(q, k, v, qpos, qstart, kpos):
    (q_arr, q_off), (k_arr, k_off), (v_arr, v_off) = q, k, v
    streams, rows = q_arr.shape[:2]
    keys = k_arr.shape[1]
    pairs = HEADS // 2
    return pl.pallas_call(
        attend_kernel,
        grid=(streams, pairs),
        in_specs=[
            cols(rows, q_off),
            cols(keys, k_off),
            cols(keys, v_off),
            pl.BlockSpec((1, 1, rows), lambda s, h: (s, 0, 0)),
            pl.BlockSpec((1, 1, rows), lambda s, h: (s, 0, 0)),
            pl.BlockSpec((1, keys, 1), lambda s, h: (s, 0, 0)),
        ],
        out_specs=[
            cols(rows, 0),
            pl.BlockSpec((1, 2, keys, rows), lambda s, h: (s, h, 0, 0)),
        ],
        out_shape=[
            jax.ShapeDtypeStruct((streams, rows, D), BF),
            jax.ShapeDtypeStruct((streams, HEADS, keys, rows), BF),
        ],
        scratch_shapes=[pltpu.VMEM((keys, rows), F32)],
        cost_estimate=pl.CostEstimate(
            flops=4 * streams * HEADS * rows * keys * PAIR,
            transcendentals=streams * HEADS * rows * keys,
            bytes_accessed=2 * streams * (HEADS * rows * keys + 4 * rows * D),
        ),
        name="attend",
    )(q_arr, k_arr, v_arr, qpos[:, None, :], qstart[:, None, :], kpos[:, :, None])


def attend_back(q, k, v, d_heads, probs):
    (q_arr, q_off), (k_arr, k_off), (v_arr, v_off) = q, k, v
    streams, rows = q_arr.shape[:2]
    keys = k_arr.shape[1]
    pairs = HEADS // 2
    return pl.pallas_call(
        attend_back_kernel,
        grid=(streams, pairs),
        in_specs=[
            cols(rows, q_off),
            cols(keys, k_off),
            cols(keys, v_off),
            cols(rows, 0),
            pl.BlockSpec((1, 2, keys, rows), lambda s, h: (s, h, 0, 0)),
        ],
        out_specs=[cols(rows, 0), cols(keys, 0), cols(keys, 0)],
        out_shape=[
            jax.ShapeDtypeStruct((streams, rows, D), BF),
            jax.ShapeDtypeStruct((streams, keys, D), BF),
            jax.ShapeDtypeStruct((streams, keys, D), BF),
        ],
        cost_estimate=pl.CostEstimate(
            flops=8 * streams * HEADS * rows * keys * PAIR,
            transcendentals=0,
            bytes_accessed=2 * streams * (HEADS * rows * keys + 7 * rows * D),
        ),
        name="attend_back",
    )(q_arr, k_arr, v_arr, d_heads, probs)


def bits_of(count):
    return [1 << b for b in range(count.bit_length() - 1)]


def swap(value, axis, count, bit):
    return lax.ppermute(value, axis, [(i, i ^ bit) for i in range(count)])


def after(value, *others):
    return lax.optimization_barrier((value,) + others)[0]


def chip_order(count):
    return bits_of(count)[2:] + [2, 1]


def gather_blocks(shard, order, n_seq, n_chip):
    parts, rel = [shard[None]], [0]
    for bit in order:
        whole = parts[0] if len(parts) == 1 else jnp.concatenate(parts, axis=0)
        parts = [whole, swap(whole, "fsdp", n_chip, bit)]
        rel = rel + [r ^ bit for r in rel]
    for bit in bits_of(n_seq):
        parts = parts + [swap(part, "seq", n_seq, bit) for part in parts]
        rel = rel + [r ^ (bit * n_chip) for r in rel]
    return parts, rel


NEAR = 4


def line_hop(value, n_chip, step, senders):
    pairs = [
        (z * NEAR + n, (z + step) * NEAR + n) for z in senders for n in range(NEAR)
    ]
    return lax.ppermute(value, "fsdp", pairs)


def line_gather(shard, n_chip, far_pos):
    length = n_chip // NEAR
    up, down = [], []
    for t in range(length - 1):
        up.append(line_hop(up[-1] if t else shard, n_chip, 1, range(t, length - 1)))
        down.append(line_hop(down[-1] if t else shard, n_chip, -1, range(1, length - t)))
    stack = jnp.stack(up[::-1] + [shard] + down)
    return stack, length - 1 - far_pos, (up[-1], down[-1])


def near_gather(stack, start, length, lo, hi, bits, n_seq, n_chip, gate):
    block = lax.dynamic_slice_in_dim(stack[:, :, lo:hi], start, length, 0)
    if gate:
        block = after(block, *gate)
    first = swap(block, "fsdp", n_chip, bits[0])
    whole = jnp.concatenate([block, first], axis=0)
    second = swap(whole, "fsdp", n_chip, bits[1])
    parts = [whole, second]
    far = list(range(length))
    rel = [(z, n, 0) for n in (0, bits[0], bits[1], bits[0] ^ bits[1]) for z in far]
    for bit in bits_of(n_seq):
        parts = parts + [swap(part, "seq", n_seq, bit) for part in parts]
        rel = rel + [(z, n, c ^ bit) for z, n, c in rel]
    return parts, rel, whole, second


def reorder_kernel(counts, table_ref, *refs):
    ins, out_ref = refs[: len(counts)], refs[len(counts)]
    place = 0
    for part_ref, count in zip(ins, counts):
        for i in range(count):
            out_ref[table_ref[place]] = part_ref[i]
            place += 1


def places(parts, rel, seq_pos, chip_pos, n_chip, chunks):
    rows, width = parts[0].shape[1:]
    counts = [part.shape[0] for part in parts]
    total = sum(counts)
    step = width // chunks
    far, near, seq = (jnp.asarray(col, jnp.int32) for col in zip(*rel))
    table = (
        jnp.bitwise_xor(seq_pos, seq) * n_chip
        + far * NEAR
        + jnp.bitwise_xor(chip_pos % NEAR, near)
    )
    return table, counts, total, rows, width, step


def reorder_columns(parts, rel, seq_pos, chip_pos, n_chip, chunks):
    table, counts, total, rows, width, step = places(
        parts, rel, seq_pos, chip_pos, n_chip, chunks
    )
    out = pl.pallas_call(
        lambda *refs: reorder_kernel(counts, *refs),
        grid=(chunks,),
        in_specs=[pl.BlockSpec(memory_space=pltpu.SMEM)]
        + [pl.BlockSpec((count, rows, step), lambda c: (0, 0, c)) for count in counts],
        out_specs=pl.BlockSpec((total, rows, step), lambda c: (0, 0, c)),
        out_shape=jax.ShapeDtypeStruct((total, rows, width), BF),
        cost_estimate=pl.CostEstimate(
            flops=0, transcendentals=0, bytes_accessed=4 * total * rows * width
        ),
        name="reorder",
    )(table, *parts)
    return out.reshape(total * rows, width)


def reorder_rows(parts, rel, seq_pos, chip_pos, n_chip, chunks):
    table, counts, total, rows, width, step = places(
        parts, rel, seq_pos, chip_pos, n_chip, chunks
    )
    out = pl.pallas_call(
        lambda *refs: reorder_kernel(counts, *refs),
        grid=(chunks,),
        in_specs=[pl.BlockSpec(memory_space=pltpu.SMEM)]
        + [pl.BlockSpec((count, rows, step), lambda c: (0, 0, c)) for count in counts],
        out_specs=pl.BlockSpec((total, None, rows, step), lambda c: (0, c, 0, 0)),
        out_shape=jax.ShapeDtypeStruct((total, chunks, rows, step), BF),
        cost_estimate=pl.CostEstimate(
            flops=0, transcendentals=0, bytes_accessed=4 * total * rows * width
        ),
        name="reorder_rows",
    )(table, *parts)
    return out.reshape(total * chunks * rows, step)


def split_bit(index, bit):
    return (index // bit) % 2


def fold(total, left, item, mine, count, wire):
    axis, bit = item
    place = left.index(item)
    give = lax.dynamic_index_in_dim(total, 1 - mine, place, keepdims=False)
    got = swap(give, axis, count, bit)
    kept = lax.dynamic_index_in_dim(total, mine, place, keepdims=False)
    left.remove(item)
    return (kept.astype(F32) + got.astype(F32)).astype(wire), give


def scatter_near(keep, recv, near, n_seq, n_chip, seq_pos, chip_pos, wire):
    seq_bits = bits_of(n_seq)[:-1][::-1]
    rows, width = keep.shape[1:]
    left = [("seq", b) for b in seq_bits] + [("far", 0), ("fsdp", 2), ("fsdp", 1)]
    shape = (2,) * len(seq_bits) + (n_chip // NEAR, 2, 2, rows, width)
    total = (keep.astype(F32) + recv.astype(F32)).astype(wire).reshape(shape)
    gave = []
    for item in [("seq", b) for b in seq_bits] + [("fsdp", b) for b in near]:
        axis, bit = item
        mine = split_bit(seq_pos if axis == "seq" else chip_pos, bit)
        total, give = fold(total, left, item, mine, n_seq if axis == "seq" else n_chip, wire)
        gave.append(give)
    return total, gave


def scatter_line(blocks, n_chip, far_pos, wire):
    length = n_chip // NEAR
    up = down = None
    for t in range(length - 1):
        to_up = jnp.clip(length - 1 - t + far_pos, 0, length - 1)
        to_down = jnp.clip(t + far_pos - length + 1, 0, length - 1)
        give_up = lax.dynamic_index_in_dim(blocks, to_up, 0, keepdims=False)
        give_down = lax.dynamic_index_in_dim(blocks, to_down, 0, keepdims=False)
        if t:
            give_up = (give_up.astype(F32) + up.astype(F32)).astype(wire)
            give_down = (give_down.astype(F32) + down.astype(F32)).astype(wire)
        up = line_hop(give_up, n_chip, 1, range(0, min(t, length - 2) + 1))
        down = line_hop(give_down, n_chip, -1, range(length - 1 - t, length))
    own = lax.dynamic_index_in_dim(blocks, far_pos, 0, keepdims=False)
    return own.astype(F32) + up.astype(F32) + down.astype(F32)


def solution(mesh):
    n_seq, n_chip = mesh.shape["seq"], mesh.shape["fsdp"]
    devices = n_seq * n_chip
    near_a, near_b = (2, 1), (1, 2)
    length = n_chip // NEAR
    top_seq = n_seq // 2
    swapped = n_seq == MB

    def local(
        inputs,
        order,
        lengths,
        cotangent,
        weight_qkv,
        bias_qv,
        weight_out,
        bias_out,
        weight_in,
        bias_in,
        weight_back,
        bias_back,
        gain_first,
        shift_first,
        gain_second,
        shift_second,
    ):
        seq_pos, chip_pos = lax.axis_index("seq"), lax.axis_index("fsdp")
        me = seq_pos * n_chip + chip_pos
        rows_here = inputs.shape[2]

        small = [
            bias_qv,
            bias_out,
            bias_in,
            bias_back,
            gain_first,
            shift_first,
            gain_second,
            shift_second,
        ]
        widths = [v.shape[0] for v in small]
        far_pos = chip_pos // NEAR
        here = (n_seq, n_chip)
        early = jnp.concatenate([weight_qkv, weight_out], axis=1)
        early_stack, start, early_hops = line_gather(early, n_chip, far_pos)
        half = early.shape[1] // 2
        a_parts, a_rel, a_whole, a_last = near_gather(
            early_stack, start, length, 0, half, near_a, *here, ()
        )
        b_parts, b_rel, b_whole, b_last = near_gather(
            early_stack, start, length, half, 2 * half, near_b, *here, ()
        )
        vec_parts, vec_rel = gather_blocks(
            after(jnp.concatenate(small), early_hops[0])[None], chip_order(n_chip), *here
        )
        own_rows = weight_in.shape[0]
        late = jnp.concatenate(
            [weight_in] + [weight_back[i : i + own_rows] for i in range(0, weight_back.shape[0], own_rows)],
            axis=1,
        )
        late_stack, start, _ = line_gather(after(late, *early_hops), n_chip, far_pos)
        in_parts, in_rel, in_whole, in_last = near_gather(
            late_stack, start, length, 0, FF, near_a, *here, (a_last, b_last)
        )
        back_parts, back_rel, back_whole, back_last = near_gather(
            late_stack, start, length, FF, 2 * FF, near_b, *here, (a_last, b_last)
        )

        spot = (seq_pos, chip_pos, n_chip)
        qk_mat = reorder_columns(a_parts, a_rel, *spot, 2)
        vo_mat = reorder_columns(b_parts, b_rel, *spot, 2)
        v_mat, out_mat = vo_mat[:, :D], vo_mat[:, D:]
        in_mat = reorder_columns(in_parts, in_rel, *spot, 4)
        back_mat = reorder_rows(back_parts, back_rel, *spot, FF // D)

        wanted = jnp.bitwise_xor(me, jnp.arange(devices, dtype=jnp.int32))
        spots = jnp.asarray(vec_rel, jnp.int32)
        pick = (wanted[:, None] == spots[None, :]).astype(BF)
        vec_all = dot_plain(pick, jnp.concatenate(vec_parts, axis=0)[:, 0])
        vectors, at = [], 0
        for width in widths:
            vectors.append(vec_all[:, at : at + width].reshape(-1))
            at += width
        qv_vec, out_vec, in_vec, back_vec, gain_one, shift_one, gain_two, shift_two = vectors

        def bring(rows):
            if not swapped:
                return rows[:, 0].reshape(MB * rows_here, D)
            mine = lax.dynamic_index_in_dim(rows[:, 0], seq_pos, 0, keepdims=False)
            other = lax.dynamic_index_in_dim(rows[:, 0], 1 - seq_pos, 0, keepdims=False)
            return jnp.concatenate([mine, swap(other, "seq", n_seq, 1)], axis=0)

        def bring_back(rows):
            if not swapped:
                return rows.reshape(MB, 1, rows_here, D)
            mine, other = rows[:rows_here], swap(rows[rows_here:], "seq", n_seq, 1)
            first = seq_pos == 0
            return jnp.stack([jnp.where(first, mine, other), jnp.where(first, other, mine)])[
                :, None
            ]

        ends = jnp.cumsum(lengths[:, 0], axis=1)
        if swapped:
            ids = lax.dynamic_index_in_dim(order[:, 0], seq_pos, 0, keepdims=False)
            ids = jnp.concatenate(
                [
                    lax.dynamic_slice_in_dim(ids, seq_pos * rows_here, rows_here, 0),
                    lax.dynamic_slice_in_dim(ids, (1 - seq_pos) * rows_here, rows_here, 0),
                ]
            )
            qpos = kpos = ids[None]
            ends = lax.dynamic_index_in_dim(ends, seq_pos, 0, keepdims=True)
        else:
            kpos = order[:, 0]
            qpos = lax.dynamic_slice_in_dim(kpos, seq_pos * rows_here, rows_here, 1)
        qstart = jnp.max(
            jnp.where(ends[:, None, :] <= qpos[:, :, None], ends[:, None, :], 0), axis=2
        )
        streams = qpos.shape[0]

        def by_stream(rows):
            return rows.reshape(streams, -1, rows.shape[-1])

        x_float = bring(inputs).astype(F32)
        grad_rows = bring(cotangent)
        grad_float = grad_rows.astype(F32)
        x_hat_one, inv_one = norm_parts(x_float)
        normed = (x_hat_one * gain_one + shift_one).astype(BF)
        q_bias = jnp.concatenate([qv_vec[:D], jnp.zeros((D,), F32)])
        qk = by_stream((dot_plain(normed, qk_mat) + q_bias).astype(BF))
        value_rows = by_stream((dot_plain(normed, v_mat) + qv_vec[D:]).astype(BF))
        pairs = HEADS // 2
        if not swapped:
            q = (qk, 0)
            k = (lax.all_gather(qk[:, :, D:], "seq", axis=1, tiled=True), 0)
            v = (lax.all_gather(value_rows, "seq", axis=1, tiled=True), 0)
        if swapped:
            qk, value_rows, _, _ = lax.optimization_barrier(
                (qk, value_rows, in_whole, back_whole)
            )
            q, k, v = (qk, 0), (qk, pairs), (value_rows, 0)
        attn_heads, probs = attend(q, k, v, qpos, qstart, kpos)
        attn_heads = attn_heads.reshape(-1, D)
        mid_stream = x_float + dot_plain(attn_heads, out_mat) + out_vec
        x_hat_two, inv_two = norm_parts(mid_stream)
        normed_two = (x_hat_two * gain_two + shift_two).astype(BF)
        pre_act = dot_plain(normed_two, in_mat) + in_vec
        hidden_float, gelu_pull = jax.vjp(gelu_tanh, pre_act)
        hidden = hidden_float.astype(BF)
        result = mid_stream + dot_plain(hidden, back_mat) + back_vec
        block_out = bring_back(result.astype(BF))

        top_mine = split_bit(seq_pos, top_seq)

        def halves(left, right):
            half = left.shape[1] // 2

            def part(which):
                return dot_first(
                    lax.dynamic_slice_in_dim(left, which * half, half, 1), right
                ).astype(BF)

            return part(1 - top_mine), part(top_mine)

        def exchange(give, keep, near):
            recv = swap(give, "seq", n_seq, top_seq)
            shape = (devices // 2, give.shape[0] // (devices // 2), give.shape[1])
            return scatter_near(
                keep.reshape(shape),
                recv.reshape(shape),
                near,
                n_seq,
                n_chip,
                seq_pos,
                chip_pos,
                BF,
            )

        back_give, back_keep = halves(hidden, grad_rows)
        back_sum, back_gave = exchange(back_give, back_keep, near_b)
        d_back_vec = jnp.sum(grad_float, axis=0)
        d_hidden = dot_last(after(grad_rows, back_give, back_keep), back_mat)
        d_pre = after(gelu_pull(d_hidden)[0].astype(BF), back_gave[-2])
        in_give, in_keep = halves(normed_two, d_pre)
        in_sum, in_gave = exchange(in_give, in_keep, near_a)
        d_pre = after(d_pre, in_give, in_keep)
        d_in_vec = jnp.sum(d_pre.astype(F32), axis=0)
        d_norm_two = dot_last(d_pre, in_mat)
        d_gain_two = jnp.sum(d_norm_two * x_hat_two, axis=0)
        d_shift_two = jnp.sum(d_norm_two, axis=0)
        d_mid = grad_float + norm_back(d_norm_two, x_hat_two, inv_two, gain_two)
        d_out_vec = jnp.sum(d_mid, axis=0)
        d_mid_low = after(d_mid.astype(BF), in_gave[-2])
        d_heads = by_stream(dot_last(d_mid_low, out_mat).astype(BF))
        d_query, d_keys, d_values = attend_back(q, k, v, d_heads, probs)
        if not swapped:
            d_keys = lax.psum_scatter(d_keys, "seq", scatter_dimension=1, tiled=True)
            d_values = lax.psum_scatter(d_values, "seq", scatter_dimension=1, tiled=True)
        d_qk = jnp.concatenate([d_query, d_keys], axis=2).reshape(-1, 2 * D)
        d_values = d_values.reshape(-1, D)
        d_qk, d_values, _, _ = lax.optimization_barrier(
            (d_qk, d_values, back_gave[-1], in_gave[-1])
        )
        qk_give, qk_keep = halves(normed, d_qk)
        v_give, v_keep = halves(normed, d_values)
        out_give, out_keep = halves(attn_heads, d_mid_low)
        qk_sum, _ = exchange(qk_give, qk_keep, near_a)
        vo_sum, _ = exchange(
            jnp.concatenate([v_give, out_give], axis=1),
            jnp.concatenate([v_keep, out_keep], axis=1),
            near_b,
        )
        groups = back_sum.shape[1] // own_rows
        back_wide = [back_sum[:, i * own_rows : (i + 1) * own_rows] for i in range(groups)]
        late_sum = scatter_line(
            jnp.concatenate([in_sum] + back_wide, axis=2), n_chip, far_pos, BF
        )
        early_sum = scatter_line(
            jnp.concatenate([qk_sum, vo_sum], axis=2), n_chip, far_pos, BF
        )
        d_in_mat = late_sum[:, :FF]
        d_back_mat = jnp.concatenate(
            [late_sum[:, FF + i * D : FF + (i + 1) * D] for i in range(groups)], axis=0
        )
        d_qkv_mat, d_out_mat = early_sum[:, : 3 * D], early_sum[:, 3 * D :]
        d_qk_late, d_values_late = lax.optimization_barrier(
            (d_qk, d_values, qk_give, qk_keep, v_give, v_keep)
        )[:2]
        q_sums = jnp.sum(d_qk_late[:, :D].astype(F32), axis=0)
        v_sums = jnp.sum(d_values_late.astype(F32), axis=0)
        d_qv_vec = jnp.concatenate([q_sums, v_sums])
        d_norm_one = dot_last(d_qk_late, qk_mat) + dot_last(d_values_late, v_mat)
        d_gain_one = jnp.sum(d_norm_one * x_hat_one, axis=0)
        d_shift_one = jnp.sum(d_norm_one, axis=0)
        d_inputs = d_mid + norm_back(d_norm_one, x_hat_one, inv_one, gain_one)
        input_grad = bring_back(d_inputs.astype(BF))

        vec_grads = [
            d_qv_vec,
            d_out_vec,
            d_in_vec,
            d_back_vec,
            d_gain_one,
            d_shift_one,
            d_gain_two,
            d_shift_two,
        ]
        packed = jnp.concatenate([g.reshape(devices, -1) for g in vec_grads], axis=1)
        packed = packed.reshape(2, devices // 2, 1, -1)
        give = lax.dynamic_index_in_dim(packed, 1 - top_mine, 0, keepdims=False)
        keep = lax.dynamic_index_in_dim(packed, top_mine, 0, keepdims=False)
        vec_near, _ = scatter_near(
            keep,
            swap(give, "seq", n_seq, top_seq),
            near_a,
            n_seq,
            n_chip,
            seq_pos,
            chip_pos,
            F32,
        )
        vec_sum = scatter_line(vec_near, n_chip, far_pos, F32)[0]
        g_out, at = [], 0
        for width in widths:
            g_out.append(vec_sum[at : at + width])
            at += width
        g_qv, g_out_vec, g_in, g_back, g_gain1, g_shift1, g_gain2, g_shift2 = g_out
        return (
            block_out,
            input_grad,
            d_qkv_mat,
            g_qv,
            d_out_mat,
            g_out_vec,
            d_in_mat,
            g_in,
            d_back_mat,
            g_back,
            g_gain1,
            g_shift1,
            g_gain2,
            g_shift2,
        )

    tokens, sharded, vector = P(None, "fsdp", "seq", None), P(("seq", "fsdp"), None), P(("seq", "fsdp"))
    streams_spec = P(None, "fsdp", None)
    return jax.shard_map(
        local,
        mesh=mesh,
        in_specs=(tokens, streams_spec, streams_spec, tokens) + (sharded, vector) * 4 + (vector,) * 4,
        out_specs=(tokens, tokens) + (sharded, vector) * 4 + (vector,) * 4,
        check_vma=False,
    )
```

```python
import jax
import jax.numpy as jnp
from jax import lax
from jax.experimental import pallas as pl
from jax.experimental.pallas import tpu as pltpu
from jax.sharding import PartitionSpec as P

D = 768
HEADS = 12
HD = 64
FF = 3072
MB = 2
PAIR = 2 * HD

eps = 1e-05
score_scale = 0.125
BF = jnp.bfloat16
F32 = jnp.float32


def norm_parts(values):
    row_mean = jnp.mean(values, axis=-1, keepdims=True)
    centred = values - row_mean
    inv_std = lax.rsqrt(jnp.mean(centred * centred, axis=-1, keepdims=True) + eps)
    return (centred * inv_std, inv_std)


def norm_back(grad_norm, x_hat, inv_std, gain):
    scaled = grad_norm * gain
    return inv_std * (
        scaled
        - jnp.mean(scaled, axis=-1, keepdims=True)
        - x_hat * jnp.mean(scaled * x_hat, axis=-1, keepdims=True)
    )


def gelu_tanh(values):
    return (
        0.5
        * values
        * (1.0 + jnp.tanh(0.7978845608028654 * (values + 0.044715 * values * values * values)))
    )


def dot_first(left, right):
    return lax.dot_general(left, right, (((0,), (0,)), ((), ())), preferred_element_type=F32)


def dot_last(left, right):
    return lax.dot_general(left, right, (((1,), (1,)), ((), ())), preferred_element_type=F32)


def dot_plain(left, right):
    return jnp.dot(left, right, preferred_element_type=F32)


def attend_kernel(q_ref, k_ref, v_ref, qpos_ref, qstart_ref, kpos_ref, out_ref, prob_ref, bias_ref):
    @pl.when(pl.program_id(1) == 0)
    def _():
        kpos = kpos_ref[0]
        seen = (kpos <= qpos_ref[0]) & (kpos >= qstart_ref[0])
        bias_ref[...] = jnp.where(seen, 0.0, -1e30)

    q, k, v = q_ref[0], k_ref[0], v_ref[0]
    lane = lax.broadcasted_iota(jnp.int32, q.shape, 1)
    scaled = q * jnp.asarray(score_scale, BF)
    halves = []
    for j in range(2):
        q_head = jnp.where((lane // HD) == j, scaled, jnp.zeros_like(scaled))
        scores = dot_last(k, q_head) + bias_ref[...]
        col_max = jnp.max(scores, axis=0, keepdims=True)
        expo = jnp.exp(scores - col_max)
        probs = (expo * (1.0 / jnp.sum(expo, axis=0, keepdims=True))).astype(BF)
        prob_ref[0, j] = probs
        halves.append(dot_first(v, probs))
    row = lax.broadcasted_iota(jnp.int32, halves[0].shape, 0)
    out_ref[0] = jnp.where(row < HD, halves[0], halves[1]).T.astype(BF)


def attend_back_kernel(q_ref, k_ref, v_ref, dh_ref, prob_ref, dq_ref, dk_ref, dv_ref):
    q, k, v, dh = q_ref[0], k_ref[0], v_ref[0], dh_ref[0]
    lane = lax.broadcasted_iota(jnp.int32, dh.shape, 1)
    dq, dk, dv = [], [], []
    for j in range(2):
        probs = prob_ref[0, j]
        dh_head = jnp.where((lane // HD) == j, dh, jnp.zeros_like(dh))
        d_prob = dot_last(v, dh_head)
        wide = probs.astype(F32)
        moved = wide * d_prob
        centre = jnp.sum(moved, axis=0, keepdims=True)
        d_scores = (moved - wide * centre).astype(BF)
        dq.append(dot_first(k, d_scores))
        dk.append(dot_plain(d_scores, q))
        dv.append(dot_plain(probs, dh))
    row = lax.broadcasted_iota(jnp.int32, dq[0].shape, 0)
    col = lax.broadcasted_iota(jnp.int32, dk[0].shape, 1)
    dq_ref[0] = (score_scale * jnp.where(row < HD, dq[0], dq[1])).T.astype(BF)
    dk_ref[0] = (score_scale * jnp.where(col < HD, dk[0], dk[1])).astype(BF)
    dv_ref[0] = jnp.where(col < HD, dv[0], dv[1]).astype(BF)


def cols(rows, offset):
    return pl.BlockSpec((1, rows, PAIR), lambda s, h: (s, 0, h + offset))


def attend(q, k, v, qpos, qstart, kpos):
    (q_arr, q_off), (k_arr, k_off), (v_arr, v_off) = q, k, v
    streams, rows = q_arr.shape[:2]
    keys = k_arr.shape[1]
    pairs = HEADS // 2
    return pl.pallas_call(
        attend_kernel,
        grid=(streams, pairs),
        in_specs=[
            cols(rows, q_off),
            cols(keys, k_off),
            cols(keys, v_off),
            pl.BlockSpec((1, 1, rows), lambda s, h: (s, 0, 0)),
            pl.BlockSpec((1, 1, rows), lambda s, h: (s, 0, 0)),
            pl.BlockSpec((1, keys, 1), lambda s, h: (s, 0, 0)),
        ],
        out_specs=[
            cols(rows, 0),
            pl.BlockSpec((1, 2, keys, rows), lambda s, h: (s, h, 0, 0)),
        ],
        out_shape=[
            jax.ShapeDtypeStruct((streams, rows, D), BF),
            jax.ShapeDtypeStruct((streams, HEADS, keys, rows), BF),
        ],
        scratch_shapes=[pltpu.VMEM((keys, rows), F32)],
        cost_estimate=pl.CostEstimate(
            flops=4 * streams * HEADS * rows * keys * PAIR,
            transcendentals=streams * HEADS * rows * keys,
            bytes_accessed=2 * streams * (HEADS * rows * keys + 4 * rows * D),
        ),
        name="attend",
    )(q_arr, k_arr, v_arr, qpos[:, None, :], qstart[:, None, :], kpos[:, :, None])


def attend_back(q, k, v, d_heads, probs):
    (q_arr, q_off), (k_arr, k_off), (v_arr, v_off) = q, k, v
    streams, rows = q_arr.shape[:2]
    keys = k_arr.shape[1]
    pairs = HEADS // 2
    return pl.pallas_call(
        attend_back_kernel,
        grid=(streams, pairs),
        in_specs=[
            cols(rows, q_off),
            cols(keys, k_off),
            cols(keys, v_off),
            cols(rows, 0),
            pl.BlockSpec((1, 2, keys, rows), lambda s, h: (s, h, 0, 0)),
        ],
        out_specs=[cols(rows, 0), cols(keys, 0), cols(keys, 0)],
        out_shape=[
            jax.ShapeDtypeStruct((streams, rows, D), BF),
            jax.ShapeDtypeStruct((streams, keys, D), BF),
            jax.ShapeDtypeStruct((streams, keys, D), BF),
        ],
        cost_estimate=pl.CostEstimate(
            flops=8 * streams * HEADS * rows * keys * PAIR,
            transcendentals=0,
            bytes_accessed=2 * streams * (HEADS * rows * keys + 7 * rows * D),
        ),
        name="attend_back",
    )(q_arr, k_arr, v_arr, d_heads, probs)


def after(value, *others):
    return lax.optimization_barrier((value,) + others)[0]


def bits_of(count):
    return [1 << b for b in range(count.bit_length() - 1)]


def swap(value, axis, count, bit):
    return lax.ppermute(value, axis, [(i, i ^ bit) for i in range(count)])


def after(value, *others):
    return lax.optimization_barrier((value,) + others)[0]


NEAR = 4


def far_shift(value, n_chip, by):
    length = n_chip // NEAR
    pairs = [
        (z * NEAR + n, (z + by) % length * NEAR + n) for z in range(length) for n in range(NEAR)
    ]
    return lax.ppermute(value, "fsdp", pairs)


def far_gather(shard, n_chip):
    return [shard] + [far_shift(shard, n_chip, k) for k in range(1, n_chip // NEAR)]


def pack_kernel(count, *refs):
    ins, outs = refs[:count], refs[count:]
    at = 0
    for out_ref in outs:
        width = out_ref.shape[2]
        for i, in_ref in enumerate(ins):
            out_ref[i] = in_ref[:, at : at + width]
        at += width


def pack(parts, widths):
    rows = parts[0].shape[0]
    return pl.pallas_call(
        lambda *refs: pack_kernel(len(parts), *refs),
        out_shape=[jax.ShapeDtypeStruct((len(parts), rows, w), BF) for w in widths],
        cost_estimate=pl.CostEstimate(
            flops=0, transcendentals=0, bytes_accessed=4 * len(parts) * rows * sum(widths)
        ),
        name="pack",
    )(*parts)


def near_rel(length, bits, n_seq):
    rel = [(z, n, 0) for n in (0, bits[0], bits[1], bits[0] ^ bits[1]) for z in range(length)]
    for bit in bits_of(n_seq):
        rel = rel + [(z, n, c ^ bit) for z, n, c in rel]
    return rel


def seq_parts(part, n_seq):
    parts = [part]
    for bit in bits_of(n_seq):
        parts = parts + [swap(p, "seq", n_seq, bit) for p in parts]
    return parts


def interleave(first, second):
    return [part for pair in zip(first, second) for part in pair]


def reorder_kernel(counts, table_ref, *refs):
    ins, out_ref = refs[: len(counts)], refs[len(counts)]
    place = 0
    for part_ref, count in zip(ins, counts):
        for i in range(count):
            out_ref[table_ref[place]] = part_ref[i]
            place += 1


def places(parts, rel, seq_pos, chip_pos, n_chip, chunks):
    rows, width = parts[0].shape[1:]
    counts = [part.shape[0] for part in parts]
    total = sum(counts)
    step = width // chunks
    far, near, seq = (jnp.asarray(col, jnp.int32) for col in zip(*rel))
    table = (
        jnp.bitwise_xor(seq_pos, seq) * n_chip
        + (chip_pos // NEAR - far) % (n_chip // NEAR) * NEAR
        + jnp.bitwise_xor(chip_pos % NEAR, near)
    )
    return table, counts, total, rows, width, step


def reorder_columns(parts, rel, seq_pos, chip_pos, n_chip, chunks):
    table, counts, total, rows, width, step = places(
        parts, rel, seq_pos, chip_pos, n_chip, chunks
    )
    out = pl.pallas_call(
        lambda *refs: reorder_kernel(counts, *refs),
        grid=(chunks,),
        in_specs=[pl.BlockSpec(memory_space=pltpu.SMEM)]
        + [pl.BlockSpec((count, rows, step), lambda c: (0, 0, c)) for count in counts],
        out_specs=pl.BlockSpec((total, rows, step), lambda c: (0, 0, c)),
        out_shape=jax.ShapeDtypeStruct((total, rows, width), BF),
        cost_estimate=pl.CostEstimate(
            flops=0, transcendentals=0, bytes_accessed=4 * total * rows * width
        ),
        name="reorder",
    )(table, *parts)
    return out.reshape(total * rows, width)


def reorder_rows(parts, rel, seq_pos, chip_pos, n_chip, chunks):
    table, counts, total, rows, width, step = places(
        parts, rel, seq_pos, chip_pos, n_chip, chunks
    )
    out = pl.pallas_call(
        lambda *refs: reorder_kernel(counts, *refs),
        grid=(chunks,),
        in_specs=[pl.BlockSpec(memory_space=pltpu.SMEM)]
        + [pl.BlockSpec((count, rows, step), lambda c: (0, 0, c)) for count in counts],
        out_specs=pl.BlockSpec((total, None, rows, step), lambda c: (0, c, 0, 0)),
        out_shape=jax.ShapeDtypeStruct((total, chunks, rows, step), BF),
        cost_estimate=pl.CostEstimate(
            flops=0, transcendentals=0, bytes_accessed=4 * total * rows * width
        ),
        name="reorder_rows",
    )(table, *parts)
    return out.reshape(total * chunks * rows, step)


def split_bit(index, bit):
    return (index // bit) % 2


class Scatter:
    def __init__(self, keep, recv, near, where, wire):
        self.n_seq, self.n_chip, self.seq_pos, self.chip_pos = where
        self.wire = wire
        rows, width = keep.shape[1:]
        seq_bits = [("seq", b) for b in bits_of(self.n_seq)[:-1][::-1]]
        self.left = seq_bits + [("far", 0), ("fsdp", 2), ("fsdp", 1)]
        shape = (2,) * len(seq_bits) + (self.n_chip // NEAR, 2, 2, rows, width)
        self.total = (keep.astype(F32) + recv.astype(F32)).astype(wire).reshape(shape)
        for item in seq_bits:
            self.send(item)
            self.add()
        self.send(("fsdp", near[0]))
        self.near = near

    def send(self, item):
        axis, bit = item
        at_seq = axis == "seq"
        mine = split_bit(self.seq_pos if at_seq else self.chip_pos, bit)
        place = self.left.index(item)
        self.give = lax.dynamic_index_in_dim(self.total, 1 - mine, place, keepdims=False)
        self.got = swap(self.give, axis, self.n_seq if at_seq else self.n_chip, bit)
        self.kept = lax.dynamic_index_in_dim(self.total, mine, place, keepdims=False)
        self.left.remove(item)

    def add(self, *gate):
        got = after(self.got, *gate) if gate else self.got
        self.total = (self.kept.astype(F32) + got.astype(F32)).astype(self.wire)

    def second(self, *gate):
        self.add(*gate)
        self.send(("fsdp", self.near[1]))
        return self.give

    def blocks(self, *gate):
        self.add(*gate)
        return self.total


def unpack_kernel(counts, far_ref, *refs):
    ins, outs = refs[: len(counts)], refs[len(counts) :]
    length = len(outs)
    for k, out_ref in enumerate(outs):
        block = lax.rem(far_ref[0] + k, length)
        at = 0
        for in_ref, pieces in zip(ins, counts):
            rows, width = out_ref.shape[0], in_ref.shape[-1]
            for j in range(pieces):
                out_ref[:, at : at + width] = in_ref[block, j]
                at += width


def unpack(parts, own_rows, far_pos):
    length = parts[0].shape[0]
    counts = [part.shape[1] // own_rows for part in parts]
    parts = [part.reshape(length, n, own_rows, part.shape[2]) for part, n in zip(parts, counts)]
    width = sum(part.shape[1] * part.shape[3] for part in parts)
    vmem = pl.BlockSpec(memory_space=pltpu.VMEM)
    return pl.pallas_call(
        lambda *refs: unpack_kernel(counts, *refs),
        in_specs=[pl.BlockSpec(memory_space=pltpu.SMEM)] + [vmem] * len(parts),
        out_shape=[jax.ShapeDtypeStruct((own_rows, width), BF)] * length,
        cost_estimate=pl.CostEstimate(
            flops=0, transcendentals=0, bytes_accessed=4 * length * own_rows * width
        ),
        name="unpack",
    )(far_pos.reshape(1).astype(jnp.int32), *parts)


def far_sum(blocks, n_chip):
    total = blocks[0].astype(F32)
    for k, block in enumerate(blocks[1:], 1):
        total = total + far_shift(block, n_chip, k).astype(F32)
    return total


def solution(mesh):
    n_seq, n_chip = mesh.shape["seq"], mesh.shape["fsdp"]
    devices = n_seq * n_chip
    near_a, near_b = (2, 1), (1, 2)
    length = n_chip // NEAR
    top_seq = n_seq // 2
    swapped = n_seq == MB

    def local(
        inputs,
        order,
        lengths,
        cotangent,
        weight_qkv,
        bias_qv,
        weight_out,
        bias_out,
        weight_in,
        bias_in,
        weight_back,
        bias_back,
        gain_first,
        shift_first,
        gain_second,
        shift_second,
    ):
        seq_pos, chip_pos = lax.axis_index("seq"), lax.axis_index("fsdp")
        me = seq_pos * n_chip + chip_pos
        rows_here = inputs.shape[2]

        small = [
            bias_qv,
            bias_out,
            bias_in,
            bias_back,
            gain_first,
            shift_first,
            gain_second,
            shift_second,
        ]
        widths = [v.shape[0] for v in small]
        far_pos = chip_pos // NEAR
        own_rows = weight_in.shape[0]

        early = jnp.concatenate([weight_qkv, weight_out], axis=1)
        half = early.shape[1] // 2
        early_far = far_gather(early, n_chip)
        vec = after(jnp.concatenate(small)[None, :], early)
        vec_far = far_gather(vec, n_chip)
        late = jnp.concatenate(
            [weight_in]
            + [weight_back[i : i + own_rows] for i in range(0, weight_back.shape[0], own_rows)],
            axis=1,
        )
        late_far = far_gather(after(late, *early_far), n_chip)

        def near(block, bit):
            return swap(block, "fsdp", n_chip, bit)

        def join(block, other):
            return jnp.concatenate([block, other], axis=0)

        a_block, b_block = pack(early_far, [half, half])
        vec_block = jnp.stack([after(v, *early_far) for v in vec_far])
        a_first, b_first = near(a_block, near_a[0]), near(b_block, near_b[0])
        vec_whole = join(vec_block, after(near(vec_block, near_a[0]), a_first, b_first))
        a_whole, b_whole = join(a_block, a_first), join(b_block, b_first)
        a_last, b_last = near(a_whole, near_a[1]), near(b_whole, near_b[1])
        vec_last = after(near(vec_whole, near_a[1]), a_last, b_last)
        a_parts = interleave(seq_parts(a_whole, n_seq), seq_parts(a_last, n_seq))
        b_parts = interleave(seq_parts(b_whole, n_seq), seq_parts(b_last, n_seq))
        vec_parts = seq_parts(join(vec_whole, vec_last), n_seq)
        in_block, back_block = pack(
            [after(part, a_last, b_last) for part in late_far], [FF, FF]
        )
        in_first, back_first = near(in_block, near_a[0]), near(back_block, near_b[0])

        a_rel, b_rel = near_rel(length, near_a, n_seq), near_rel(length, near_b, n_seq)
        spot = (seq_pos, chip_pos, n_chip)
        qk_mat = reorder_columns(a_parts, a_rel, *spot, 2)
        vo_mat = reorder_columns(b_parts, b_rel, *spot, 2)
        v_mat, out_mat = vo_mat[:, :D], vo_mat[:, D:]

        holders = places(vec_parts, a_rel, *spot, 1)[0]
        pick = (jnp.arange(devices, dtype=jnp.int32)[:, None] == holders[None, :]).astype(BF)
        vec_all = dot_plain(pick, jnp.concatenate(vec_parts, axis=0)[:, 0])
        vectors, at = [], 0
        for width in widths:
            vectors.append(vec_all[:, at : at + width].reshape(-1))
            at += width
        qv_vec, out_vec, in_vec, back_vec, gain_one, shift_one, gain_two, shift_two = vectors

        def bring(rows):
            if not swapped:
                return rows[:, 0].reshape(MB * rows_here, D)
            mine = lax.dynamic_index_in_dim(rows[:, 0], seq_pos, 0, keepdims=False)
            other = lax.dynamic_index_in_dim(rows[:, 0], 1 - seq_pos, 0, keepdims=False)
            return jnp.concatenate([mine, swap(other, "seq", n_seq, 1)], axis=0)

        def bring_back(rows):
            if not swapped:
                return rows.reshape(MB, 1, rows_here, D)
            mine, other = rows[:rows_here], swap(rows[rows_here:], "seq", n_seq, 1)
            first = seq_pos == 0
            return jnp.stack([jnp.where(first, mine, other), jnp.where(first, other, mine)])[
                :, None
            ]

        ends = jnp.cumsum(lengths[:, 0], axis=1)
        if swapped:
            ids = lax.dynamic_index_in_dim(order[:, 0], seq_pos, 0, keepdims=False)
            ids = jnp.concatenate(
                [
                    lax.dynamic_slice_in_dim(ids, seq_pos * rows_here, rows_here, 0),
                    lax.dynamic_slice_in_dim(ids, (1 - seq_pos) * rows_here, rows_here, 0),
                ]
            )
            qpos = kpos = ids[None]
            ends = lax.dynamic_index_in_dim(ends, seq_pos, 0, keepdims=True)
        else:
            kpos = order[:, 0]
            qpos = lax.dynamic_slice_in_dim(kpos, seq_pos * rows_here, rows_here, 1)
        qstart = jnp.max(
            jnp.where(ends[:, None, :] <= qpos[:, :, None], ends[:, None, :], 0), axis=2
        )
        streams = qpos.shape[0]

        def by_stream(rows):
            return rows.reshape(streams, -1, rows.shape[-1])

        x_float = bring(inputs).astype(F32)
        grad_rows = bring(cotangent)
        grad_float = grad_rows.astype(F32)
        x_hat_one, inv_one = norm_parts(x_float)
        normed = (x_hat_one * gain_one + shift_one).astype(BF)
        q_bias = jnp.concatenate([qv_vec[:D], jnp.zeros((D,), F32)])
        qk = by_stream((dot_plain(normed, qk_mat) + q_bias).astype(BF))
        value_rows = by_stream((dot_plain(normed, v_mat) + qv_vec[D:]).astype(BF))
        pairs = HEADS // 2
        if not swapped:
            q = (qk, 0)
            k = (lax.all_gather(qk[:, :, D:], "seq", axis=1, tiled=True), 0)
            v = (lax.all_gather(value_rows, "seq", axis=1, tiled=True), 0)
        in_whole = join(in_block, after(in_first, qk))
        back_whole = join(back_block, after(back_first, value_rows))
        if swapped:
            qk, value_rows, _, _ = lax.optimization_barrier(
                (qk, value_rows, in_whole, back_whole)
            )
            q, k, v = (qk, 0), (qk, pairs), (value_rows, 0)
        attn_heads, probs = attend(q, k, v, qpos, qstart, kpos)
        in_last = near(in_whole, near_a[1])
        back_last = near(back_whole, near_b[1])
        in_wholes = seq_parts(in_whole, n_seq)
        back_wholes = seq_parts(back_whole, n_seq)
        attn_heads = attn_heads.reshape(-1, D)
        mid_stream = x_float + dot_plain(attn_heads, out_mat) + out_vec
        x_hat_two, inv_two = norm_parts(mid_stream)
        normed_two = (x_hat_two * gain_two + shift_two).astype(BF)
        in_last, back_last = after(in_last, normed_two), after(back_last, normed_two)
        in_parts = interleave(in_wholes, seq_parts(in_last, n_seq))
        back_parts = interleave(back_wholes, seq_parts(back_last, n_seq))
        in_mat = reorder_columns(in_parts, a_rel, *spot, 4)
        back_mat = reorder_rows(back_parts, b_rel, *spot, FF // D)
        pre_act = dot_plain(normed_two, in_mat) + in_vec
        hidden_float, gelu_pull = jax.vjp(gelu_tanh, pre_act)
        hidden = hidden_float.astype(BF)
        top_mine = split_bit(seq_pos, top_seq)

        def halves(left, right):
            half = left.shape[1] // 2

            def part(which):
                return dot_first(
                    lax.dynamic_slice_in_dim(left, which * half, half, 1), right
                ).astype(BF)

            return part(1 - top_mine), part(top_mine)

        where = (n_seq, n_chip, seq_pos, chip_pos)

        def scatter(give, keep, near, wire=BF):
            recv = swap(give, "seq", n_seq, top_seq)
            shape = (devices // 2, give.shape[0] // (devices // 2), give.shape[1])
            return Scatter(keep.reshape(shape), recv.reshape(shape), near, where, wire)

        back_sum = scatter(*halves(hidden, grad_rows), near_b)
        d_hidden = dot_last(after(grad_rows, back_sum.give), back_mat)
        d_pre = gelu_pull(d_hidden)[0].astype(BF)
        in_sum = scatter(*halves(normed_two, d_pre), near_a)
        d_pre = after(d_pre, in_sum.give)
        d_norm_two = dot_last(d_pre, in_mat)
        d_mid = grad_float + norm_back(d_norm_two, x_hat_two, inv_two, gain_two)
        d_mid_low = d_mid.astype(BF)
        d_heads = by_stream(dot_last(d_mid_low, out_mat).astype(BF))
        d_heads = after(d_heads, back_sum.second(d_heads))
        d_query, d_keys, d_values = attend_back(q, k, v, d_heads, probs)
        in_give = in_sum.second(d_query)
        if not swapped:
            d_keys = lax.psum_scatter(d_keys, "seq", scatter_dimension=1, tiled=True)
            d_values = lax.psum_scatter(d_values, "seq", scatter_dimension=1, tiled=True)
        d_qk = jnp.concatenate([d_query, d_keys], axis=2).reshape(-1, 2 * D)
        d_values = d_values.reshape(-1, D)
        d_qk, d_values, _ = lax.optimization_barrier((d_qk, d_values, in_give))
        qk_give, qk_keep = halves(normed, d_qk)
        v_give, v_keep = halves(normed, d_values)
        out_give, out_keep = halves(attn_heads, d_mid_low)
        vo_sum = scatter(
            jnp.concatenate([v_give, out_give], axis=1),
            jnp.concatenate([v_keep, out_keep], axis=1),
            near_b,
        )
        qk_sum = scatter(qk_give, qk_keep, near_a)
        sent = (qk_sum.give, vo_sum.give)
        late_blocks = unpack(
            [in_sum.blocks(*sent), back_sum.blocks(*sent)], own_rows, far_pos
        )
        d_qk, d_values, _ = lax.optimization_barrier((d_qk, d_values, late_blocks[0]))
        d_norm_one = dot_last(d_qk, qk_mat) + dot_last(d_values, v_mat)
        d_inputs = d_mid + norm_back(d_norm_one, x_hat_one, inv_one, gain_one)
        input_grad = d_inputs.astype(BF)
        sent = (qk_sum.second(input_grad), vo_sum.second(input_grad))
        input_grad = bring_back(after(input_grad, *sent))

        hidden, d_pre, grad_late, d_qk, d_values, d_mid_late, _, _ = lax.optimization_barrier(
            (hidden, d_pre, grad_float, d_qk, d_values, d_mid) + sent
        )
        result = mid_stream + dot_plain(hidden, back_mat) + back_vec
        block_out = result.astype(BF)
        d_back_vec = jnp.sum(grad_late, axis=0)
        d_in_vec = jnp.sum(d_pre.astype(F32), axis=0)
        d_gain_two = jnp.sum(d_norm_two * x_hat_two, axis=0)
        d_shift_two = jnp.sum(d_norm_two, axis=0)
        d_out_vec = jnp.sum(d_mid_late, axis=0)
        q_sums = jnp.sum(d_qk[:, :D].astype(F32), axis=0)
        v_sums = jnp.sum(d_values.astype(F32), axis=0)
        d_qv_vec = jnp.concatenate([q_sums, v_sums])
        d_gain_one = jnp.sum(d_norm_one * x_hat_one, axis=0)
        d_shift_one = jnp.sum(d_norm_one, axis=0)

        vec_grads = [
            d_qv_vec,
            d_out_vec,
            d_in_vec,
            d_back_vec,
            d_gain_one,
            d_shift_one,
            d_gain_two,
            d_shift_two,
        ]
        packed = jnp.concatenate([g.reshape(devices, -1) for g in vec_grads], axis=1)
        packed = packed.reshape(2, devices // 2, -1)
        give = lax.dynamic_index_in_dim(packed, 1 - top_mine, 0, keepdims=False)
        keep = lax.dynamic_index_in_dim(packed, top_mine, 0, keepdims=False)
        vec_scatter = scatter(give, keep, near_a, F32)
        early_blocks = unpack(
            [qk_sum.blocks(vec_scatter.give), vo_sum.blocks(vec_scatter.give)], own_rows, far_pos
        )
        block_out = bring_back(after(block_out, early_blocks[0]))
        vec_scatter.second()
        vec_blocks = vec_scatter.blocks()
        vec_blocks = [
            lax.dynamic_index_in_dim(vec_blocks, (far_pos + i) % length, 0, keepdims=False)
            for i in range(length)
        ]
        late_sum = far_sum(late_blocks, n_chip)
        early_sum = far_sum(early_blocks, n_chip)
        vec_sum = far_sum(vec_blocks, n_chip)[0]
        d_in_mat = late_sum[:, :FF]
        d_back_mat = jnp.concatenate(
            [late_sum[:, i : i + D] for i in range(FF, 2 * FF, D)], axis=0
        )
        d_qkv_mat, d_out_mat = early_sum[:, : 3 * D], early_sum[:, 3 * D :]
        g_out, at = [], 0
        for width in widths:
            g_out.append(vec_sum[at : at + width])
            at += width
        g_qv, g_out_vec, g_in, g_back, g_gain1, g_shift1, g_gain2, g_shift2 = g_out
        return (
            block_out,
            input_grad,
            d_qkv_mat,
            g_qv,
            d_out_mat,
            g_out_vec,
            d_in_mat,
            g_in,
            d_back_mat,
            g_back,
            g_gain1,
            g_shift1,
            g_gain2,
            g_shift2,
        )

    tokens, sharded, vector = P(None, "fsdp", "seq", None), P(("seq", "fsdp"), None), P(("seq", "fsdp"))
    streams_spec = P(None, "fsdp", None)
    return jax.shard_map(
        local,
        mesh=mesh,
        in_specs=(tokens, streams_spec, streams_spec, tokens) + (sharded, vector) * 4 + (vector,) * 4,
        out_specs=(tokens, tokens) + (sharded, vector) * 4 + (vector,) * 4,
        check_vma=False,
    )
```

```python
import jax
import jax.numpy as jnp
from jax import lax
from jax.experimental import pallas as pl
from jax.experimental.pallas import tpu as pltpu
from jax.sharding import PartitionSpec as P

D = 768
HEADS = 12
HD = 64
FF = 3072
MB = 2
PAIR = 2 * HD

eps = 1e-05
score_scale = 0.125
BF = jnp.bfloat16
F32 = jnp.float32
SMALL = pl.CostEstimate(flops=1, transcendentals=0, bytes_accessed=1)


def norm_parts(values):
    row_mean = jnp.mean(values, axis=-1, keepdims=True)
    centred = values - row_mean
    inv_std = lax.rsqrt(jnp.mean(centred * centred, axis=-1, keepdims=True) + eps)
    return (centred * inv_std, inv_std)


def norm_back(grad_norm, x_hat, inv_std, gain):
    scaled = grad_norm * gain
    return inv_std * (
        scaled
        - jnp.mean(scaled, axis=-1, keepdims=True)
        - x_hat * jnp.mean(scaled * x_hat, axis=-1, keepdims=True)
    )


def gelu_tanh(values):
    return (
        0.5
        * values
        * (1.0 + jnp.tanh(0.7978845608028654 * (values + 0.044715 * values * values * values)))
    )


def dot_first(left, right):
    return lax.dot_general(left, right, (((0,), (0,)), ((), ())), preferred_element_type=F32)


def dot_last(left, right):
    return lax.dot_general(left, right, (((1,), (1,)), ((), ())), preferred_element_type=F32)


def dot_plain(left, right):
    return jnp.dot(left, right, preferred_element_type=F32)


def attend_kernel(q_ref, k_ref, v_ref, qpos_ref, qstart_ref, kpos_ref, out_ref, prob_ref, bias_ref):
    @pl.when(pl.program_id(1) == 0)
    def _():
        kpos = kpos_ref[0]
        seen = (kpos <= qpos_ref[0]) & (kpos >= qstart_ref[0])
        bias_ref[...] = jnp.where(seen, 0.0, -1e30)

    q, k, v = q_ref[0], k_ref[0], v_ref[0]
    lane = lax.broadcasted_iota(jnp.int32, q.shape, 1)
    scaled = q * jnp.asarray(score_scale, BF)
    halves = []
    for j in range(2):
        q_head = jnp.where((lane // HD) == j, scaled, jnp.zeros_like(scaled))
        scores = dot_last(k, q_head) + bias_ref[...]
        col_max = jnp.max(scores, axis=0, keepdims=True)
        expo = jnp.exp(scores - col_max)
        probs = (expo * (1.0 / jnp.sum(expo, axis=0, keepdims=True))).astype(BF)
        prob_ref[0, j] = probs
        halves.append(dot_first(v, probs))
    row = lax.broadcasted_iota(jnp.int32, halves[0].shape, 0)
    out_ref[0] = jnp.where(row < HD, halves[0], halves[1]).T.astype(BF)


def attend_back_kernel(q_ref, k_ref, v_ref, dh_ref, prob_ref, dq_ref, dk_ref, dv_ref):
    q, k, v, dh = q_ref[0], k_ref[0], v_ref[0], dh_ref[0]
    lane = lax.broadcasted_iota(jnp.int32, dh.shape, 1)
    dq, dk, dv = [], [], []
    for j in range(2):
        probs = prob_ref[0, j]
        dh_head = jnp.where((lane // HD) == j, dh, jnp.zeros_like(dh))
        d_prob = dot_last(v, dh_head)
        wide = probs.astype(F32)
        moved = wide * d_prob
        centre = jnp.sum(moved, axis=0, keepdims=True)
        d_scores = (moved - wide * centre).astype(BF)
        dq.append(dot_first(k, d_scores))
        dk.append(dot_plain(d_scores, q))
        dv.append(dot_plain(probs, dh))
    row = lax.broadcasted_iota(jnp.int32, dq[0].shape, 0)
    col = lax.broadcasted_iota(jnp.int32, dk[0].shape, 1)
    dq_ref[0] = (score_scale * jnp.where(row < HD, dq[0], dq[1])).T.astype(BF)
    dk_ref[0] = (score_scale * jnp.where(col < HD, dk[0], dk[1])).astype(BF)
    dv_ref[0] = jnp.where(col < HD, dv[0], dv[1]).astype(BF)


def cols(rows, offset):
    return pl.BlockSpec((1, rows, PAIR), lambda s, h: (s, 0, h + offset))


def attend(q, k, v, qpos, qstart, kpos):
    (q_arr, q_off), (k_arr, k_off), (v_arr, v_off) = q, k, v
    streams, rows = q_arr.shape[:2]
    keys = k_arr.shape[1]
    pairs = HEADS // 2
    return pl.pallas_call(
        attend_kernel,
        grid=(streams, pairs),
        in_specs=[
            cols(rows, q_off),
            cols(keys, k_off),
            cols(keys, v_off),
            pl.BlockSpec((1, 1, rows), lambda s, h: (s, 0, 0)),
            pl.BlockSpec((1, 1, rows), lambda s, h: (s, 0, 0)),
            pl.BlockSpec((1, keys, 1), lambda s, h: (s, 0, 0)),
        ],
        out_specs=[
            cols(rows, 0),
            pl.BlockSpec((1, 2, keys, rows), lambda s, h: (s, h, 0, 0)),
        ],
        out_shape=[
            jax.ShapeDtypeStruct((streams, rows, D), BF),
            jax.ShapeDtypeStruct((streams, HEADS, keys, rows), BF),
        ],
        scratch_shapes=[pltpu.VMEM((keys, rows), F32)],
        cost_estimate=SMALL,
        name="attend",
    )(q_arr, k_arr, v_arr, qpos[:, None, :], qstart[:, None, :], kpos[:, :, None])


def attend_back(q, k, v, d_heads, probs):
    (q_arr, q_off), (k_arr, k_off), (v_arr, v_off) = q, k, v
    streams, rows = q_arr.shape[:2]
    keys = k_arr.shape[1]
    pairs = HEADS // 2
    return pl.pallas_call(
        attend_back_kernel,
        grid=(streams, pairs),
        in_specs=[
            cols(rows, q_off),
            cols(keys, k_off),
            cols(keys, v_off),
            cols(rows, 0),
            pl.BlockSpec((1, 2, keys, rows), lambda s, h: (s, h, 0, 0)),
        ],
        out_specs=[cols(rows, 0), cols(keys, 0), cols(keys, 0)],
        out_shape=[
            jax.ShapeDtypeStruct((streams, rows, D), BF),
            jax.ShapeDtypeStruct((streams, keys, D), BF),
            jax.ShapeDtypeStruct((streams, keys, D), BF),
        ],
        cost_estimate=SMALL,
        name="attend_back",
    )(q_arr, k_arr, v_arr, d_heads, probs)


def after(value, *others):
    return lax.optimization_barrier((value,) + others)[0]


def bits_of(count):
    return [1 << b for b in range(count.bit_length() - 1)]


def swap(value, axis, count, bit):
    return lax.ppermute(value, axis, [(i, i ^ bit) for i in range(count)])


def after(value, *others):
    return lax.optimization_barrier((value,) + others)[0]


NEAR = 4


def far_shift(value, n_chip, by):
    return swap(value, "fsdp", n_chip, by * NEAR)


def far_gather(shard, n_chip):
    return [shard] + [far_shift(shard, n_chip, k) for k in range(1, n_chip // NEAR)]


def pack_kernel(count, *refs):
    ins, outs = refs[:count], refs[count:]
    at = 0
    for out_ref in outs:
        width = out_ref.shape[2]
        for i, in_ref in enumerate(ins):
            out_ref[i] = in_ref[:, at : at + width]
        at += width


def pack(parts, widths):
    rows = parts[0].shape[0]
    return pl.pallas_call(
        lambda *refs: pack_kernel(len(parts), *refs),
        out_shape=[jax.ShapeDtypeStruct((len(parts), rows, w), BF) for w in widths],
        cost_estimate=SMALL,
        name="pack",
    )(*parts)


def lay_kernel(*refs):
    out_ref, at = refs[-1], 0
    rows = out_ref.shape[0]
    for in_ref in refs[:-1]:
        width = in_ref.shape[1]
        for first in range(0, in_ref.shape[0], rows):
            out_ref[:, at : at + width] = in_ref[first : first + rows]
            at += width


def lay(rows, *parts):
    width = sum(part.shape[0] // rows * part.shape[1] for part in parts)
    return pl.pallas_call(
        lay_kernel,
        out_shape=jax.ShapeDtypeStruct((rows, width), BF),
        cost_estimate=SMALL,
        name="lay",
    )(*parts)


def near_rel(length, bits, n_seq):
    rel = [(z, n, 0) for n in (0, bits[0], bits[1], bits[0] ^ bits[1]) for z in range(length)]
    for bit in bits_of(n_seq):
        rel = rel + [(z, n, c ^ bit) for z, n, c in rel]
    return rel


def seq_parts(part, n_seq):
    parts = [part]
    for bit in bits_of(n_seq):
        parts = parts + [swap(p, "seq", n_seq, bit) for p in parts]
    return parts


def interleave(first, second):
    return [part for pair in zip(first, second) for part in pair]


def reorder_kernel(counts, table_ref, *refs):
    ins, out_ref = refs[: len(counts)], refs[len(counts)]
    place = 0
    for part_ref, count in zip(ins, counts):

        def move(i, carry, part_ref=part_ref, place=place):
            out_ref[table_ref[place + i]] = part_ref[i]
            return carry

        lax.fori_loop(0, count, move, 0)
        place += count


def places(parts, rel, seq_pos, chip_pos, n_chip, chunks):
    rows, width = parts[0].shape[1:]
    counts = [part.shape[0] for part in parts]
    total = sum(counts)
    step = width // chunks
    far, near, seq = (jnp.asarray(col, jnp.int32) for col in zip(*rel))
    table = (
        jnp.bitwise_xor(seq_pos, seq) * n_chip
        + jnp.bitwise_xor(chip_pos // NEAR, far) * NEAR
        + jnp.bitwise_xor(chip_pos % NEAR, near)
    )
    return table, counts, total, rows, width, step


def reorder_columns(parts, rel, seq_pos, chip_pos, n_chip, chunks):
    table, counts, total, rows, width, step = places(
        parts, rel, seq_pos, chip_pos, n_chip, chunks
    )
    out = pl.pallas_call(
        lambda *refs: reorder_kernel(counts, *refs),
        grid=(chunks,),
        in_specs=[pl.BlockSpec(memory_space=pltpu.SMEM)]
        + [pl.BlockSpec((count, rows, step), lambda c: (0, 0, c)) for count in counts],
        out_specs=pl.BlockSpec((total, rows, step), lambda c: (0, 0, c)),
        out_shape=jax.ShapeDtypeStruct((total, rows, width), BF),
        cost_estimate=SMALL,
        name="reorder",
    )(table, *parts)
    return out.reshape(total * rows, width)


def reorder_rows(parts, rel, seq_pos, chip_pos, n_chip, chunks):
    table, counts, total, rows, width, step = places(
        parts, rel, seq_pos, chip_pos, n_chip, chunks
    )
    out = pl.pallas_call(
        lambda *refs: reorder_kernel(counts, *refs),
        grid=(chunks,),
        in_specs=[pl.BlockSpec(memory_space=pltpu.SMEM)]
        + [pl.BlockSpec((count, rows, step), lambda c: (0, 0, c)) for count in counts],
        out_specs=pl.BlockSpec((total, None, rows, step), lambda c: (0, c, 0, 0)),
        out_shape=jax.ShapeDtypeStruct((total, chunks, rows, step), BF),
        cost_estimate=SMALL,
        name="reorder_rows",
    )(table, *parts)
    return out.reshape(total * chunks * rows, step)


def split_bit(index, bit):
    return (index // bit) % 2


def fold_kernel(axis, mine_ref, kept_ref, got_ref, give_ref, keep_ref):
    mine = mine_ref[0]

    def block(f, carry):
        for side, out_ref in ((1 - mine, give_ref), (mine, keep_ref)):
            if len(kept_ref.shape) == 4:
                spots = [((f, side), (f,))]
            elif axis == 1:
                spots = [((f, side, j), (f, j)) for j in range(2)]
            else:
                spots = [((f, j, side), (f, j)) for j in range(2)]
            for source, target in spots:
                total = kept_ref[source].astype(F32) + got_ref[source].astype(F32)
                out_ref[target] = total.astype(out_ref.dtype)
        return carry

    lax.fori_loop(0, kept_ref.shape[0], block, 0)


def fold(kept, got, axis, mine):
    shape = kept.shape[:axis] + kept.shape[axis + 1 :]
    vmem = pl.BlockSpec(memory_space=pltpu.VMEM)
    return pl.pallas_call(
        lambda *refs: fold_kernel(axis, *refs),
        in_specs=[pl.BlockSpec(memory_space=pltpu.SMEM), vmem, vmem],
        out_specs=[vmem] * 2,
        out_shape=[jax.ShapeDtypeStruct(shape, kept.dtype)] * 2,
        cost_estimate=SMALL,
        name="fold",
    )(mine.reshape(1).astype(jnp.int32), kept, got)


CHUNK = 384


def gather_rows_kernel(out_ref_width, *refs):
    ins, out_ref = refs[:-1], refs[-1]
    at = 0
    for in_ref in ins:
        for first in range(0, in_ref.shape[1], CHUNK):
            row, col = at // out_ref_width, at % out_ref_width
            out_ref[row : row + 1, col : col + CHUNK] = in_ref[:, first : first + CHUNK]
            at += CHUNK


def gather_rows(vectors, rows):
    width = sum(v.shape[1] for v in vectors) // rows
    return pl.pallas_call(
        lambda *refs: gather_rows_kernel(width, *refs),
        out_shape=jax.ShapeDtypeStruct((rows, width), F32),
        cost_estimate=SMALL,
        name="gather_rows",
    )(*vectors)


class Scatter:
    def __init__(self, keep, recv, near, where):
        self.n_seq, self.n_chip, self.seq_pos, self.chip_pos = where
        rows, width = keep.shape[1:]
        for bit in bits_of(self.n_seq)[:-1][::-1]:
            total = (keep.astype(F32) + recv.astype(F32)).astype(keep.dtype)
            total = total.reshape(2, -1, rows, width)
            mine = split_bit(self.seq_pos, bit)
            give = lax.dynamic_index_in_dim(total, 1 - mine, 0, keepdims=False)
            keep = lax.dynamic_index_in_dim(total, mine, 0, keepdims=False)
            recv = swap(give, "seq", self.n_seq, bit)
        shape = (self.n_chip // NEAR, 2, 2, rows, width)
        self.kept, self.got = keep.reshape(shape), recv.reshape(shape)
        self.near = near
        self.step(near[0], 1 if near[0] == 2 else 2)

    def step(self, bit, axis, *gate):
        got = after(self.got, *gate) if gate else self.got
        mine = split_bit(self.chip_pos, bit)
        self.give, self.kept = fold(self.kept, got, axis, mine)
        self.got = swap(self.give, "fsdp", self.n_chip, bit)

    def second(self, *gate):
        self.step(self.near[1], 1, *gate)
        return self.give

    def pair(self, *gate):
        return self.kept, after(self.got, *gate) if gate else self.got


def unpack_kernel(counts, extra, far_ref, *refs):
    pairs, outs = refs[: 2 * len(counts)], refs[2 * len(counts) + extra :]
    length = len(outs)
    rows = outs[0].shape[0]
    for k, out_ref in enumerate(outs):
        block = jnp.bitwise_xor(far_ref[0], k)
        at = 0
        for i, pieces in enumerate(counts):
            kept_ref, got_ref = pairs[2 * i : 2 * i + 2]
            width = kept_ref.shape[-1]
            for j in range(pieces):
                total = kept_ref[block, j].astype(F32) + got_ref[block, j].astype(F32)
                out_ref[:, at : at + width] = total.astype(BF)
                at += width
        if extra:
            out_ref[:, at:] = refs[2 * len(counts)][...].astype(BF)


def unpack(pairs, own_rows, far_pos, *extra):
    length = pairs[0][0].shape[0]
    counts = [kept.shape[1] // own_rows for kept, _ in pairs]
    parts = [
        part.reshape(length, n, own_rows, part.shape[2])
        for pair, n in zip(pairs, counts)
        for part in pair
    ]
    width = sum(part.shape[1] * part.shape[3] for part in parts[::2])
    width += sum(part.shape[1] for part in extra)
    vmem = pl.BlockSpec(memory_space=pltpu.VMEM)
    return pl.pallas_call(
        lambda *refs: unpack_kernel(counts, len(extra), *refs),
        in_specs=[pl.BlockSpec(memory_space=pltpu.SMEM)] + [vmem] * (len(parts) + len(extra)),
        out_shape=[jax.ShapeDtypeStruct((own_rows, width), BF)] * length,
        cost_estimate=SMALL,
        name="unpack",
    )(far_pos.reshape(1).astype(jnp.int32), *parts, *extra)


def far_sum(blocks, n_chip, *gate):
    got = [far_shift(block, n_chip, k) for k, block in enumerate(blocks[1:], 1)]
    total = blocks[0].astype(F32)
    for block in got:
        total = total + (after(block, *gate) if gate else block).astype(F32)
    return total


def solution(mesh):
    n_seq, n_chip = mesh.shape["seq"], mesh.shape["fsdp"]
    devices = n_seq * n_chip
    near_a, near_b = (2, 1), (1, 2)
    length = n_chip // NEAR
    top_seq = n_seq // 2
    swapped = n_seq == MB

    def local(
        inputs,
        order,
        lengths,
        cotangent,
        weight_qkv,
        bias_qv,
        weight_out,
        bias_out,
        weight_in,
        bias_in,
        weight_back,
        bias_back,
        gain_first,
        shift_first,
        gain_second,
        shift_second,
    ):
        seq_pos, chip_pos = lax.axis_index("seq"), lax.axis_index("fsdp")
        me = seq_pos * n_chip + chip_pos
        rows_here = inputs.shape[2]

        small = [
            bias_qv,
            bias_out,
            bias_in,
            bias_back,
            gain_first,
            shift_first,
            gain_second,
            shift_second,
        ]
        widths = [v.shape[0] for v in small]
        far_pos = chip_pos // NEAR
        own_rows = weight_in.shape[0]

        lanes = -(-max(widths) // 128) * 128
        groups = -(-len(small) // own_rows)
        vec = [jnp.pad(v, (0, lanes - v.shape[0])) for v in small]
        vec = jnp.pad(jnp.stack(vec), ((0, own_rows * groups - len(small)), (0, 0)))
        vec = vec.reshape(own_rows, groups * lanes)
        early = lay(own_rows, weight_qkv, weight_out, vec)
        half = 2 * D
        early_far = far_gather(early, n_chip)
        late = lay(own_rows, weight_in, weight_back)
        late_far = far_gather(after(late, *early_far), n_chip)

        def near(block, bit):
            return swap(block, "fsdp", n_chip, bit)

        def join(block, other):
            return jnp.concatenate([block, other], axis=0)

        a_block, b_block = pack(early_far, [half, half + groups * lanes])
        a_first, b_first = near(a_block, near_a[0]), near(b_block, near_b[0])
        a_whole, b_whole = join(a_block, a_first), join(b_block, b_first)
        a_last, b_last = near(a_whole, near_a[1]), near(b_whole, near_b[1])
        a_parts = interleave(seq_parts(a_whole, n_seq), seq_parts(a_last, n_seq))
        b_parts = interleave(seq_parts(b_whole, n_seq), seq_parts(b_last, n_seq))
        in_block, back_block = pack(
            [after(part, a_last, b_last) for part in late_far], [FF, FF]
        )
        in_first, back_first = near(in_block, near_a[0]), near(back_block, near_b[0])

        a_rel, b_rel = near_rel(length, near_a, n_seq), near_rel(length, near_b, n_seq)
        spot = (seq_pos, chip_pos, n_chip)
        qk_mat = reorder_columns(a_parts, a_rel, *spot, 2)
        vo_mat = reorder_columns(b_parts, b_rel, *spot, 1)
        v_mat, out_mat = vo_mat[:, :D], vo_mat[:, D : 2 * D]

        holders = places(b_parts, b_rel, *spot, 1)[0]
        pick = (jnp.arange(devices, dtype=jnp.int32)[:, None] == holders[None, :]).astype(BF)
        used = -(-len(small) // groups)
        vec_held = jnp.concatenate([part[:, :used, half:] for part in b_parts], axis=0)
        vec_all = dot_plain(pick, vec_held.reshape(devices, -1))
        vectors = [
            vec_all[:, i * lanes : i * lanes + width].reshape(-1) for i, width in enumerate(widths)
        ]
        qv_vec, out_vec, in_vec, back_vec, gain_one, shift_one, gain_two, shift_two = vectors

        def bring(rows):
            if not swapped:
                return rows[:, 0].reshape(MB * rows_here, D)
            mine = lax.dynamic_index_in_dim(rows[:, 0], seq_pos, 0, keepdims=False)
            other = lax.dynamic_index_in_dim(rows[:, 0], 1 - seq_pos, 0, keepdims=False)
            return jnp.concatenate([mine, swap(other, "seq", n_seq, 1)], axis=0)

        def bring_back(rows):
            if not swapped:
                return rows.reshape(MB, 1, rows_here, D)
            mine, other = rows[:rows_here], swap(rows[rows_here:], "seq", n_seq, 1)
            first = seq_pos == 0
            return jnp.stack([jnp.where(first, mine, other), jnp.where(first, other, mine)])[
                :, None
            ]

        ends = jnp.cumsum(lengths[:, 0], axis=1)
        if swapped:
            ids = lax.dynamic_index_in_dim(order[:, 0], seq_pos, 0, keepdims=False)
            ids = jnp.concatenate(
                [
                    lax.dynamic_slice_in_dim(ids, seq_pos * rows_here, rows_here, 0),
                    lax.dynamic_slice_in_dim(ids, (1 - seq_pos) * rows_here, rows_here, 0),
                ]
            )
            qpos = kpos = ids[None]
            ends = lax.dynamic_index_in_dim(ends, seq_pos, 0, keepdims=True)
        else:
            kpos = order[:, 0]
            qpos = lax.dynamic_slice_in_dim(kpos, seq_pos * rows_here, rows_here, 1)
        qstart = jnp.max(
            jnp.where(ends[:, None, :] <= qpos[:, :, None], ends[:, None, :], 0), axis=2
        )
        streams = qpos.shape[0]

        def by_stream(rows):
            return rows.reshape(streams, -1, rows.shape[-1])

        x_float = bring(inputs).astype(F32)
        grad_rows = bring(cotangent)
        grad_float = grad_rows.astype(F32)
        x_hat_one, inv_one = norm_parts(x_float)
        normed = (x_hat_one * gain_one + shift_one).astype(BF)
        q_bias = jnp.concatenate([qv_vec[:D], jnp.zeros((D,), F32)])
        qk = by_stream((dot_plain(normed, qk_mat) + q_bias).astype(BF))
        value_rows = by_stream((dot_plain(normed, v_mat) + qv_vec[D:]).astype(BF))
        pairs = HEADS // 2
        if not swapped:
            q = (qk, 0)
            k = (lax.all_gather(qk[:, :, D:], "seq", axis=1, tiled=True), 0)
            v = (lax.all_gather(value_rows, "seq", axis=1, tiled=True), 0)
        in_whole = join(in_block, after(in_first, vo_mat))
        back_whole = join(back_block, after(back_first, vo_mat))
        if swapped:
            qk, value_rows, _, _, grad_rows = lax.optimization_barrier(
                (qk, value_rows, in_whole, back_whole, grad_rows)
            )
            grad_float = grad_rows.astype(F32)
            q, k, v = (qk, 0), (qk, pairs), (value_rows, 0)
        attn_heads, probs = attend(q, k, v, qpos, qstart, kpos)
        in_last = near(in_whole, near_a[1])
        back_last = near(back_whole, near_b[1])
        in_wholes = seq_parts(in_whole, n_seq)
        back_wholes = seq_parts(back_whole, n_seq)
        attn_heads = attn_heads.reshape(-1, D)
        mid_stream = x_float + dot_plain(attn_heads, out_mat) + out_vec
        x_hat_two, inv_two = norm_parts(mid_stream)
        normed_two = (x_hat_two * gain_two + shift_two).astype(BF)
        in_last, back_last, _ = lax.optimization_barrier((in_last, back_last, normed_two))
        in_parts = interleave(in_wholes, seq_parts(in_last, n_seq))
        back_parts = interleave(back_wholes, seq_parts(back_last, n_seq))
        in_mat = reorder_columns(in_parts, a_rel, *spot, 4)
        in_mat, *back_parts = lax.optimization_barrier((in_mat, *back_parts))
        pre_act = dot_plain(normed_two, in_mat) + in_vec
        hidden_float, gelu_pull = jax.vjp(gelu_tanh, pre_act)
        hidden = hidden_float.astype(BF)

        top_mine = split_bit(seq_pos, top_seq)

        def halves(left, right):
            half = left.shape[1] // 2

            def part(which):
                return dot_first(
                    lax.dynamic_slice_in_dim(left, which * half, half, 1), right
                ).astype(BF)

            return part(1 - top_mine), part(top_mine)

        where = (n_seq, n_chip, seq_pos, chip_pos)

        def scatter(recv, keep, near):
            shape = (devices // 2, keep.shape[0] // (devices // 2), keep.shape[1])
            return Scatter(keep.reshape(shape), recv.reshape(shape), near, where)

        back_give, back_keep = halves(hidden, grad_rows)
        back_recv = swap(back_give, "seq", n_seq, top_seq)
        back_parts = [after(part, back_give) for part in back_parts]
        back_mat = reorder_rows(back_parts, b_rel, *spot, FF // D)
        d_hidden = dot_last(after(grad_rows, back_keep), back_mat)
        d_pre = gelu_pull(d_hidden)[0].astype(BF)
        in_give, in_keep = halves(normed_two, d_pre)
        in_recv = swap(in_give, "seq", n_seq, top_seq)
        back_sum = scatter(after(back_recv, in_give), back_keep, near_b)
        in_sum = scatter(in_recv, in_keep, near_a)
        d_pre = after(d_pre, in_sum.give, back_sum.give)
        d_norm_two = dot_last(d_pre, in_mat)
        d_mid = grad_float + norm_back(d_norm_two, x_hat_two, inv_two, gain_two)
        d_mid_low = d_mid.astype(BF)
        d_heads = by_stream(dot_last(d_mid_low, out_mat).astype(BF))
        d_query, d_keys, d_values = attend_back(q, k, v, d_heads, probs)
        sent = (in_sum.second(d_query), back_sum.second(d_query))
        if not swapped:
            d_keys = lax.psum_scatter(d_keys, "seq", scatter_dimension=1, tiled=True)
            d_values = lax.psum_scatter(d_values, "seq", scatter_dimension=1, tiled=True)
        d_qk = jnp.concatenate([d_query, d_keys], axis=2).reshape(-1, 2 * D)
        d_values = d_values.reshape(-1, D)
        d_qk, d_values, _, _ = lax.optimization_barrier((d_qk, d_values) + sent)
        qk_give, qk_keep = halves(normed, d_qk)
        v_give, v_keep = halves(normed, d_values)
        out_give, out_keep = halves(attn_heads, d_mid_low)
        vo_give = jnp.concatenate([v_give, out_give], axis=1)
        vo_keep = jnp.concatenate([v_keep, out_keep], axis=1)
        qk_recv, vo_recv = (swap(give, "seq", n_seq, top_seq) for give in (qk_give, vo_give))
        qk_sum = scatter(qk_recv, qk_keep, near_a)
        vo_sum = scatter(vo_recv, vo_keep, near_b)
        sent = (qk_sum.give, vo_sum.give)
        late_blocks = unpack([in_sum.pair(*sent), back_sum.pair(*sent)], own_rows, far_pos)
        d_qk, d_values, d_pre, grad_late, d_mid_late, _, _ = lax.optimization_barrier(
            (d_qk, d_values, d_pre, grad_rows, d_mid) + sent
        )
        d_back_vec = jnp.sum(grad_late.astype(F32), axis=0, keepdims=True)
        d_in_vec = jnp.sum(d_pre.astype(F32), axis=0, keepdims=True)
        d_norm_late = after(d_norm_two, *sent)
        d_gain_two = jnp.sum(d_norm_late * x_hat_two, axis=0, keepdims=True)
        d_shift_two = jnp.sum(d_norm_late, axis=0, keepdims=True)
        d_out_vec = jnp.sum(d_mid_late, axis=0, keepdims=True)
        q_sums = jnp.sum(d_qk[:, :D].astype(F32), axis=0, keepdims=True)
        v_sums = jnp.sum(d_values.astype(F32), axis=0, keepdims=True)
        d_norm_half = dot_last(after(d_qk, late_blocks[0]), qk_mat)
        sent = (qk_sum.second(d_norm_half), vo_sum.second(d_norm_half))
        d_norm_one = d_norm_half + dot_last(after(d_values, *sent), v_mat)
        d_inputs = d_mid + norm_back(d_norm_one, x_hat_one, inv_one, gain_one)
        input_grad = d_inputs.astype(BF)
        d_gain_one = jnp.sum(d_norm_one * x_hat_one, axis=0, keepdims=True)
        d_shift_one = jnp.sum(d_norm_one, axis=0, keepdims=True)

        vec_grads = [
            q_sums,
            v_sums,
            d_out_vec,
            d_in_vec,
            d_back_vec,
            d_gain_one,
            d_shift_one,
            d_gain_two,
            d_shift_two,
        ]
        vec_sum = gather_rows(vec_grads, own_rows)
        for bit in bits_of(n_seq):
            vec_sum = vec_sum + swap(vec_sum, "seq", n_seq, bit)
        qk_pair, vo_pair = qk_sum.pair(input_grad), vo_sum.pair(input_grad)
        vec_sum = vec_sum + swap(vec_sum, "fsdp", n_chip, 1)
        got = after(swap(vec_sum, "fsdp", n_chip, 2), qk_pair[1], vo_pair[1])
        early_blocks = unpack([qk_pair, vo_pair], own_rows, far_pos, vec_sum + got)
        hidden, _ = lax.optimization_barrier((hidden, early_blocks[0]))
        block_out = (mid_stream + dot_plain(hidden, back_mat) + back_vec).astype(BF)
        input_grad = bring_back(after(input_grad, early_blocks[0]))
        block_out = bring_back(block_out)
        late_sum = far_sum(late_blocks, n_chip, early_blocks[0])
        early_sum = far_sum(early_blocks, n_chip)
        d_in_mat = late_sum[:, :FF]
        d_back_mat = jnp.concatenate(
            [late_sum[:, i : i + D] for i in range(FF, 2 * FF, D)], axis=0
        )
        d_qkv_mat, d_out_mat = early_sum[:, : 3 * D], early_sum[:, 3 * D : 4 * D]
        vec_sum = early_sum[:, 4 * D :]
        long = vec_sum.shape[1]
        g_out, at = [], 0
        for width in widths:
            spot_at = at + me * width
            got = lax.dynamic_slice(vec_sum, (spot_at // long, spot_at % long), (1, width))
            g_out.append(got[0])
            at += width * devices
        g_qv, g_out_vec, g_in, g_back, g_gain1, g_shift1, g_gain2, g_shift2 = g_out
        return (
            block_out,
            input_grad,
            d_qkv_mat,
            g_qv,
            d_out_mat,
            g_out_vec,
            d_in_mat,
            g_in,
            d_back_mat,
            g_back,
            g_gain1,
            g_shift1,
            g_gain2,
            g_shift2,
        )

    tokens, sharded, vector = P(None, "fsdp", "seq", None), P(("seq", "fsdp"), None), P(("seq", "fsdp"))
    streams_spec = P(None, "fsdp", None)
    return jax.shard_map(
        local,
        mesh=mesh,
        in_specs=(tokens, streams_spec, streams_spec, tokens) + (sharded, vector) * 4 + (vector,) * 4,
        out_specs=(tokens, tokens) + (sharded, vector) * 4 + (vector,) * 4,
        check_vma=False,
    )
```

```python
import jax
import jax.numpy as jnp
from jax import lax
from jax.experimental import pallas as pl
from jax.experimental.pallas import tpu as pltpu
from jax.sharding import PartitionSpec as P

D = 768
HEADS = 12
HD = 64
FF = 3072
MB = 2
PAIR = 2 * HD

eps = 1e-05
score_scale = 0.125
BF = jnp.bfloat16
F32 = jnp.float32
SMALL = pl.CostEstimate(flops=1, transcendentals=0, bytes_accessed=1)


def norm_parts(values):
    row_mean = jnp.mean(values, axis=-1, keepdims=True)
    centred = values - row_mean
    inv_std = lax.rsqrt(jnp.mean(centred * centred, axis=-1, keepdims=True) + eps)
    return (centred * inv_std, inv_std)


def norm_back(grad_norm, x_hat, inv_std, gain):
    scaled = grad_norm * gain
    return inv_std * (
        scaled
        - jnp.mean(scaled, axis=-1, keepdims=True)
        - x_hat * jnp.mean(scaled * x_hat, axis=-1, keepdims=True)
    )


def gelu_tanh(values):
    return (
        0.5
        * values
        * (1.0 + jnp.tanh(0.7978845608028654 * (values + 0.044715 * values * values * values)))
    )


def dot_first(left, right):
    return lax.dot_general(left, right, (((0,), (0,)), ((), ())), preferred_element_type=F32)


def dot_last(left, right):
    return lax.dot_general(left, right, (((1,), (1,)), ((), ())), preferred_element_type=F32)


def dot_plain(left, right):
    return jnp.dot(left, right, preferred_element_type=F32)


def attend_kernel(q_ref, k_ref, v_ref, qpos_ref, qstart_ref, kpos_ref, out_ref, prob_ref, bias_ref):
    @pl.when(pl.program_id(1) == 0)
    def _():
        kpos = kpos_ref[0]
        seen = (kpos <= qpos_ref[0]) & (kpos >= qstart_ref[0])
        bias_ref[...] = jnp.where(seen, 0.0, -1e30)

    q, k, v = q_ref[0], k_ref[0], v_ref[0]
    lane = lax.broadcasted_iota(jnp.int32, q.shape, 1)
    scaled = q * jnp.asarray(score_scale, BF)
    halves = []
    for j in range(2):
        q_head = jnp.where((lane // HD) == j, scaled, jnp.zeros_like(scaled))
        scores = dot_last(k, q_head) + bias_ref[...]
        col_max = jnp.max(scores, axis=0, keepdims=True)
        expo = jnp.exp(scores - col_max)
        probs = (expo * (1.0 / jnp.sum(expo, axis=0, keepdims=True))).astype(BF)
        prob_ref[0, j] = probs
        halves.append(dot_first(v, probs))
    row = lax.broadcasted_iota(jnp.int32, halves[0].shape, 0)
    out_ref[0] = jnp.where(row < HD, halves[0], halves[1]).T.astype(BF)


def attend_back_kernel(q_ref, k_ref, v_ref, dh_ref, prob_ref, dq_ref, dk_ref, dv_ref):
    q, k, v, dh = q_ref[0], k_ref[0], v_ref[0], dh_ref[0]
    lane = lax.broadcasted_iota(jnp.int32, dh.shape, 1)
    dq, dk, dv = [], [], []
    for j in range(2):
        probs = prob_ref[0, j]
        dh_head = jnp.where((lane // HD) == j, dh, jnp.zeros_like(dh))
        d_prob = dot_last(v, dh_head)
        wide = probs.astype(F32)
        moved = wide * d_prob
        centre = jnp.sum(moved, axis=0, keepdims=True)
        d_scores = (moved - wide * centre).astype(BF)
        dq.append(dot_first(k, d_scores))
        dk.append(dot_plain(d_scores, q))
        dv.append(dot_plain(probs, dh))
    row = lax.broadcasted_iota(jnp.int32, dq[0].shape, 0)
    col = lax.broadcasted_iota(jnp.int32, dk[0].shape, 1)
    dq_ref[0] = (score_scale * jnp.where(row < HD, dq[0], dq[1])).T.astype(BF)
    dk_ref[0] = (score_scale * jnp.where(col < HD, dk[0], dk[1])).astype(BF)
    dv_ref[0] = jnp.where(col < HD, dv[0], dv[1]).astype(BF)


def cols(rows, offset):
    return pl.BlockSpec((1, rows, PAIR), lambda s, h: (s, 0, h + offset))


def attend(q, k, v, qpos, qstart, kpos):
    (q_arr, q_off), (k_arr, k_off), (v_arr, v_off) = q, k, v
    streams, rows = q_arr.shape[:2]
    keys = k_arr.shape[1]
    pairs = HEADS // 2
    return pl.pallas_call(
        attend_kernel,
        grid=(streams, pairs),
        in_specs=[
            cols(rows, q_off),
            cols(keys, k_off),
            cols(keys, v_off),
            pl.BlockSpec((1, 1, rows), lambda s, h: (s, 0, 0)),
            pl.BlockSpec((1, 1, rows), lambda s, h: (s, 0, 0)),
            pl.BlockSpec((1, keys, 1), lambda s, h: (s, 0, 0)),
        ],
        out_specs=[
            cols(rows, 0),
            pl.BlockSpec((1, 2, keys, rows), lambda s, h: (s, h, 0, 0)),
        ],
        out_shape=[
            jax.ShapeDtypeStruct((streams, rows, D), BF),
            jax.ShapeDtypeStruct((streams, HEADS, keys, rows), BF),
        ],
        scratch_shapes=[pltpu.VMEM((keys, rows), F32)],
        cost_estimate=SMALL,
        name="attend",
    )(q_arr, k_arr, v_arr, qpos[:, None, :], qstart[:, None, :], kpos[:, :, None])


def attend_back(q, k, v, d_heads, probs):
    (q_arr, q_off), (k_arr, k_off), (v_arr, v_off) = q, k, v
    streams, rows = q_arr.shape[:2]
    keys = k_arr.shape[1]
    pairs = HEADS // 2
    return pl.pallas_call(
        attend_back_kernel,
        grid=(streams, pairs),
        in_specs=[
            cols(rows, q_off),
            cols(keys, k_off),
            cols(keys, v_off),
            cols(rows, 0),
            pl.BlockSpec((1, 2, keys, rows), lambda s, h: (s, h, 0, 0)),
        ],
        out_specs=[cols(rows, 0), cols(keys, 0), cols(keys, 0)],
        out_shape=[
            jax.ShapeDtypeStruct((streams, rows, D), BF),
            jax.ShapeDtypeStruct((streams, keys, D), BF),
            jax.ShapeDtypeStruct((streams, keys, D), BF),
        ],
        cost_estimate=SMALL,
        name="attend_back",
    )(q_arr, k_arr, v_arr, d_heads, probs)


def after(value, *others):
    return lax.optimization_barrier((value,) + others)[0]


def bits_of(count):
    return [1 << b for b in range(count.bit_length() - 1)]


def swap(value, axis, count, bit):
    return lax.ppermute(value, axis, [(i, i ^ bit) for i in range(count)])


def after(value, *others):
    return lax.optimization_barrier((value,) + others)[0]


NEAR = 4


def far_shift(value, n_chip, by):
    return swap(value, "fsdp", n_chip, by * NEAR)


def far_gather(shard, n_chip):
    return [shard] + [far_shift(shard, n_chip, k) for k in range(1, n_chip // NEAR)]


def pack_kernel(count, *refs):
    ins, outs = refs[:count], refs[count:]
    at = 0
    for out_ref in outs:
        width = out_ref.shape[2]
        for i, in_ref in enumerate(ins):
            out_ref[i] = in_ref[:, at : at + width]
        at += width


def pack(parts, widths):
    rows = parts[0].shape[0]
    return pl.pallas_call(
        lambda *refs: pack_kernel(len(parts), *refs),
        out_shape=[jax.ShapeDtypeStruct((len(parts), rows, w), BF) for w in widths],
        cost_estimate=SMALL,
        name="pack",
    )(*parts)


def lay_kernel(*refs):
    out_ref, at = refs[-1], 0
    rows = out_ref.shape[0]
    for in_ref in refs[:-1]:
        width = in_ref.shape[1]
        for first in range(0, in_ref.shape[0], rows):
            out_ref[:, at : at + width] = in_ref[first : first + rows]
            at += width


def lay(rows, *parts):
    width = sum(part.shape[0] // rows * part.shape[1] for part in parts)
    return pl.pallas_call(
        lay_kernel,
        out_shape=jax.ShapeDtypeStruct((rows, width), BF),
        cost_estimate=SMALL,
        name="lay",
    )(*parts)


def lay_small_kernel(groups, lanes, count, *refs):
    mats, small, out_ref = refs[:count], refs[count:-1], refs[-1]
    rows, at = out_ref.shape[0], 0
    for in_ref in mats:
        out_ref[:, at : at + in_ref.shape[1]] = in_ref[...]
        at += in_ref.shape[1]
    out_ref[:, at:] = jnp.zeros((rows, groups * lanes), BF)
    for i, in_ref in enumerate(small):
        width = in_ref.shape[1]
        first = at + i % groups * lanes
        row = lax.broadcasted_iota(jnp.int32, (rows, width), 0)
        held = out_ref[:, first : first + width].astype(F32)
        value = jnp.broadcast_to(in_ref[...].astype(F32), (rows, width))
        out_ref[:, first : first + width] = jnp.where(row == i // groups, value, held).astype(BF)


def lay_small(rows, mats, small, groups, lanes):
    width = sum(mat.shape[1] for mat in mats) + groups * lanes
    return pl.pallas_call(
        lambda *refs: lay_small_kernel(groups, lanes, len(mats), *refs),
        out_shape=jax.ShapeDtypeStruct((rows, width), BF),
        cost_estimate=SMALL,
        name="lay_small",
    )(*mats, *[v[None] for v in small])


def near_rel(length, bits, n_seq):
    rel = [(z, n, 0) for n in (0, bits[0], bits[1], bits[0] ^ bits[1]) for z in range(length)]
    for bit in bits_of(n_seq):
        rel = rel + [(z, n, c ^ bit) for z, n, c in rel]
    return rel


def seq_parts(part, n_seq):
    parts = [part]
    for bit in bits_of(n_seq):
        parts = parts + [swap(p, "seq", n_seq, bit) for p in parts]
    return parts


def interleave(first, second):
    return [part for pair in zip(first, second) for part in pair]


def reorder_kernel(counts, table_ref, *refs):
    ins, out_ref = refs[: len(counts)], refs[len(counts)]
    place = 0
    for part_ref, count in zip(ins, counts):

        def move(i, carry, part_ref=part_ref, place=place):
            out_ref[table_ref[place + i]] = part_ref[i]
            return carry

        lax.fori_loop(0, count, move, 0)
        place += count


def places(parts, rel, seq_pos, chip_pos, n_chip, chunks):
    rows, width = parts[0].shape[1:]
    counts = [part.shape[0] for part in parts]
    total = sum(counts)
    step = width // chunks
    far, near, seq = (jnp.asarray(col, jnp.int32) for col in zip(*rel))
    table = (
        jnp.bitwise_xor(seq_pos, seq) * n_chip
        + jnp.bitwise_xor(chip_pos // NEAR, far) * NEAR
        + jnp.bitwise_xor(chip_pos % NEAR, near)
    )
    return table, counts, total, rows, width, step


def reorder_columns(parts, rel, seq_pos, chip_pos, n_chip, chunks):
    table, counts, total, rows, width, step = places(
        parts, rel, seq_pos, chip_pos, n_chip, chunks
    )
    out = pl.pallas_call(
        lambda *refs: reorder_kernel(counts, *refs),
        grid=(chunks,),
        in_specs=[pl.BlockSpec(memory_space=pltpu.SMEM)]
        + [pl.BlockSpec((count, rows, step), lambda c: (0, 0, c)) for count in counts],
        out_specs=pl.BlockSpec((total, rows, step), lambda c: (0, 0, c)),
        out_shape=jax.ShapeDtypeStruct((total, rows, width), BF),
        cost_estimate=SMALL,
        name="reorder",
    )(table, *parts)
    return out.reshape(total * rows, width)


def reorder_rows(parts, rel, seq_pos, chip_pos, n_chip, chunks):
    table, counts, total, rows, width, step = places(
        parts, rel, seq_pos, chip_pos, n_chip, chunks
    )
    out = pl.pallas_call(
        lambda *refs: reorder_kernel(counts, *refs),
        grid=(chunks,),
        in_specs=[pl.BlockSpec(memory_space=pltpu.SMEM)]
        + [pl.BlockSpec((count, rows, step), lambda c: (0, 0, c)) for count in counts],
        out_specs=pl.BlockSpec((total, None, rows, step), lambda c: (0, c, 0, 0)),
        out_shape=jax.ShapeDtypeStruct((total, chunks, rows, step), BF),
        cost_estimate=SMALL,
        name="reorder_rows",
    )(table, *parts)
    return out.reshape(total * chunks * rows, step)


def split_bit(index, bit):
    return (index // bit) % 2


def fold_kernel(axes, mine_ref, *refs):
    count = len(axes)
    ins, outs = refs[: 2 * count], refs[2 * count :]
    for i, axis in enumerate(axes):
        (kept_ref, got_ref), (give_ref, keep_ref) = ins[2 * i : 2 * i + 2], outs[2 * i : 2 * i + 2]
        mine = mine_ref[i]

        def block(f, carry, kept_ref=kept_ref, got_ref=got_ref, mine=mine, axis=axis, to=(give_ref, keep_ref)):
            for side, out_ref in zip((1 - mine, mine), to):
                if len(kept_ref.shape) == 4:
                    spots = [((f, side), (f,))]
                elif axis == 1:
                    spots = [((f, side, j), (f, j)) for j in range(2)]
                else:
                    spots = [((f, j, side), (f, j)) for j in range(2)]
                for source, target in spots:
                    out_ref[target] = kept_ref[source] + got_ref[source]
            return carry

        lax.fori_loop(0, kept_ref.shape[0], block, 0)


def fold(pairs, axes, mines):
    vmem = pl.BlockSpec(memory_space=pltpu.VMEM)
    shapes = [
        kept.shape[:axis] + kept.shape[axis + 1 :] for (kept, _), axis in zip(pairs, axes)
    ]
    outs = pl.pallas_call(
        lambda *refs: fold_kernel(axes, *refs),
        in_specs=[pl.BlockSpec(memory_space=pltpu.SMEM)] + [vmem] * (2 * len(pairs)),
        out_specs=[vmem] * (2 * len(pairs)),
        out_shape=[jax.ShapeDtypeStruct(shape, BF) for shape in shapes for _ in range(2)],
        cost_estimate=SMALL,
        name="fold",
    )(jnp.stack(mines).astype(jnp.int32), *[part for pair in pairs for part in pair])
    return list(zip(outs[::2], outs[1::2]))


CHUNK = 384


def gather_rows_kernel(out_ref_width, *refs):
    ins, out_ref = refs[:-1], refs[-1]
    at = 0
    for in_ref in ins:
        for first in range(0, in_ref.shape[1], CHUNK):
            row, col = at // out_ref_width, at % out_ref_width
            out_ref[row : row + 1, col : col + CHUNK] = in_ref[:, first : first + CHUNK]
            at += CHUNK


def gather_rows(vectors, rows):
    width = sum(v.shape[1] for v in vectors) // rows
    return pl.pallas_call(
        lambda *refs: gather_rows_kernel(width, *refs),
        out_shape=jax.ShapeDtypeStruct((rows, width), F32),
        cost_estimate=SMALL,
        name="gather_rows",
    )(*vectors)


class Scatter:
    def __init__(self, sums, where):
        self.n_seq, self.n_chip, self.seq_pos, self.chip_pos = where
        self.pairs, self.near = [], []
        for keep, recv, near in sums:
            rows, width = keep.shape[1:]
            for bit in bits_of(self.n_seq)[:-1][::-1]:
                total = (keep + recv).reshape(2, -1, rows, width)
                mine = split_bit(self.seq_pos, bit)
                give = lax.dynamic_index_in_dim(total, 1 - mine, 0, keepdims=False)
                keep = lax.dynamic_index_in_dim(total, mine, 0, keepdims=False)
                recv = swap(give, "seq", self.n_seq, bit)
            shape = (self.n_chip // NEAR, 2, 2, rows, width)
            self.pairs.append((keep.reshape(shape), recv.reshape(shape)))
            self.near.append(near)
        self.step([near[0] for near in self.near], [1 if near[0] == 2 else 2 for near in self.near])

    def step(self, bits, axes):
        mines = [split_bit(self.chip_pos, bit) for bit in bits]
        parts = fold(self.pairs, axes, mines)
        self.gives = tuple(give for give, _ in parts)
        self.pairs = [
            (kept, swap(give, "fsdp", self.n_chip, bit)) for (give, kept), bit in zip(parts, bits)
        ]

    def second(self, *gate):
        self.pairs = self.gated(*gate)
        self.step([near[1] for near in self.near], [1] * len(self.near))
        return self.gives

    def gated(self, *gate):
        return [(kept, after(got, *gate)) for kept, got in self.pairs]


def unpack_kernel(counts, extra, far_ref, *refs):
    pairs, outs = refs[: 2 * len(counts)], refs[2 * len(counts) + extra :]
    length = len(outs)
    rows = outs[0].shape[0]
    for k, out_ref in enumerate(outs):
        block = jnp.bitwise_xor(far_ref[0], k)
        at = 0
        for i, pieces in enumerate(counts):
            kept_ref, got_ref = pairs[2 * i : 2 * i + 2]
            width = kept_ref.shape[-1]
            for j in range(pieces):
                out_ref[:, at : at + width] = kept_ref[block, j] + got_ref[block, j]
                at += width
        if extra:
            out_ref[:, at:] = refs[2 * len(counts)][...].astype(BF)


def unpack(pairs, own_rows, far_pos, *extra):
    length = pairs[0][0].shape[0]
    counts = [kept.shape[1] // own_rows for kept, _ in pairs]
    parts = [
        part.reshape(length, n, own_rows, part.shape[2])
        for pair, n in zip(pairs, counts)
        for part in pair
    ]
    width = sum(part.shape[1] * part.shape[3] for part in parts[::2])
    width += sum(part.shape[1] for part in extra)
    vmem = pl.BlockSpec(memory_space=pltpu.VMEM)
    return pl.pallas_call(
        lambda *refs: unpack_kernel(counts, len(extra), *refs),
        in_specs=[pl.BlockSpec(memory_space=pltpu.SMEM)] + [vmem] * (len(parts) + len(extra)),
        out_shape=[jax.ShapeDtypeStruct((own_rows, width), BF)] * length,
        cost_estimate=SMALL,
        name="unpack",
    )(far_pos.reshape(1).astype(jnp.int32), *parts, *extra)


def far_sum(blocks, n_chip, *gate):
    got = [far_shift(block, n_chip, k) for k, block in enumerate(blocks[1:], 1)]
    total = blocks[0].astype(F32)
    for block in got:
        total = total + (after(block, *gate) if gate else block).astype(F32)
    return total


def solution(mesh):
    n_seq, n_chip = mesh.shape["seq"], mesh.shape["fsdp"]
    devices = n_seq * n_chip
    near_a, near_b = (2, 1), (1, 2)
    length = n_chip // NEAR
    top_seq = n_seq // 2
    swapped = n_seq == MB

    def local(
        inputs,
        order,
        lengths,
        cotangent,
        weight_qkv,
        bias_qv,
        weight_out,
        bias_out,
        weight_in,
        bias_in,
        weight_back,
        bias_back,
        gain_first,
        shift_first,
        gain_second,
        shift_second,
    ):
        seq_pos, chip_pos = lax.axis_index("seq"), lax.axis_index("fsdp")
        me = seq_pos * n_chip + chip_pos
        rows_here = inputs.shape[2]

        small = [
            bias_qv,
            bias_out,
            bias_in,
            bias_back,
            gain_first,
            shift_first,
            gain_second,
            shift_second,
        ]
        widths = [v.shape[0] for v in small]
        far_pos = chip_pos // NEAR
        own_rows = weight_in.shape[0]

        lanes = -(-max(widths) // 128) * 128
        groups = -(-len(small) // own_rows)
        early = lay_small(own_rows, [weight_qkv, weight_out], small, groups, lanes)
        half = 2 * D
        early_far = far_gather(early, n_chip)
        late = lay(own_rows, weight_in, weight_back)
        late_far = far_gather(after(late, *early_far), n_chip)

        def near(block, bit):
            return swap(block, "fsdp", n_chip, bit)

        def join(block, other):
            return jnp.concatenate([block, other], axis=0)

        a_block, b_block = pack(early_far, [half, half + groups * lanes])
        a_first, b_first = near(a_block, near_a[0]), near(b_block, near_b[0])
        a_whole, b_whole = join(a_block, a_first), join(b_block, b_first)
        a_last, b_last = near(a_whole, near_a[1]), near(b_whole, near_b[1])
        a_parts = interleave(seq_parts(a_whole, n_seq), seq_parts(a_last, n_seq))
        b_parts = interleave(seq_parts(b_whole, n_seq), seq_parts(b_last, n_seq))
        gated = lax.optimization_barrier(tuple(late_far) + (a_last, b_last))[: len(late_far)]
        in_block, back_block = pack(gated, [FF, FF])
        in_first, back_first = near(in_block, near_a[0]), near(back_block, near_b[0])

        a_rel, b_rel = near_rel(length, near_a, n_seq), near_rel(length, near_b, n_seq)
        spot = (seq_pos, chip_pos, n_chip)
        qk_mat = reorder_columns(a_parts, a_rel, *spot, 2)
        vo_mat = reorder_columns(b_parts, b_rel, *spot, 1)
        v_mat, out_mat = vo_mat[:, :D], vo_mat[:, D : 2 * D]

        holders = places(b_parts, b_rel, *spot, 1)[0]
        pick = (jnp.arange(devices, dtype=jnp.int32)[:, None] == holders[None, :]).astype(BF)
        used = -(-len(small) // groups)
        vec_held = jnp.concatenate([part[:, :used, half:] for part in b_parts], axis=0)
        vec_all = dot_plain(pick, vec_held.reshape(devices, -1))
        in_whole = join(in_block, after(in_first, vo_mat))
        back_whole = join(back_block, after(back_first, vo_mat))
        vec_all = after(vec_all, in_whole, back_whole)
        vectors = [
            vec_all[:, i * lanes : i * lanes + width].reshape(-1) for i, width in enumerate(widths)
        ]
        qv_vec, out_vec, in_vec, back_vec, gain_one, shift_one, gain_two, shift_two = vectors

        def bring(rows):
            if not swapped:
                return rows[:, 0].reshape(MB * rows_here, D)
            mine = lax.dynamic_index_in_dim(rows[:, 0], seq_pos, 0, keepdims=False)
            other = lax.dynamic_index_in_dim(rows[:, 0], 1 - seq_pos, 0, keepdims=False)
            return jnp.concatenate([mine, swap(other, "seq", n_seq, 1)], axis=0)

        def bring_back(rows):
            if not swapped:
                return rows.reshape(MB, 1, rows_here, D)
            mine, other = rows[:rows_here], swap(rows[rows_here:], "seq", n_seq, 1)
            first = seq_pos == 0
            return jnp.stack([jnp.where(first, mine, other), jnp.where(first, other, mine)])[
                :, None
            ]

        ends = jnp.cumsum(lengths[:, 0], axis=1)
        if swapped:
            ids = lax.dynamic_index_in_dim(order[:, 0], seq_pos, 0, keepdims=False)
            ids = jnp.concatenate(
                [
                    lax.dynamic_slice_in_dim(ids, seq_pos * rows_here, rows_here, 0),
                    lax.dynamic_slice_in_dim(ids, (1 - seq_pos) * rows_here, rows_here, 0),
                ]
            )
            qpos = kpos = ids[None]
            ends = lax.dynamic_index_in_dim(ends, seq_pos, 0, keepdims=True)
        else:
            kpos = order[:, 0]
            qpos = lax.dynamic_slice_in_dim(kpos, seq_pos * rows_here, rows_here, 1)
        qstart = jnp.max(
            jnp.where(ends[:, None, :] <= qpos[:, :, None], ends[:, None, :], 0), axis=2
        )
        streams = qpos.shape[0]

        def by_stream(rows):
            return rows.reshape(streams, -1, rows.shape[-1])

        x_float = bring(inputs).astype(F32)
        grad_rows = bring(cotangent)
        grad_float = grad_rows.astype(F32)
        x_hat_one, inv_one = norm_parts(x_float)
        normed = (x_hat_one * gain_one + shift_one).astype(BF)
        q_bias = jnp.concatenate([qv_vec[:D], jnp.zeros((D,), F32)])
        qk = by_stream((dot_plain(normed, qk_mat) + q_bias).astype(BF))
        value_rows = by_stream((dot_plain(normed, v_mat) + qv_vec[D:]).astype(BF))
        pairs = HEADS // 2
        if not swapped:
            q = (qk, 0)
            k = (lax.all_gather(qk[:, :, D:], "seq", axis=1, tiled=True), 0)
            v = (lax.all_gather(value_rows, "seq", axis=1, tiled=True), 0)
        if swapped:
            qk, value_rows, _, _, grad_rows = lax.optimization_barrier(
                (qk, value_rows, in_whole, back_whole, grad_rows)
            )
            grad_float = grad_rows.astype(F32)
            q, k, v = (qk, 0), (qk, pairs), (value_rows, 0)
        attn_heads, probs = attend(q, k, v, qpos, qstart, kpos)
        in_last = near(in_whole, near_a[1])
        back_last = near(back_whole, near_b[1])
        in_wholes = seq_parts(in_whole, n_seq)
        back_wholes = seq_parts(back_whole, n_seq)
        attn_heads = attn_heads.reshape(-1, D)
        mid_stream = x_float + dot_plain(attn_heads, out_mat) + out_vec
        x_hat_two, inv_two = norm_parts(mid_stream)
        normed_two = (x_hat_two * gain_two + shift_two).astype(BF)
        in_last, back_last, _ = lax.optimization_barrier((in_last, back_last, normed_two))
        in_parts = interleave(in_wholes, seq_parts(in_last, n_seq))
        back_parts = interleave(back_wholes, seq_parts(back_last, n_seq))
        in_mat = reorder_columns(in_parts, a_rel, *spot, 4)
        d_back_vec = jnp.sum(grad_rows.astype(F32), axis=0, keepdims=True)
        in_mat, d_back_vec, *back_parts = lax.optimization_barrier((in_mat, d_back_vec, *back_parts))
        pre_act = dot_plain(normed_two, in_mat) + in_vec
        hidden_float, gelu_pull = jax.vjp(gelu_tanh, pre_act)
        hidden = hidden_float.astype(BF)

        top_mine = split_bit(seq_pos, top_seq)

        def halves(left, right):
            half = left.shape[1] // 2

            def part(which):
                return dot_first(
                    lax.dynamic_slice_in_dim(left, which * half, half, 1), right
                ).astype(BF)

            return part(1 - top_mine), part(top_mine)

        where = (n_seq, n_chip, seq_pos, chip_pos)

        def scatter(*sums):
            shaped = []
            for recv, keep, near in sums:
                shape = (devices // 2, keep.shape[0] // (devices // 2), keep.shape[1])
                shaped.append((keep.reshape(shape), recv.reshape(shape), near))
            return Scatter(shaped, where)

        back_give, back_keep = halves(hidden, grad_rows)
        back_recv = swap(back_give, "seq", n_seq, top_seq)
        back_parts = [after(part, back_give) for part in back_parts]
        back_mat = reorder_rows(back_parts, b_rel, *spot, FF // D)
        d_hidden = dot_last(after(grad_rows, back_keep, back_recv), back_mat)
        d_pre = gelu_pull(d_hidden)[0].astype(BF)
        in_give, in_keep = halves(normed_two, d_pre)
        in_recv = swap(in_give, "seq", n_seq, top_seq)
        late_sum = scatter((in_recv, in_keep, near_a), (back_recv, back_keep, near_b))
        d_pre = after(d_pre, *late_sum.gives)
        d_norm_two = dot_last(d_pre, in_mat)
        d_mid = grad_float + norm_back(d_norm_two, x_hat_two, inv_two, gain_two)
        d_mid_low = d_mid.astype(BF)
        d_heads = by_stream(dot_last(d_mid_low, out_mat).astype(BF))
        d_query, d_keys, d_values = attend_back(q, k, v, d_heads, probs)
        sent = late_sum.second(d_query)
        if not swapped:
            d_keys = lax.psum_scatter(d_keys, "seq", scatter_dimension=1, tiled=True)
            d_values = lax.psum_scatter(d_values, "seq", scatter_dimension=1, tiled=True)
        d_qk = jnp.concatenate([d_query, d_keys], axis=2).reshape(-1, 2 * D)
        d_values = d_values.reshape(-1, D)
        d_qk, d_values, _, _ = lax.optimization_barrier((d_qk, d_values) + sent)
        qk_give, qk_keep = halves(normed, d_qk)
        v_give, v_keep = halves(normed, d_values)
        out_give, out_keep = halves(attn_heads, d_mid_low)
        vo_give = jnp.concatenate([v_give, out_give], axis=1)
        vo_keep = jnp.concatenate([v_keep, out_keep], axis=1)
        qk_recv, vo_recv = (swap(give, "seq", n_seq, top_seq) for give in (qk_give, vo_give))
        early_sum = scatter((qk_recv, qk_keep, near_a), (vo_recv, vo_keep, near_b))
        sent = early_sum.gives
        late_blocks = unpack(late_sum.gated(*sent), own_rows, far_pos)
        d_qk, d_values, d_pre, d_mid_late, _, _ = lax.optimization_barrier(
            (d_qk, d_values, d_pre, d_mid) + sent
        )
        d_in_vec = jnp.sum(d_pre.astype(F32), axis=0, keepdims=True)
        d_norm_late = after(d_norm_two, *sent)
        d_gain_two = jnp.sum(d_norm_late * x_hat_two, axis=0, keepdims=True)
        d_shift_two = jnp.sum(d_norm_late, axis=0, keepdims=True)
        d_out_vec = jnp.sum(d_mid_late, axis=0, keepdims=True)
        q_sums = jnp.sum(d_qk[:, :D].astype(F32), axis=0, keepdims=True)
        v_sums = jnp.sum(d_values.astype(F32), axis=0, keepdims=True)
        d_norm_half = dot_last(after(d_qk, late_blocks[0]), qk_mat)
        sent = early_sum.second(d_norm_half)
        d_norm_one = d_norm_half + dot_last(after(d_values, *sent), v_mat)
        pairs_left = early_sum.gated(d_norm_one)
        d_norm_one = after(d_norm_one, *[got for _, got in pairs_left])
        d_inputs = d_mid + norm_back(d_norm_one, x_hat_one, inv_one, gain_one)
        input_grad = d_inputs.astype(BF)
        d_gain_one = jnp.sum(d_norm_one * x_hat_one, axis=0, keepdims=True)
        d_shift_one = jnp.sum(d_norm_one, axis=0, keepdims=True)

        vec_grads = [
            q_sums,
            v_sums,
            d_out_vec,
            d_in_vec,
            d_back_vec,
            d_gain_one,
            d_shift_one,
            d_gain_two,
            d_shift_two,
        ]
        vec_sum = gather_rows(vec_grads, own_rows)
        for bit in bits_of(n_seq):
            vec_sum = vec_sum + swap(vec_sum, "seq", n_seq, bit)
        vec_sum = vec_sum + swap(vec_sum, "fsdp", n_chip, 1)
        vec_sum = vec_sum + swap(vec_sum, "fsdp", n_chip, 2)
        early_blocks = unpack(pairs_left, own_rows, far_pos, vec_sum)
        hidden, _ = lax.optimization_barrier((hidden, early_blocks[0]))
        block_out = (mid_stream + dot_plain(hidden, back_mat) + back_vec).astype(BF)
        input_grad = bring_back(after(input_grad, early_blocks[0]))
        block_out = bring_back(block_out)
        late_sum = far_sum(late_blocks, n_chip, early_blocks[0])
        early_sum = far_sum(early_blocks, n_chip)
        d_in_mat = late_sum[:, :FF]
        d_back_mat = jnp.concatenate(
            [late_sum[:, i : i + D] for i in range(FF, 2 * FF, D)], axis=0
        )
        d_qkv_mat, d_out_mat = early_sum[:, : 3 * D], early_sum[:, 3 * D : 4 * D]
        vec_sum = early_sum[:, 4 * D :]
        long = vec_sum.shape[1]
        g_out, at = [], 0
        for width in widths:
            spot_at = at + me * width
            got = lax.dynamic_slice(vec_sum, (spot_at // long, spot_at % long), (1, width))
            g_out.append(got[0])
            at += width * devices
        g_qv, g_out_vec, g_in, g_back, g_gain1, g_shift1, g_gain2, g_shift2 = g_out
        return (
            block_out,
            input_grad,
            d_qkv_mat,
            g_qv,
            d_out_mat,
            g_out_vec,
            d_in_mat,
            g_in,
            d_back_mat,
            g_back,
            g_gain1,
            g_shift1,
            g_gain2,
            g_shift2,
        )

    tokens, sharded, vector = P(None, "fsdp", "seq", None), P(("seq", "fsdp"), None), P(("seq", "fsdp"))
    streams_spec = P(None, "fsdp", None)
    return jax.shard_map(
        local,
        mesh=mesh,
        in_specs=(tokens, streams_spec, streams_spec, tokens) + (sharded, vector) * 4 + (vector,) * 4,
        out_specs=(tokens, tokens) + (sharded, vector) * 4 + (vector,) * 4,
        check_vma=False,
    )
```

```python
import jax
import jax.numpy as jnp
from jax import lax
from jax.experimental import pallas as pl
from jax.experimental.pallas import tpu as pltpu
from jax.sharding import PartitionSpec as P

D = 768
HEADS = 12
HD = 64
FF = 3072
MB = 2
PAIR = 2 * HD

eps = 1e-05
score_scale = 0.125
BF = jnp.bfloat16
F32 = jnp.float32
SMALL = pl.CostEstimate(flops=1, transcendentals=0, bytes_accessed=1)


def norm_parts(values):
    row_mean = jnp.mean(values, axis=-1, keepdims=True)
    centred = values - row_mean
    inv_std = lax.rsqrt(jnp.mean(centred * centred, axis=-1, keepdims=True) + eps)
    return (centred * inv_std, inv_std)


def norm_back(grad_norm, x_hat, inv_std, gain):
    scaled = grad_norm * gain
    return inv_std * (
        scaled
        - jnp.mean(scaled, axis=-1, keepdims=True)
        - x_hat * jnp.mean(scaled * x_hat, axis=-1, keepdims=True)
    )


def gelu_tanh(values):
    return (
        0.5
        * values
        * (1.0 + jnp.tanh(0.7978845608028654 * (values + 0.044715 * values * values * values)))
    )


def dot_first(left, right):
    return lax.dot_general(left, right, (((0,), (0,)), ((), ())), preferred_element_type=F32)


def dot_last(left, right):
    return lax.dot_general(left, right, (((1,), (1,)), ((), ())), preferred_element_type=F32)


def dot_plain(left, right):
    return jnp.dot(left, right, preferred_element_type=F32)


def attend_kernel(q_ref, k_ref, v_ref, qpos_ref, qstart_ref, kpos_ref, out_ref, prob_ref, bias_ref):
    @pl.when(pl.program_id(1) == 0)
    def _():
        kpos = kpos_ref[0]
        seen = (kpos <= qpos_ref[0]) & (kpos >= qstart_ref[0])
        bias_ref[...] = jnp.where(seen, 0.0, -1e30)

    q, k, v = q_ref[0], k_ref[0], v_ref[0]
    lane = lax.broadcasted_iota(jnp.int32, q.shape, 1)
    scaled = q * jnp.asarray(score_scale, BF)
    halves = []
    for j in range(2):
        q_head = jnp.where((lane // HD) == j, scaled, jnp.zeros_like(scaled))
        scores = dot_last(k, q_head) + bias_ref[...]
        col_max = jnp.max(scores, axis=0, keepdims=True)
        expo = jnp.exp(scores - col_max)
        probs = (expo * (1.0 / jnp.sum(expo, axis=0, keepdims=True))).astype(BF)
        prob_ref[0, j] = probs
        halves.append(dot_first(v, probs))
    row = lax.broadcasted_iota(jnp.int32, halves[0].shape, 0)
    out_ref[0] = jnp.where(row < HD, halves[0], halves[1]).T.astype(BF)


def attend_back_kernel(q_ref, k_ref, v_ref, dh_ref, prob_ref, *out_refs):
    dqk_refs, dv_ref = out_refs[:-1], out_refs[-1]
    q, k, v, dh = q_ref[0], k_ref[0], v_ref[0], dh_ref[0]
    lane = lax.broadcasted_iota(jnp.int32, dh.shape, 1)
    dq, dk, dv = [], [], []
    for j in range(2):
        probs = prob_ref[0, j]
        dh_head = jnp.where((lane // HD) == j, dh, jnp.zeros_like(dh))
        d_prob = dot_last(v, dh_head)
        wide = probs.astype(F32)
        moved = wide * d_prob
        centre = jnp.sum(moved, axis=0, keepdims=True)
        d_scores = (moved - wide * centre).astype(BF)
        dq.append(dot_first(k, d_scores))
        dk.append(dot_plain(d_scores, q))
        dv.append(dot_plain(probs, dh))
    row = lax.broadcasted_iota(jnp.int32, dq[0].shape, 0)
    col = lax.broadcasted_iota(jnp.int32, dk[0].shape, 1)
    dq_out = (score_scale * jnp.where(row < HD, dq[0], dq[1])).T.astype(BF)
    dk_out = (score_scale * jnp.where(col < HD, dk[0], dk[1])).astype(BF)
    if len(dqk_refs) == 1:
        at = pl.program_id(1) * PAIR
        dqk_refs[0][0, :, pl.ds(pl.multiple_of(at, PAIR), PAIR)] = dq_out
        dqk_refs[0][0, :, pl.ds(pl.multiple_of(D + at, PAIR), PAIR)] = dk_out
    else:
        dqk_refs[0][0], dqk_refs[1][0] = dq_out, dk_out
    dv_ref[0] = jnp.where(col < HD, dv[0], dv[1]).astype(BF)


def cols(rows, offset):
    return pl.BlockSpec((1, rows, PAIR), lambda s, h: (s, 0, h + offset))


def attend(q, k, v, qpos, qstart, kpos):
    (q_arr, q_off), (k_arr, k_off), (v_arr, v_off) = q, k, v
    streams, rows = q_arr.shape[:2]
    keys = k_arr.shape[1]
    pairs = HEADS // 2
    return pl.pallas_call(
        attend_kernel,
        grid=(streams, pairs),
        in_specs=[
            cols(rows, q_off),
            cols(keys, k_off),
            cols(keys, v_off),
            pl.BlockSpec((1, 1, rows), lambda s, h: (s, 0, 0)),
            pl.BlockSpec((1, 1, rows), lambda s, h: (s, 0, 0)),
            pl.BlockSpec((1, keys, 1), lambda s, h: (s, 0, 0)),
        ],
        out_specs=[
            cols(rows, 0),
            pl.BlockSpec((1, 2, keys, rows), lambda s, h: (s, h, 0, 0)),
        ],
        out_shape=[
            jax.ShapeDtypeStruct((streams, rows, D), BF),
            jax.ShapeDtypeStruct((streams, HEADS, keys, rows), BF),
        ],
        scratch_shapes=[pltpu.VMEM((keys, rows), F32)],
        cost_estimate=SMALL,
        name="attend",
    )(q_arr, k_arr, v_arr, qpos[:, None, :], qstart[:, None, :], kpos[:, :, None])


def attend_back(q, k, v, d_heads, probs):
    (q_arr, q_off), (k_arr, k_off), (v_arr, v_off) = q, k, v
    streams, rows = q_arr.shape[:2]
    keys = k_arr.shape[1]
    pairs = HEADS // 2
    if rows == keys:
        specs = [pl.BlockSpec((1, rows, 2 * D), lambda s, h: (s, 0, 0))]
        shapes = [(rows, 2 * D)]
    else:
        specs, shapes = [cols(rows, 0), cols(keys, 0)], [(rows, D), (keys, D)]
    return pl.pallas_call(
        attend_back_kernel,
        grid=(streams, pairs),
        in_specs=[
            cols(rows, q_off),
            cols(keys, k_off),
            cols(keys, v_off),
            cols(rows, 0),
            pl.BlockSpec((1, 2, keys, rows), lambda s, h: (s, h, 0, 0)),
        ],
        out_specs=specs + [cols(keys, 0)],
        out_shape=[jax.ShapeDtypeStruct((streams,) + shape, BF) for shape in shapes + [(keys, D)]],
        cost_estimate=SMALL,
        name="attend_back",
    )(q_arr, k_arr, v_arr, d_heads, probs)


def after(value, *others):
    return lax.optimization_barrier((value,) + others)[0]


def bits_of(count):
    return [1 << b for b in range(count.bit_length() - 1)]


def swap(value, axis, count, bit):
    return lax.ppermute(value, axis, [(i, i ^ bit) for i in range(count)])


def after(value, *others):
    return lax.optimization_barrier((value,) + others)[0]


NEAR = 4


def far_shift(value, n_chip, by):
    return swap(value, "fsdp", n_chip, by * NEAR)


def far_gather(shard, n_chip):
    return [shard] + [far_shift(shard, n_chip, k) for k in range(1, n_chip // NEAR)]


def pack_kernel(count, *refs):
    ins, outs = refs[:count], refs[count:]
    at = 0
    for out_ref in outs:
        width = out_ref.shape[2]
        for i, in_ref in enumerate(ins):
            out_ref[i] = in_ref[:, at : at + width]
        at += width


def pack(parts, widths):
    rows = parts[0].shape[0]
    return pl.pallas_call(
        lambda *refs: pack_kernel(len(parts), *refs),
        out_shape=[jax.ShapeDtypeStruct((len(parts), rows, w), BF) for w in widths],
        cost_estimate=SMALL,
        name="pack",
    )(*parts)


def lay_kernel(*refs):
    out_ref, at = refs[-1], 0
    rows = out_ref.shape[0]
    for in_ref in refs[:-1]:
        width = in_ref.shape[1]
        for first in range(0, in_ref.shape[0], rows):
            out_ref[:, at : at + width] = in_ref[first : first + rows]
            at += width


def lay(rows, *parts):
    width = sum(part.shape[0] // rows * part.shape[1] for part in parts)
    return pl.pallas_call(
        lay_kernel,
        out_shape=jax.ShapeDtypeStruct((rows, width), BF),
        cost_estimate=SMALL,
        name="lay",
    )(*parts)


def lay_small_kernel(groups, lanes, count, *refs):
    mats, small, out_ref = refs[:count], refs[count:-1], refs[-1]
    rows, at = out_ref.shape[0], 0
    for in_ref in mats:
        out_ref[:, at : at + in_ref.shape[1]] = in_ref[...]
        at += in_ref.shape[1]
    out_ref[:, at:] = jnp.zeros((rows, groups * lanes), BF)
    for i, in_ref in enumerate(small):
        width = in_ref.shape[1]
        first = at + i % groups * lanes
        row = lax.broadcasted_iota(jnp.int32, (rows, width), 0)
        held = out_ref[:, first : first + width].astype(F32)
        value = jnp.broadcast_to(in_ref[...].astype(F32), (rows, width))
        out_ref[:, first : first + width] = jnp.where(row == i // groups, value, held).astype(BF)


def lay_small(rows, mats, small, groups, lanes):
    width = sum(mat.shape[1] for mat in mats) + groups * lanes
    return pl.pallas_call(
        lambda *refs: lay_small_kernel(groups, lanes, len(mats), *refs),
        out_shape=jax.ShapeDtypeStruct((rows, width), BF),
        cost_estimate=SMALL,
        name="lay_small",
    )(*mats, *[v[None] for v in small])


def near_rel(length, bits, n_seq):
    rel = [(z, n, 0) for n in (0, bits[0], bits[1], bits[0] ^ bits[1]) for z in range(length)]
    for bit in bits_of(n_seq):
        rel = rel + [(z, n, c ^ bit) for z, n, c in rel]
    return rel


def seq_parts(part, n_seq):
    parts = [part]
    for bit in bits_of(n_seq):
        parts = parts + [swap(p, "seq", n_seq, bit) for p in parts]
    return parts


def interleave(first, second):
    return [part for pair in zip(first, second) for part in pair]


def reorder_kernel(counts, table_ref, *refs):
    ins, out_ref = refs[: len(counts)], refs[len(counts)]
    place = 0
    for part_ref, count in zip(ins, counts):

        def move(i, carry, part_ref=part_ref, place=place):
            out_ref[table_ref[place + i]] = part_ref[i]
            return carry

        lax.fori_loop(0, count, move, 0)
        place += count


def places(parts, rel, seq_pos, chip_pos, n_chip, chunks):
    rows, width = parts[0].shape[1:]
    counts = [part.shape[0] for part in parts]
    total = sum(counts)
    step = width // chunks
    far, near, seq = (jnp.asarray(col, jnp.int32) for col in zip(*rel))
    table = (
        jnp.bitwise_xor(seq_pos, seq) * n_chip
        + jnp.bitwise_xor(chip_pos // NEAR, far) * NEAR
        + jnp.bitwise_xor(chip_pos % NEAR, near)
    )
    return table, counts, total, rows, width, step


def reorder_columns(parts, rel, seq_pos, chip_pos, n_chip, chunks):
    table, counts, total, rows, width, step = places(
        parts, rel, seq_pos, chip_pos, n_chip, chunks
    )
    out = pl.pallas_call(
        lambda *refs: reorder_kernel(counts, *refs),
        grid=(chunks,),
        in_specs=[pl.BlockSpec(memory_space=pltpu.SMEM)]
        + [pl.BlockSpec((count, rows, step), lambda c: (0, 0, c)) for count in counts],
        out_specs=pl.BlockSpec((total, rows, step), lambda c: (0, 0, c)),
        out_shape=jax.ShapeDtypeStruct((total, rows, width), BF),
        cost_estimate=SMALL,
        name="reorder",
    )(table, *parts)
    return out.reshape(total * rows, width)


def reorder_rows(parts, rel, seq_pos, chip_pos, n_chip, chunks):
    table, counts, total, rows, width, step = places(
        parts, rel, seq_pos, chip_pos, n_chip, chunks
    )
    out = pl.pallas_call(
        lambda *refs: reorder_kernel(counts, *refs),
        grid=(chunks,),
        in_specs=[pl.BlockSpec(memory_space=pltpu.SMEM)]
        + [pl.BlockSpec((count, rows, step), lambda c: (0, 0, c)) for count in counts],
        out_specs=pl.BlockSpec((total, None, rows, step), lambda c: (0, c, 0, 0)),
        out_shape=jax.ShapeDtypeStruct((total, chunks, rows, step), BF),
        cost_estimate=SMALL,
        name="reorder_rows",
    )(table, *parts)
    return out.reshape(total * chunks * rows, step)


def split_bit(index, bit):
    return (index // bit) % 2


def fold_kernel(axes, mine_ref, *refs):
    count = len(axes)
    ins, outs = refs[: 2 * count], refs[2 * count :]
    for i, axis in enumerate(axes):
        (kept_ref, got_ref), (give_ref, keep_ref) = ins[2 * i : 2 * i + 2], outs[2 * i : 2 * i + 2]
        mine = mine_ref[i]

        def block(f, carry, kept_ref=kept_ref, got_ref=got_ref, mine=mine, axis=axis, to=(give_ref, keep_ref)):
            for side, out_ref in zip((1 - mine, mine), to):
                if len(kept_ref.shape) == 4:
                    spots = [((f, side), (f,))]
                elif axis == 1:
                    spots = [((f, side, j), (f, j)) for j in range(2)]
                else:
                    spots = [((f, j, side), (f, j)) for j in range(2)]
                for source, target in spots:
                    out_ref[target] = kept_ref[source] + got_ref[source]
            return carry

        lax.fori_loop(0, kept_ref.shape[0], block, 0)


def fold(pairs, axes, mines):
    vmem = pl.BlockSpec(memory_space=pltpu.VMEM)
    shapes = [
        kept.shape[:axis] + kept.shape[axis + 1 :] for (kept, _), axis in zip(pairs, axes)
    ]
    outs = pl.pallas_call(
        lambda *refs: fold_kernel(axes, *refs),
        in_specs=[pl.BlockSpec(memory_space=pltpu.SMEM)] + [vmem] * (2 * len(pairs)),
        out_specs=[vmem] * (2 * len(pairs)),
        out_shape=[jax.ShapeDtypeStruct(shape, BF) for shape in shapes for _ in range(2)],
        cost_estimate=SMALL,
        name="fold",
    )(jnp.stack(mines).astype(jnp.int32), *[part for pair in pairs for part in pair])
    return list(zip(outs[::2], outs[1::2]))


CHUNK = 384


def gather_rows_kernel(out_ref_width, *refs):
    ins, out_ref = refs[:-1], refs[-1]
    at = 0
    for in_ref in ins:
        for first in range(0, in_ref.shape[1], CHUNK):
            row, col = at // out_ref_width, at % out_ref_width
            out_ref[row : row + 1, col : col + CHUNK] = in_ref[:, first : first + CHUNK]
            at += CHUNK


def gather_rows(vectors, rows):
    width = sum(v.shape[1] for v in vectors) // rows
    return pl.pallas_call(
        lambda *refs: gather_rows_kernel(width, *refs),
        out_shape=jax.ShapeDtypeStruct((rows, width), F32),
        cost_estimate=SMALL,
        name="gather_rows",
    )(*vectors)


class Scatter:
    def __init__(self, sums, where):
        self.n_seq, self.n_chip, self.seq_pos, self.chip_pos = where
        self.pairs, self.near = [], []
        for keep, recv, near in sums:
            rows, width = keep.shape[1:]
            for bit in bits_of(self.n_seq)[:-1][::-1]:
                total = (keep + recv).reshape(2, -1, rows, width)
                mine = split_bit(self.seq_pos, bit)
                give = lax.dynamic_index_in_dim(total, 1 - mine, 0, keepdims=False)
                keep = lax.dynamic_index_in_dim(total, mine, 0, keepdims=False)
                recv = swap(give, "seq", self.n_seq, bit)
            shape = (self.n_chip // NEAR, 2, 2, rows, width)
            self.pairs.append((keep.reshape(shape), recv.reshape(shape)))
            self.near.append(near)
        self.step([near[0] for near in self.near], [1 if near[0] == 2 else 2 for near in self.near])

    def step(self, bits, axes):
        mines = [split_bit(self.chip_pos, bit) for bit in bits]
        parts = fold(self.pairs, axes, mines)
        self.gives = tuple(give for give, _ in parts)
        self.pairs = [
            (kept, swap(give, "fsdp", self.n_chip, bit)) for (give, kept), bit in zip(parts, bits)
        ]

    def second(self, *gate):
        self.pairs = self.gated(*gate)
        self.step([near[1] for near in self.near], [1] * len(self.near))
        return self.gives

    def gated(self, *gate):
        return [(kept, after(got, *gate)) for kept, got in self.pairs]


def unpack_kernel(counts, extra, far_ref, *refs):
    pairs, outs = refs[: 2 * len(counts)], refs[2 * len(counts) + extra :]
    length = len(outs)
    rows = outs[0].shape[0]
    for k, out_ref in enumerate(outs):
        block = jnp.bitwise_xor(far_ref[0], k)
        at = 0
        for i, pieces in enumerate(counts):
            kept_ref, got_ref = pairs[2 * i : 2 * i + 2]
            width = kept_ref.shape[-1]
            for j in range(pieces):
                out_ref[:, at : at + width] = kept_ref[block, j] + got_ref[block, j]
                at += width
        if extra:
            out_ref[:, at:] = refs[2 * len(counts)][...].astype(BF)


def unpack(pairs, own_rows, far_pos, *extra):
    length = pairs[0][0].shape[0]
    counts = [kept.shape[1] // own_rows for kept, _ in pairs]
    parts = [
        part.reshape(length, n, own_rows, part.shape[2])
        for pair, n in zip(pairs, counts)
        for part in pair
    ]
    width = sum(part.shape[1] * part.shape[3] for part in parts[::2])
    width += sum(part.shape[1] for part in extra)
    vmem = pl.BlockSpec(memory_space=pltpu.VMEM)
    return pl.pallas_call(
        lambda *refs: unpack_kernel(counts, len(extra), *refs),
        in_specs=[pl.BlockSpec(memory_space=pltpu.SMEM)] + [vmem] * (len(parts) + len(extra)),
        out_shape=[jax.ShapeDtypeStruct((own_rows, width), BF)] * length,
        cost_estimate=SMALL,
        name="unpack",
    )(far_pos.reshape(1).astype(jnp.int32), *parts, *extra)


def far_sum(blocks, n_chip, *gate):
    got = [far_shift(block, n_chip, k) for k, block in enumerate(blocks[1:], 1)]
    total = blocks[0].astype(F32)
    for block in got:
        total = total + (after(block, *gate) if gate else block).astype(F32)
    return total


def solution(mesh):
    n_seq, n_chip = mesh.shape["seq"], mesh.shape["fsdp"]
    devices = n_seq * n_chip
    near_a, near_b = (2, 1), (1, 2)
    length = n_chip // NEAR
    top_seq = n_seq // 2
    swapped = n_seq == MB

    def local(
        inputs,
        order,
        lengths,
        cotangent,
        weight_qkv,
        bias_qv,
        weight_out,
        bias_out,
        weight_in,
        bias_in,
        weight_back,
        bias_back,
        gain_first,
        shift_first,
        gain_second,
        shift_second,
    ):
        seq_pos, chip_pos = lax.axis_index("seq"), lax.axis_index("fsdp")
        me = seq_pos * n_chip + chip_pos
        rows_here = inputs.shape[2]

        small = [
            bias_qv,
            bias_out,
            bias_in,
            bias_back,
            gain_first,
            shift_first,
            gain_second,
            shift_second,
        ]
        widths = [v.shape[0] for v in small]
        far_pos = chip_pos // NEAR
        own_rows = weight_in.shape[0]

        lanes = -(-max(widths) // 128) * 128
        groups = -(-len(small) // own_rows)
        early = lay_small(own_rows, [weight_qkv, weight_out], small, groups, lanes)
        half = 2 * D
        early_far = far_gather(early, n_chip)
        late = lay(own_rows, weight_in, weight_back)
        late_far = far_gather(after(late, *early_far), n_chip)

        def near(block, bit):
            return swap(block, "fsdp", n_chip, bit)

        def join(block, other):
            return jnp.concatenate([block, other], axis=0)

        a_block, b_block = pack(early_far, [half, half + groups * lanes])
        a_first, b_first = near(a_block, near_a[0]), near(b_block, near_b[0])
        a_whole, b_whole = join(a_block, a_first), join(b_block, b_first)
        a_last, b_last = near(a_whole, near_a[1]), near(b_whole, near_b[1])
        a_parts = interleave(seq_parts(a_whole, n_seq), seq_parts(a_last, n_seq))
        b_parts = interleave(seq_parts(b_whole, n_seq), seq_parts(b_last, n_seq))
        gated = lax.optimization_barrier(tuple(late_far) + (a_last, b_last))[: len(late_far)]
        in_block, back_block = pack(gated, [FF, FF])
        in_first, back_first = near(in_block, near_a[0]), near(back_block, near_b[0])

        a_rel, b_rel = near_rel(length, near_a, n_seq), near_rel(length, near_b, n_seq)
        spot = (seq_pos, chip_pos, n_chip)
        qk_mat = reorder_columns(a_parts, a_rel, *spot, 2)
        vo_mat = reorder_columns(b_parts, b_rel, *spot, 1)
        v_mat, out_mat = vo_mat[:, :D], vo_mat[:, D : 2 * D]

        holders = places(b_parts, b_rel, *spot, 1)[0]
        pick = (jnp.arange(devices, dtype=jnp.int32)[:, None] == holders[None, :]).astype(BF)
        used = -(-len(small) // groups)
        vec_held = jnp.concatenate([part[:, :used, half:] for part in b_parts], axis=0)
        vec_all = dot_plain(pick, vec_held.reshape(devices, -1))
        in_whole = join(in_block, after(in_first, vo_mat))
        back_whole = join(back_block, after(back_first, vo_mat))
        vec_all = after(vec_all, in_whole, back_whole)
        vectors = [
            vec_all[:, i * lanes : i * lanes + width].reshape(-1) for i, width in enumerate(widths)
        ]
        qv_vec, out_vec, in_vec, back_vec, gain_one, shift_one, gain_two, shift_two = vectors

        def bring(rows):
            if not swapped:
                return rows[:, 0].reshape(MB * rows_here, D)
            mine = lax.dynamic_index_in_dim(rows[:, 0], seq_pos, 0, keepdims=False)
            other = lax.dynamic_index_in_dim(rows[:, 0], 1 - seq_pos, 0, keepdims=False)
            return jnp.concatenate([mine, swap(other, "seq", n_seq, 1)], axis=0)

        def bring_back(*results):
            if not swapped:
                return [rows.reshape(MB, 1, rows_here, D) for rows in results]
            others = swap(jnp.stack([rows[rows_here:] for rows in results]), "seq", n_seq, 1)
            first = seq_pos == 0
            return [
                jnp.stack(
                    [
                        jnp.where(first, rows[:rows_here], other),
                        jnp.where(first, other, rows[:rows_here]),
                    ]
                )[:, None]
                for rows, other in zip(results, others)
            ]

        ends = jnp.cumsum(lengths[:, 0], axis=1)
        if swapped:
            ids = lax.dynamic_index_in_dim(order[:, 0], seq_pos, 0, keepdims=False)
            ids = jnp.concatenate(
                [
                    lax.dynamic_slice_in_dim(ids, seq_pos * rows_here, rows_here, 0),
                    lax.dynamic_slice_in_dim(ids, (1 - seq_pos) * rows_here, rows_here, 0),
                ]
            )
            qpos = kpos = ids[None]
            ends = lax.dynamic_index_in_dim(ends, seq_pos, 0, keepdims=True)
        else:
            kpos = order[:, 0]
            qpos = lax.dynamic_slice_in_dim(kpos, seq_pos * rows_here, rows_here, 1)
        qstart = jnp.max(
            jnp.where(ends[:, None, :] <= qpos[:, :, None], ends[:, None, :], 0), axis=2
        )
        streams = qpos.shape[0]

        def by_stream(rows):
            return rows.reshape(streams, -1, rows.shape[-1])

        x_float = bring(inputs).astype(F32)
        grad_rows = bring(cotangent)
        grad_float = grad_rows.astype(F32)
        x_hat_one, inv_one = norm_parts(x_float)
        normed = (x_hat_one * gain_one + shift_one).astype(BF)
        q_bias = jnp.concatenate([qv_vec[:D], jnp.zeros((D,), F32)])
        qk = by_stream((dot_plain(normed, qk_mat) + q_bias).astype(BF))
        value_rows = by_stream((dot_plain(normed, v_mat) + qv_vec[D:]).astype(BF))
        pairs = HEADS // 2
        if not swapped:
            q = (qk, 0)
            k = (lax.all_gather(qk[:, :, D:], "seq", axis=1, tiled=True), 0)
            v = (lax.all_gather(value_rows, "seq", axis=1, tiled=True), 0)
        if swapped:
            qk, value_rows, _, _, grad_rows = lax.optimization_barrier(
                (qk, value_rows, in_whole, back_whole, grad_rows)
            )
            grad_float = grad_rows.astype(F32)
            q, k, v = (qk, 0), (qk, pairs), (value_rows, 0)
        attn_heads, probs = attend(q, k, v, qpos, qstart, kpos)
        in_last = near(in_whole, near_a[1])
        back_last = near(back_whole, near_b[1])
        in_wholes = seq_parts(in_whole, n_seq)
        back_wholes = seq_parts(back_whole, n_seq)
        attn_heads = attn_heads.reshape(-1, D)
        mid_stream = x_float + dot_plain(attn_heads, out_mat) + out_vec
        x_hat_two, inv_two = norm_parts(mid_stream)
        normed_two = (x_hat_two * gain_two + shift_two).astype(BF)
        in_last, back_last, _ = lax.optimization_barrier((in_last, back_last, normed_two))
        in_parts = interleave(in_wholes, seq_parts(in_last, n_seq))
        back_parts = interleave(back_wholes, seq_parts(back_last, n_seq))
        in_mat = reorder_columns(in_parts, a_rel, *spot, 4)
        d_back_vec = jnp.sum(grad_rows.astype(F32), axis=0, keepdims=True)
        in_mat, d_back_vec, *back_parts = lax.optimization_barrier((in_mat, d_back_vec, *back_parts))
        pre_act = dot_plain(normed_two, in_mat) + in_vec
        hidden_float, gelu_pull = jax.vjp(gelu_tanh, pre_act)
        hidden = hidden_float.astype(BF)

        top_mine = split_bit(seq_pos, top_seq)

        def halves(left, right):
            half = left.shape[1] // 2

            def part(which):
                return dot_first(
                    lax.dynamic_slice_in_dim(left, which * half, half, 1), right
                ).astype(BF)

            return part(1 - top_mine), part(top_mine)

        where = (n_seq, n_chip, seq_pos, chip_pos)

        def scatter(*sums):
            shaped = []
            for recv, keep, near in sums:
                shape = (devices // 2, keep.shape[0] // (devices // 2), keep.shape[1])
                shaped.append((keep.reshape(shape), recv.reshape(shape), near))
            return Scatter(shaped, where)

        back_give, back_keep = halves(hidden, grad_rows)
        back_recv = swap(back_give, "seq", n_seq, top_seq)
        back_parts = [after(part, back_give) for part in back_parts]
        back_mat = reorder_rows(back_parts, b_rel, *spot, FF // D)
        d_hidden = dot_last(after(grad_rows, back_keep, back_recv), back_mat)
        d_pre = gelu_pull(d_hidden)[0].astype(BF)
        in_give, in_keep = halves(normed_two, d_pre)
        in_recv = swap(in_give, "seq", n_seq, top_seq)
        late_sum = scatter((in_recv, in_keep, near_a), (back_recv, back_keep, near_b))
        d_pre = after(d_pre, *late_sum.gives)
        d_norm_two = dot_last(d_pre, in_mat)
        d_mid = grad_float + norm_back(d_norm_two, x_hat_two, inv_two, gain_two)
        d_mid_low = d_mid.astype(BF)
        d_heads = by_stream(dot_last(d_mid_low, out_mat).astype(BF))
        out_give, out_keep = halves(attn_heads, d_mid_low)
        d_heads = after(d_heads, out_give, out_keep)
        *d_parts, d_values = attend_back(q, k, v, d_heads, probs)
        sent = late_sum.second(d_values)
        if not swapped:
            d_keys = lax.psum_scatter(d_parts[1], "seq", scatter_dimension=1, tiled=True)
            d_values = lax.psum_scatter(d_values, "seq", scatter_dimension=1, tiled=True)
            d_parts = [jnp.concatenate([d_parts[0], d_keys], axis=2)]
        d_qk = d_parts[0].reshape(-1, 2 * D)
        d_values = d_values.reshape(-1, D)
        d_qk, d_values, _, _ = lax.optimization_barrier((d_qk, d_values) + sent)
        qk_give, qk_keep = halves(normed, d_qk)
        v_give, v_keep = halves(normed, d_values)
        vo_give = jnp.concatenate([v_give, out_give], axis=1)
        vo_keep = jnp.concatenate([v_keep, out_keep], axis=1)
        qk_recv, vo_recv = (swap(give, "seq", n_seq, top_seq) for give in (qk_give, vo_give))
        early_sum = scatter((qk_recv, qk_keep, near_a), (vo_recv, vo_keep, near_b))
        sent = early_sum.gives
        late_blocks = unpack(late_sum.gated(*sent), own_rows, far_pos)
        d_qk, d_values, d_pre, d_mid_late, _, _ = lax.optimization_barrier(
            (d_qk, d_values, d_pre, d_mid) + sent
        )
        d_in_vec = jnp.sum(d_pre.astype(F32), axis=0, keepdims=True)
        d_norm_late = after(d_norm_two, *sent)
        d_gain_two = jnp.sum(d_norm_late * x_hat_two, axis=0, keepdims=True)
        d_shift_two = jnp.sum(d_norm_late, axis=0, keepdims=True)
        d_out_vec = jnp.sum(d_mid_late, axis=0, keepdims=True)
        q_sums = jnp.sum(d_qk[:, :D].astype(F32), axis=0, keepdims=True)
        v_sums = jnp.sum(d_values.astype(F32), axis=0, keepdims=True)
        d_norm_half = dot_last(after(d_qk, late_blocks[0]), qk_mat)
        sent = early_sum.second(d_norm_half)
        d_norm_one = d_norm_half + dot_last(after(d_values, *sent), v_mat)
        pairs_left = early_sum.gated(d_norm_one)
        d_norm_one = after(d_norm_one, *[got for _, got in pairs_left])
        d_inputs = d_mid + norm_back(d_norm_one, x_hat_one, inv_one, gain_one)
        input_grad = d_inputs.astype(BF)
        d_gain_one = jnp.sum(d_norm_one * x_hat_one, axis=0, keepdims=True)
        d_shift_one = jnp.sum(d_norm_one, axis=0, keepdims=True)

        vec_grads = [
            q_sums,
            v_sums,
            d_out_vec,
            d_in_vec,
            d_back_vec,
            d_gain_one,
            d_shift_one,
            d_gain_two,
            d_shift_two,
        ]
        vec_sum = gather_rows(vec_grads, own_rows)
        for bit in bits_of(n_seq):
            vec_sum = vec_sum + swap(vec_sum, "seq", n_seq, bit)
        vec_sum = vec_sum + swap(vec_sum, "fsdp", n_chip, 1)
        vec_sum = vec_sum + swap(vec_sum, "fsdp", n_chip, 2)
        early_blocks = unpack(pairs_left, own_rows, far_pos, vec_sum)
        hidden, _ = lax.optimization_barrier((hidden, early_blocks[0]))
        block_out = (mid_stream + dot_plain(hidden, back_mat) + back_vec).astype(BF)
        block_out, input_grad = bring_back(block_out, input_grad)
        late_sum = far_sum(late_blocks, n_chip, early_blocks[0])
        early_sum = far_sum(early_blocks, n_chip)
        d_in_mat = late_sum[:, :FF]
        d_back_mat = jnp.concatenate(
            [late_sum[:, i : i + D] for i in range(FF, 2 * FF, D)], axis=0
        )
        d_qkv_mat, d_out_mat = early_sum[:, : 3 * D], early_sum[:, 3 * D : 4 * D]
        vec_sum = early_sum[:, 4 * D :]
        long = vec_sum.shape[1]
        g_out, at = [], 0
        for width in widths:
            spot_at = at + me * width
            got = lax.dynamic_slice(vec_sum, (spot_at // long, spot_at % long), (1, width))
            g_out.append(got[0])
            at += width * devices
        g_qv, g_out_vec, g_in, g_back, g_gain1, g_shift1, g_gain2, g_shift2 = g_out
        return (
            block_out,
            input_grad,
            d_qkv_mat,
            g_qv,
            d_out_mat,
            g_out_vec,
            d_in_mat,
            g_in,
            d_back_mat,
            g_back,
            g_gain1,
            g_shift1,
            g_gain2,
            g_shift2,
        )

    tokens, sharded, vector = P(None, "fsdp", "seq", None), P(("seq", "fsdp"), None), P(("seq", "fsdp"))
    streams_spec = P(None, "fsdp", None)
    return jax.shard_map(
        local,
        mesh=mesh,
        in_specs=(tokens, streams_spec, streams_spec, tokens) + (sharded, vector) * 4 + (vector,) * 4,
        out_specs=(tokens, tokens) + (sharded, vector) * 4 + (vector,) * 4,
        check_vma=False,
    )
```

```python
import jax
import jax.numpy as jnp
from jax import lax
from jax.experimental import pallas as pl
from jax.experimental.pallas import tpu as pltpu
from jax.sharding import PartitionSpec as P

D = 768
HEADS = 12
HD = 64
FF = 3072
MB = 2
PAIR = 2 * HD

eps = 1e-05
score_scale = 0.125
BF = jnp.bfloat16
F32 = jnp.float32
SMALL = pl.CostEstimate(flops=1, transcendentals=0, bytes_accessed=1)


def norm_parts(values):
    row_mean = jnp.mean(values, axis=-1, keepdims=True)
    centred = values - row_mean
    inv_std = lax.rsqrt(jnp.mean(centred * centred, axis=-1, keepdims=True) + eps)
    return (centred * inv_std, inv_std)


def norm_back(grad_norm, x_hat, inv_std, gain):
    scaled = grad_norm * gain
    return inv_std * (
        scaled
        - jnp.mean(scaled, axis=-1, keepdims=True)
        - x_hat * jnp.mean(scaled * x_hat, axis=-1, keepdims=True)
    )


def gelu_tanh(values):
    return (
        0.5
        * values
        * (1.0 + jnp.tanh(0.7978845608028654 * (values + 0.044715 * values * values * values)))
    )


def dot_first(left, right):
    return lax.dot_general(left, right, (((0,), (0,)), ((), ())), preferred_element_type=F32)


def dot_last(left, right):
    return lax.dot_general(left, right, (((1,), (1,)), ((), ())), preferred_element_type=F32)


def dot_plain(left, right):
    return jnp.dot(left, right, preferred_element_type=F32)


def attend_kernel(q_ref, k_ref, v_ref, qpos_ref, qstart_ref, kpos_ref, out_ref, prob_ref, bias_ref):
    @pl.when(pl.program_id(1) == 0)
    def _():
        kpos = kpos_ref[0]
        seen = (kpos <= qpos_ref[0]) & (kpos >= qstart_ref[0])
        bias_ref[...] = jnp.where(seen, 0.0, -1e30)

    q, k, v = q_ref[0], k_ref[0], v_ref[0]
    lane = lax.broadcasted_iota(jnp.int32, q.shape, 1)
    scaled = q * jnp.asarray(score_scale, BF)
    halves = []
    for j in range(2):
        q_head = jnp.where((lane // HD) == j, scaled, jnp.zeros_like(scaled))
        scores = dot_last(k, q_head) + bias_ref[...]
        col_max = jnp.max(scores, axis=0, keepdims=True)
        expo = jnp.exp(scores - col_max)
        probs = (expo * (1.0 / jnp.sum(expo, axis=0, keepdims=True))).astype(BF)
        prob_ref[0, j] = probs
        halves.append(dot_first(v, probs))
    row = lax.broadcasted_iota(jnp.int32, halves[0].shape, 0)
    out_ref[0] = jnp.where(row < HD, halves[0], halves[1]).T.astype(BF)


def attend_back_kernel(q_ref, k_ref, v_ref, dh_ref, prob_ref, *out_refs):
    dqk_refs, dv_ref = out_refs[:-1], out_refs[-1]
    q, k, v, dh = q_ref[0], k_ref[0], v_ref[0], dh_ref[0]
    lane = lax.broadcasted_iota(jnp.int32, dh.shape, 1)
    dq, dk, dv = [], [], []
    for j in range(2):
        probs = prob_ref[0, j]
        dh_head = jnp.where((lane // HD) == j, dh, jnp.zeros_like(dh))
        d_prob = dot_last(v, dh_head)
        wide = probs.astype(F32)
        moved = wide * d_prob
        centre = jnp.sum(moved, axis=0, keepdims=True)
        d_scores = (moved - wide * centre).astype(BF)
        dq.append(dot_first(k, d_scores))
        dk.append(dot_plain(d_scores, q))
        dv.append(dot_plain(probs, dh))
    row = lax.broadcasted_iota(jnp.int32, dq[0].shape, 0)
    col = lax.broadcasted_iota(jnp.int32, dk[0].shape, 1)
    dq_out = (score_scale * jnp.where(row < HD, dq[0], dq[1])).T.astype(BF)
    dk_out = (score_scale * jnp.where(col < HD, dk[0], dk[1])).astype(BF)
    if len(dqk_refs) == 1:
        at = pl.program_id(1) * PAIR
        dqk_refs[0][0, :, pl.ds(pl.multiple_of(at, PAIR), PAIR)] = dq_out
        dqk_refs[0][0, :, pl.ds(pl.multiple_of(D + at, PAIR), PAIR)] = dk_out
    else:
        dqk_refs[0][0], dqk_refs[1][0] = dq_out, dk_out
    dv_ref[0] = jnp.where(col < HD, dv[0], dv[1]).astype(BF)


def cols(rows, offset):
    return pl.BlockSpec((1, rows, PAIR), lambda s, h: (s, 0, h + offset))


def attend(q, k, v, qpos, qstart, kpos):
    (q_arr, q_off), (k_arr, k_off), (v_arr, v_off) = q, k, v
    streams, rows = q_arr.shape[:2]
    keys = k_arr.shape[1]
    pairs = HEADS // 2
    return pl.pallas_call(
        attend_kernel,
        grid=(streams, pairs),
        in_specs=[
            cols(rows, q_off),
            cols(keys, k_off),
            cols(keys, v_off),
            pl.BlockSpec((1, 1, rows), lambda s, h: (s, 0, 0)),
            pl.BlockSpec((1, 1, rows), lambda s, h: (s, 0, 0)),
            pl.BlockSpec((1, keys, 1), lambda s, h: (s, 0, 0)),
        ],
        out_specs=[
            cols(rows, 0),
            pl.BlockSpec((1, 2, keys, rows), lambda s, h: (s, h, 0, 0)),
        ],
        out_shape=[
            jax.ShapeDtypeStruct((streams, rows, D), BF),
            jax.ShapeDtypeStruct((streams, HEADS, keys, rows), BF),
        ],
        scratch_shapes=[pltpu.VMEM((keys, rows), F32)],
        cost_estimate=SMALL,
        name="attend",
    )(q_arr, k_arr, v_arr, qpos[:, None, :], qstart[:, None, :], kpos[:, :, None])


def attend_back(q, k, v, d_heads, probs):
    (q_arr, q_off), (k_arr, k_off), (v_arr, v_off) = q, k, v
    streams, rows = q_arr.shape[:2]
    keys = k_arr.shape[1]
    pairs = HEADS // 2
    if rows == keys:
        specs = [pl.BlockSpec((1, rows, 2 * D), lambda s, h: (s, 0, 0))]
        shapes = [(rows, 2 * D)]
    else:
        specs, shapes = [cols(rows, 0), cols(keys, 0)], [(rows, D), (keys, D)]
    return pl.pallas_call(
        attend_back_kernel,
        grid=(streams, pairs),
        in_specs=[
            cols(rows, q_off),
            cols(keys, k_off),
            cols(keys, v_off),
            cols(rows, 0),
            pl.BlockSpec((1, 2, keys, rows), lambda s, h: (s, h, 0, 0)),
        ],
        out_specs=specs + [cols(keys, 0)],
        out_shape=[jax.ShapeDtypeStruct((streams,) + shape, BF) for shape in shapes + [(keys, D)]],
        cost_estimate=SMALL,
        name="attend_back",
    )(q_arr, k_arr, v_arr, d_heads, probs)


def after(value, *others):
    return lax.optimization_barrier((value,) + others)[0]


def bits_of(count):
    return [1 << b for b in range(count.bit_length() - 1)]


def swap(value, axis, count, bit):
    return lax.ppermute(value, axis, [(i, i ^ bit) for i in range(count)])


def after(value, *others):
    return lax.optimization_barrier((value,) + others)[0]


NEAR = 4


def far_shift(value, n_chip, by):
    return swap(value, "fsdp", n_chip, by * NEAR)


def far_gather(shard, n_chip):
    return [shard] + [far_shift(shard, n_chip, k) for k in range(1, n_chip // NEAR)]


def pack_kernel(count, *refs):
    ins, outs = refs[:count], refs[count:]
    at = 0
    for out_ref in outs:
        width = out_ref.shape[2]
        for i, in_ref in enumerate(ins):
            out_ref[i] = in_ref[:, at : at + width]
        at += width


def pack(parts, widths):
    rows = parts[0].shape[0]
    return pl.pallas_call(
        lambda *refs: pack_kernel(len(parts), *refs),
        out_shape=[jax.ShapeDtypeStruct((len(parts), rows, w), BF) for w in widths],
        cost_estimate=SMALL,
        name="pack",
    )(*parts)


def lay_kernel(*refs):
    out_ref, at = refs[-1], 0
    rows = out_ref.shape[0]
    for in_ref in refs[:-1]:
        width = in_ref.shape[1]
        for first in range(0, in_ref.shape[0], rows):
            out_ref[:, at : at + width] = in_ref[first : first + rows]
            at += width


def lay(rows, *parts):
    width = sum(part.shape[0] // rows * part.shape[1] for part in parts)
    return pl.pallas_call(
        lay_kernel,
        out_shape=jax.ShapeDtypeStruct((rows, width), BF),
        cost_estimate=SMALL,
        name="lay",
    )(*parts)


def lay_small_kernel(groups, lanes, count, *refs):
    mats, small, out_ref = refs[:count], refs[count:-1], refs[-1]
    rows, at = out_ref.shape[0], 0
    for in_ref in mats:
        out_ref[:, at : at + in_ref.shape[1]] = in_ref[...]
        at += in_ref.shape[1]
    out_ref[:, at:] = jnp.zeros((rows, groups * lanes), BF)
    for i, in_ref in enumerate(small):
        width = in_ref.shape[1]
        first = at + i % groups * lanes
        row = lax.broadcasted_iota(jnp.int32, (rows, width), 0)
        held = out_ref[:, first : first + width].astype(F32)
        value = jnp.broadcast_to(in_ref[...].astype(F32), (rows, width))
        out_ref[:, first : first + width] = jnp.where(row == i // groups, value, held).astype(BF)


def lay_small(rows, mats, small, groups, lanes):
    width = sum(mat.shape[1] for mat in mats) + groups * lanes
    return pl.pallas_call(
        lambda *refs: lay_small_kernel(groups, lanes, len(mats), *refs),
        out_shape=jax.ShapeDtypeStruct((rows, width), BF),
        cost_estimate=SMALL,
        name="lay_small",
    )(*mats, *[v[None] for v in small])


def near_rel(length, bits, n_seq):
    rel = [(z, n, 0) for n in (0, bits[0], bits[1], bits[0] ^ bits[1]) for z in range(length)]
    for bit in bits_of(n_seq):
        rel = rel + [(z, n, c ^ bit) for z, n, c in rel]
    return rel


def seq_parts(part, n_seq):
    parts = [part]
    for bit in bits_of(n_seq):
        parts = parts + [swap(p, "seq", n_seq, bit) for p in parts]
    return parts


def interleave(first, second):
    return [part for pair in zip(first, second) for part in pair]


def reorder_kernel(counts, table_ref, *refs):
    ins, out_ref = refs[: len(counts)], refs[len(counts)]
    place = 0
    for part_ref, count in zip(ins, counts):

        def move(i, carry, part_ref=part_ref, place=place):
            out_ref[table_ref[place + i]] = part_ref[i]
            return carry

        lax.fori_loop(0, count, move, 0)
        place += count


def places(parts, rel, seq_pos, chip_pos, n_chip, chunks):
    rows, width = parts[0].shape[1:]
    counts = [part.shape[0] for part in parts]
    total = sum(counts)
    step = width // chunks
    far, near, seq = (jnp.asarray(col, jnp.int32) for col in zip(*rel))
    table = (
        jnp.bitwise_xor(seq_pos, seq) * n_chip
        + jnp.bitwise_xor(chip_pos // NEAR, far) * NEAR
        + jnp.bitwise_xor(chip_pos % NEAR, near)
    )
    return table, counts, total, rows, width, step


def reorder_columns(parts, rel, seq_pos, chip_pos, n_chip, chunks):
    table, counts, total, rows, width, step = places(
        parts, rel, seq_pos, chip_pos, n_chip, chunks
    )
    out = pl.pallas_call(
        lambda *refs: reorder_kernel(counts, *refs),
        grid=(chunks,),
        in_specs=[pl.BlockSpec(memory_space=pltpu.SMEM)]
        + [pl.BlockSpec((count, rows, step), lambda c: (0, 0, c)) for count in counts],
        out_specs=pl.BlockSpec((total, rows, step), lambda c: (0, 0, c)),
        out_shape=jax.ShapeDtypeStruct((total, rows, width), BF),
        cost_estimate=SMALL,
        name="reorder",
    )(table, *parts)
    return out.reshape(total * rows, width)


def reorder_rows(parts, rel, seq_pos, chip_pos, n_chip, chunks):
    table, counts, total, rows, width, step = places(
        parts, rel, seq_pos, chip_pos, n_chip, chunks
    )
    out = pl.pallas_call(
        lambda *refs: reorder_kernel(counts, *refs),
        grid=(chunks,),
        in_specs=[pl.BlockSpec(memory_space=pltpu.SMEM)]
        + [pl.BlockSpec((count, rows, step), lambda c: (0, 0, c)) for count in counts],
        out_specs=pl.BlockSpec((total, None, rows, step), lambda c: (0, c, 0, 0)),
        out_shape=jax.ShapeDtypeStruct((total, chunks, rows, step), BF),
        cost_estimate=SMALL,
        name="reorder_rows",
    )(table, *parts)
    return out.reshape(total * chunks * rows, step)


def split_bit(index, bit):
    return (index // bit) % 2


def fold_kernel(axes, mine_ref, *refs):
    count = len(axes)
    ins, outs = refs[: 2 * count], refs[2 * count :]
    for i, axis in enumerate(axes):
        (kept_ref, got_ref), (give_ref, keep_ref) = ins[2 * i : 2 * i + 2], outs[2 * i : 2 * i + 2]
        mine = mine_ref[i]

        def block(f, carry, kept_ref=kept_ref, got_ref=got_ref, mine=mine, axis=axis, to=(give_ref, keep_ref)):
            for side, out_ref in zip((1 - mine, mine), to):
                if len(kept_ref.shape) == 4:
                    spots = [((f, side), (f,))]
                elif axis == 1:
                    spots = [((f, side, j), (f, j)) for j in range(2)]
                else:
                    spots = [((f, j, side), (f, j)) for j in range(2)]
                for source, target in spots:
                    out_ref[target] = kept_ref[source] + got_ref[source]
            return carry

        lax.fori_loop(0, kept_ref.shape[0], block, 0)


def fold(pairs, axes, mines):
    vmem = pl.BlockSpec(memory_space=pltpu.VMEM)
    shapes = [
        kept.shape[:axis] + kept.shape[axis + 1 :] for (kept, _), axis in zip(pairs, axes)
    ]
    outs = pl.pallas_call(
        lambda *refs: fold_kernel(axes, *refs),
        in_specs=[pl.BlockSpec(memory_space=pltpu.SMEM)] + [vmem] * (2 * len(pairs)),
        out_specs=[vmem] * (2 * len(pairs)),
        out_shape=[jax.ShapeDtypeStruct(shape, BF) for shape in shapes for _ in range(2)],
        cost_estimate=SMALL,
        name="fold",
    )(jnp.stack(mines).astype(jnp.int32), *[part for pair in pairs for part in pair])
    return list(zip(outs[::2], outs[1::2]))


CHUNK = 384


def gather_rows_kernel(out_ref_width, *refs):
    ins, out_ref = refs[:-1], refs[-1]
    at = 0
    for in_ref in ins:
        for first in range(0, in_ref.shape[1], CHUNK):
            row, col = at // out_ref_width, at % out_ref_width
            out_ref[row : row + 1, col : col + CHUNK] = in_ref[:, first : first + CHUNK]
            at += CHUNK


def gather_rows(vectors, rows):
    width = sum(v.shape[1] for v in vectors) // rows
    return pl.pallas_call(
        lambda *refs: gather_rows_kernel(width, *refs),
        out_shape=jax.ShapeDtypeStruct((rows, width), F32),
        cost_estimate=SMALL,
        name="gather_rows",
    )(*vectors)


class Scatter:
    def __init__(self, sums, where):
        self.n_seq, self.n_chip, self.seq_pos, self.chip_pos = where
        self.pairs, self.near = [], []
        for keep, recv, near in sums:
            rows, width = keep.shape[1:]
            for bit in bits_of(self.n_seq)[:-1][::-1]:
                total = (keep + recv).reshape(2, -1, rows, width)
                mine = split_bit(self.seq_pos, bit)
                give = lax.dynamic_index_in_dim(total, 1 - mine, 0, keepdims=False)
                keep = lax.dynamic_index_in_dim(total, mine, 0, keepdims=False)
                recv = swap(give, "seq", self.n_seq, bit)
            shape = (self.n_chip // NEAR, 2, 2, rows, width)
            self.pairs.append((keep.reshape(shape), recv.reshape(shape)))
            self.near.append(near)
        self.step([near[0] for near in self.near], [1 if near[0] == 2 else 2 for near in self.near])

    def step(self, bits, axes):
        mines = [split_bit(self.chip_pos, bit) for bit in bits]
        parts = fold(self.pairs, axes, mines)
        self.gives = tuple(give for give, _ in parts)
        self.pairs = [
            (kept, swap(give, "fsdp", self.n_chip, bit)) for (give, kept), bit in zip(parts, bits)
        ]

    def second(self, *gate):
        self.pairs = self.gated(*gate)
        self.step([near[1] for near in self.near], [1] * len(self.near))
        return self.gives

    def gated(self, *gate):
        return [(kept, after(got, *gate)) for kept, got in self.pairs]


def unpack_kernel(counts, extra, far_ref, *refs):
    pairs, outs = refs[: 2 * len(counts)], refs[2 * len(counts) + extra :]
    length = len(outs)
    rows = outs[0].shape[0]
    for k, out_ref in enumerate(outs):
        block = jnp.bitwise_xor(far_ref[0], k)
        at = 0
        for i, pieces in enumerate(counts):
            kept_ref, got_ref = pairs[2 * i : 2 * i + 2]
            width = kept_ref.shape[-1]
            for j in range(pieces):
                out_ref[:, at : at + width] = kept_ref[block, j] + got_ref[block, j]
                at += width
        if extra:
            out_ref[:, at:] = refs[2 * len(counts)][...].astype(BF)


def unpack(pairs, own_rows, far_pos, *extra):
    length = pairs[0][0].shape[0]
    counts = [kept.shape[1] // own_rows for kept, _ in pairs]
    parts = [
        part.reshape(length, n, own_rows, part.shape[2])
        for pair, n in zip(pairs, counts)
        for part in pair
    ]
    width = sum(part.shape[1] * part.shape[3] for part in parts[::2])
    width += sum(part.shape[1] for part in extra)
    vmem = pl.BlockSpec(memory_space=pltpu.VMEM)
    return pl.pallas_call(
        lambda *refs: unpack_kernel(counts, len(extra), *refs),
        in_specs=[pl.BlockSpec(memory_space=pltpu.SMEM)] + [vmem] * (len(parts) + len(extra)),
        out_shape=[jax.ShapeDtypeStruct((own_rows, width), BF)] * length,
        cost_estimate=SMALL,
        name="unpack",
    )(far_pos.reshape(1).astype(jnp.int32), *parts, *extra)


def far_sum(blocks, n_chip, *gate):
    got = [far_shift(block, n_chip, k) for k, block in enumerate(blocks[1:], 1)]
    total = blocks[0].astype(F32)
    for block in got:
        total = total + (after(block, *gate) if gate else block).astype(F32)
    return total


def solution(mesh):
    n_seq, n_chip = mesh.shape["seq"], mesh.shape["fsdp"]
    devices = n_seq * n_chip
    near_a, near_b = (2, 1), (1, 2)
    length = n_chip // NEAR
    top_seq = n_seq // 2
    swapped = n_seq == MB

    def local(
        inputs,
        order,
        lengths,
        cotangent,
        weight_qkv,
        bias_qv,
        weight_out,
        bias_out,
        weight_in,
        bias_in,
        weight_back,
        bias_back,
        gain_first,
        shift_first,
        gain_second,
        shift_second,
    ):
        seq_pos, chip_pos = lax.axis_index("seq"), lax.axis_index("fsdp")
        me = seq_pos * n_chip + chip_pos
        rows_here = inputs.shape[2]

        small = [
            bias_qv,
            bias_out,
            bias_in,
            bias_back,
            gain_first,
            shift_first,
            gain_second,
            shift_second,
        ]
        widths = [v.shape[0] for v in small]
        far_pos = chip_pos // NEAR
        own_rows = weight_in.shape[0]

        lanes = -(-max(widths) // 128) * 128
        groups = -(-len(small) // own_rows)
        early = lay_small(own_rows, [weight_qkv, weight_out], small, groups, lanes)
        half = 2 * D
        early_far = far_gather(early, n_chip)
        late = lay(own_rows, weight_in, weight_back)
        late_far = far_gather(after(late, *early_far), n_chip)

        def near(block, bit):
            return swap(block, "fsdp", n_chip, bit)

        def join(block, other):
            return jnp.concatenate([block, other], axis=0)

        a_block, b_block = pack(early_far, [half, half + groups * lanes])
        a_first, b_first = near(a_block, near_a[0]), near(b_block, near_b[0])
        a_whole, b_whole = join(a_block, a_first), join(b_block, b_first)
        a_last, b_last = near(a_whole, near_a[1]), near(b_whole, near_b[1])
        a_parts = interleave(seq_parts(a_whole, n_seq), seq_parts(a_last, n_seq))
        b_parts = interleave(seq_parts(b_whole, n_seq), seq_parts(b_last, n_seq))
        gated = lax.optimization_barrier(tuple(late_far) + (a_last, b_last))[: len(late_far)]
        in_block, back_block = pack(gated, [FF, FF])
        in_first, back_first = near(in_block, near_a[0]), near(back_block, near_b[0])

        a_rel, b_rel = near_rel(length, near_a, n_seq), near_rel(length, near_b, n_seq)
        spot = (seq_pos, chip_pos, n_chip)
        qk_mat = reorder_columns(a_parts, a_rel, *spot, 2)
        vo_mat = reorder_columns(b_parts, b_rel, *spot, 1)
        v_mat, out_mat = vo_mat[:, :D], vo_mat[:, D : 2 * D]

        holders = places(b_parts, b_rel, *spot, 1)[0]
        pick = (jnp.arange(devices, dtype=jnp.int32)[:, None] == holders[None, :]).astype(BF)
        used = -(-len(small) // groups)
        vec_held = jnp.concatenate([part[:, :used, half:] for part in b_parts], axis=0)
        vec_all = dot_plain(pick, vec_held.reshape(devices, -1))
        in_whole = join(in_block, after(in_first, vo_mat))
        back_whole = join(back_block, after(back_first, vo_mat))
        vec_all = after(vec_all, in_whole, back_whole)
        vectors = [
            vec_all[:, i * lanes : i * lanes + width].reshape(-1) for i, width in enumerate(widths)
        ]
        qv_vec, out_vec, in_vec, back_vec, gain_one, shift_one, gain_two, shift_two = vectors

        def bring(rows):
            if not swapped:
                return rows[:, 0].reshape(MB * rows_here, D)
            mine = lax.dynamic_index_in_dim(rows[:, 0], seq_pos, 0, keepdims=False)
            other = lax.dynamic_index_in_dim(rows[:, 0], 1 - seq_pos, 0, keepdims=False)
            return jnp.concatenate([mine, swap(other, "seq", n_seq, 1)], axis=0)

        def bring_back(*results):
            if not swapped:
                return [rows.reshape(MB, 1, rows_here, D) for rows in results]
            others = swap(jnp.stack([rows[rows_here:] for rows in results]), "seq", n_seq, 1)
            first = seq_pos == 0
            return [
                jnp.stack(
                    [
                        jnp.where(first, rows[:rows_here], other),
                        jnp.where(first, other, rows[:rows_here]),
                    ]
                )[:, None]
                for rows, other in zip(results, others)
            ]

        ends = jnp.cumsum(lengths[:, 0], axis=1)
        if swapped:
            ids = lax.dynamic_index_in_dim(order[:, 0], seq_pos, 0, keepdims=False)
            ids = jnp.concatenate(
                [
                    lax.dynamic_slice_in_dim(ids, seq_pos * rows_here, rows_here, 0),
                    lax.dynamic_slice_in_dim(ids, (1 - seq_pos) * rows_here, rows_here, 0),
                ]
            )
            qpos = kpos = ids[None]
            ends = lax.dynamic_index_in_dim(ends, seq_pos, 0, keepdims=True)
        else:
            kpos = order[:, 0]
            qpos = lax.dynamic_slice_in_dim(kpos, seq_pos * rows_here, rows_here, 1)
        qstart = jnp.max(
            jnp.where(ends[:, None, :] <= qpos[:, :, None], ends[:, None, :], 0), axis=2
        )
        streams = qpos.shape[0]

        def by_stream(rows):
            return rows.reshape(streams, -1, rows.shape[-1])

        x_float = bring(inputs).astype(F32)
        grad_rows = bring(cotangent)
        grad_float = grad_rows.astype(F32)
        x_hat_one, inv_one = norm_parts(x_float)
        normed = (x_hat_one * gain_one + shift_one).astype(BF)
        q_bias = jnp.concatenate([qv_vec[:D], jnp.zeros((D,), F32)])
        qk = by_stream((dot_plain(normed, qk_mat) + q_bias).astype(BF))
        value_rows = by_stream((dot_plain(normed, v_mat) + qv_vec[D:]).astype(BF))
        pairs = HEADS // 2
        if not swapped:
            q = (qk, 0)
            k = (lax.all_gather(qk[:, :, D:], "seq", axis=1, tiled=True), 0)
            v = (lax.all_gather(value_rows, "seq", axis=1, tiled=True), 0)
        if swapped:
            qk, value_rows, _, _, grad_rows = lax.optimization_barrier(
                (qk, value_rows, in_whole, back_whole, grad_rows)
            )
            grad_float = grad_rows.astype(F32)
            q, k, v = (qk, 0), (qk, pairs), (value_rows, 0)
        attn_heads, probs = attend(q, k, v, qpos, qstart, kpos)
        in_last = near(in_whole, near_a[1])
        back_last = near(back_whole, near_b[1])
        in_wholes = seq_parts(in_whole, n_seq)
        back_wholes = seq_parts(back_whole, n_seq)
        attn_heads = attn_heads.reshape(-1, D)
        mid_stream = x_float + dot_plain(attn_heads, out_mat) + out_vec
        x_hat_two, inv_two = norm_parts(mid_stream)
        normed_two = (x_hat_two * gain_two + shift_two).astype(BF)
        in_last, back_last, _ = lax.optimization_barrier((in_last, back_last, normed_two))
        in_parts = interleave(in_wholes, seq_parts(in_last, n_seq))
        back_parts = interleave(back_wholes, seq_parts(back_last, n_seq))
        in_mat = reorder_columns(in_parts, a_rel, *spot, 4)
        d_back_vec = jnp.sum(grad_rows.astype(F32), axis=0, keepdims=True)
        in_mat, d_back_vec, *back_parts = lax.optimization_barrier((in_mat, d_back_vec, *back_parts))
        pre_act = dot_plain(normed_two, in_mat) + in_vec
        hidden_float, gelu_pull = jax.vjp(gelu_tanh, pre_act)
        hidden = hidden_float.astype(BF)

        top_mine = split_bit(seq_pos, top_seq)

        def halves(left, right):
            half = left.shape[1] // 2

            def part(which):
                return dot_first(
                    lax.dynamic_slice_in_dim(left, which * half, half, 1), right
                ).astype(BF)

            return part(1 - top_mine), part(top_mine)

        where = (n_seq, n_chip, seq_pos, chip_pos)

        def scatter(*sums):
            shaped = []
            for recv, keep, near in sums:
                shape = (devices // 2, keep.shape[0] // (devices // 2), keep.shape[1])
                shaped.append((keep.reshape(shape), recv.reshape(shape), near))
            return Scatter(shaped, where)

        back_give, back_keep = halves(hidden, grad_rows)
        back_recv = swap(back_give, "seq", n_seq, top_seq)
        back_parts = [after(part, back_give) for part in back_parts]
        back_mat = reorder_rows(back_parts, b_rel, *spot, FF // D)
        d_hidden = dot_last(after(grad_rows, back_keep, back_recv), back_mat)
        d_pre = gelu_pull(d_hidden)[0].astype(BF)
        in_give, in_keep = halves(normed_two, d_pre)
        in_recv = swap(in_give, "seq", n_seq, top_seq)
        late_sum = scatter((in_recv, in_keep, near_a), (back_recv, back_keep, near_b))
        d_pre = after(d_pre, *late_sum.gives)
        d_norm_two = dot_last(d_pre, in_mat)
        d_mid = grad_float + norm_back(d_norm_two, x_hat_two, inv_two, gain_two)
        d_mid_low = d_mid.astype(BF)
        d_heads = by_stream(dot_last(d_mid_low, out_mat).astype(BF))
        out_give, out_keep = halves(attn_heads, d_mid_low)
        d_heads = after(d_heads, out_give, out_keep)
        *d_parts, d_values = attend_back(q, k, v, d_heads, probs)
        sent = late_sum.second(d_values)
        if not swapped:
            d_keys = lax.psum_scatter(d_parts[1], "seq", scatter_dimension=1, tiled=True)
            d_values = lax.psum_scatter(d_values, "seq", scatter_dimension=1, tiled=True)
            d_parts = [jnp.concatenate([d_parts[0], d_keys], axis=2)]
        d_qk = d_parts[0].reshape(-1, 2 * D)
        d_values = d_values.reshape(-1, D)
        d_qk, d_values, _, _ = lax.optimization_barrier((d_qk, d_values) + sent)
        qk_give, qk_keep = halves(normed, d_qk)
        v_give, v_keep = halves(normed, d_values)
        vo_give = jnp.concatenate([v_give, out_give], axis=1)
        vo_keep = jnp.concatenate([v_keep, out_keep], axis=1)
        qk_recv, vo_recv = (swap(give, "seq", n_seq, top_seq) for give in (qk_give, vo_give))
        early_sum = scatter((qk_recv, qk_keep, near_a), (vo_recv, vo_keep, near_b))
        sent = early_sum.gives
        d_qk, d_values, d_pre, d_mid_late, _, _ = lax.optimization_barrier(
            (d_qk, d_values, d_pre, d_mid) + sent
        )
        d_in_vec = jnp.sum(d_pre.astype(F32), axis=0, keepdims=True)
        d_norm_late = after(d_norm_two, *sent)
        d_gain_two = jnp.sum(d_norm_late * x_hat_two, axis=0, keepdims=True)
        d_shift_two = jnp.sum(d_norm_late, axis=0, keepdims=True)
        d_out_vec = jnp.sum(d_mid_late, axis=0, keepdims=True)
        late_pairs = late_sum.gated(d_in_vec, d_gain_two, d_shift_two, *sent)
        late_blocks = unpack(late_pairs, own_rows, far_pos)
        q_sums = jnp.sum(d_qk[:, :D].astype(F32), axis=0, keepdims=True)
        v_sums = jnp.sum(d_values.astype(F32), axis=0, keepdims=True)
        d_norm_half = dot_last(after(d_qk, late_blocks[0]), qk_mat)
        sent = early_sum.second(d_norm_half)
        d_norm_one = d_norm_half + dot_last(after(d_values, *sent), v_mat)
        pairs_left = early_sum.gated(d_norm_one)
        d_norm_one = after(d_norm_one, *[got for _, got in pairs_left])
        d_inputs = d_mid + norm_back(d_norm_one, x_hat_one, inv_one, gain_one)
        input_grad = d_inputs.astype(BF)
        d_gain_one = jnp.sum(d_norm_one * x_hat_one, axis=0, keepdims=True)
        d_shift_one = jnp.sum(d_norm_one, axis=0, keepdims=True)

        vec_grads = [
            q_sums,
            v_sums,
            d_out_vec,
            d_in_vec,
            d_back_vec,
            d_gain_one,
            d_shift_one,
            d_gain_two,
            d_shift_two,
        ]
        vec_sum = gather_rows(vec_grads, own_rows)
        for bit in bits_of(n_seq):
            vec_sum = vec_sum + swap(vec_sum, "seq", n_seq, bit)
        vec_sum = vec_sum + swap(vec_sum, "fsdp", n_chip, 1)
        vec_sum = vec_sum + swap(vec_sum, "fsdp", n_chip, 2)
        early_blocks = unpack(pairs_left, own_rows, far_pos, vec_sum)
        hidden, _ = lax.optimization_barrier((hidden, early_blocks[0]))
        block_out = (mid_stream + dot_plain(hidden, back_mat) + back_vec).astype(BF)
        block_out, input_grad = bring_back(block_out, input_grad)
        late_sum = far_sum(late_blocks, n_chip, early_blocks[0])
        early_sum = far_sum(early_blocks, n_chip)
        d_in_mat = late_sum[:, :FF]
        d_back_mat = jnp.concatenate(
            [late_sum[:, i : i + D] for i in range(FF, 2 * FF, D)], axis=0
        )
        d_qkv_mat, d_out_mat = early_sum[:, : 3 * D], early_sum[:, 3 * D : 4 * D]
        vec_sum = early_sum[:, 4 * D :]
        long = vec_sum.shape[1]
        g_out, at = [], 0
        for width in widths:
            spot_at = at + me * width
            got = lax.dynamic_slice(vec_sum, (spot_at // long, spot_at % long), (1, width))
            g_out.append(got[0])
            at += width * devices
        g_qv, g_out_vec, g_in, g_back, g_gain1, g_shift1, g_gain2, g_shift2 = g_out
        return (
            block_out,
            input_grad,
            d_qkv_mat,
            g_qv,
            d_out_mat,
            g_out_vec,
            d_in_mat,
            g_in,
            d_back_mat,
            g_back,
            g_gain1,
            g_shift1,
            g_gain2,
            g_shift2,
        )

    tokens, sharded, vector = P(None, "fsdp", "seq", None), P(("seq", "fsdp"), None), P(("seq", "fsdp"))
    streams_spec = P(None, "fsdp", None)
    return jax.shard_map(
        local,
        mesh=mesh,
        in_specs=(tokens, streams_spec, streams_spec, tokens) + (sharded, vector) * 4 + (vector,) * 4,
        out_specs=(tokens, tokens) + (sharded, vector) * 4 + (vector,) * 4,
        check_vma=False,
    )
```
